256 devices in a mesh: dp: 16 (over x, y), expert: 16 (over z, core).
Axes of the slice: x: 4, y: 4, z: 8, core: 2. Of those that a mesh axis runs over, the one named last changes fastest.
Arguments:
- hidden_in: bfloat16 [256, 2, 2880], P(('expert', 'dp')), may hold values from -6 to 6
- queries: bfloat16 [256, 2, 4096], P(('expert', 'dp')), may hold values from -2 to 2
- new_keys: bfloat16 [256, 2, 512], P(('expert', 'dp')), may hold values from -2 to 2
- new_values: bfloat16 [256, 2, 512], P(('expert', 'dp')), may hold values from -6 to 6
- key_cache: bfloat16 [256, 512, 512], P(('expert', 'dp')), may hold values from -2 to 2
- value_cache: bfloat16 [256, 512, 512], P(('expert', 'dp')), may hold values from -6 to 6
- prompt_lengths: int32 [256], P(('expert', 'dp')), may hold values from 64 to 512, as said below
- out_weight: bfloat16 [4096, 2880], P('expert'), may hold values from -0.375 to 0.375
- norm_gain: float32 [2880], replicated, may hold values from 0.1 to 1.9
- expert_ids: int32 [256, 2, 4], P('expert'), may hold values from 0 to 31, all different within a row; in each aligned block of 32 rows (0 to 31, 32 to 63, ..., all dimensions but the last counted through in order) at most 12 rows name the same one
- top_logits: bfloat16 [256, 2, 4], P('expert'), may hold values from -4 to 4
- gate_weight: bfloat16 [32, 2880, 2880], P('expert', None, 'dp'), may hold values from -0.109375 to 0.109375
- up_weight: bfloat16 [32, 2880, 2880], P('expert', None, 'dp'), may hold values from -0.109375 to 0.109375
- down_weight: bfloat16 [32, 2880, 2880], P('expert', 'dp'), may hold values from -0.109375 to 0.109375
Outputs:
- layer_out: bfloat16 [256, 2, 2880], P(('expert', 'dp'))
The draws below stay inside these ranges and needn't reach their ends.
Inputs may be any that keep to these rules, and one draw needn't show every extreme that they name: `prompt_lengths`: some row has exactly 512 live slots. `expert_ids`: A row names 4 different experts at each position. Over the 16 rows held by one index of the expert axis and both positions, no expert is named more than 12 times, and in some such group one expert is named exactly 12 times.
All inputs are finite; a program needn't handle non-finite values.
Results may differ from the reference program's by a relative error of at most 0.02.
Values may be sent and summed in bfloat16 or wider, within the bound.
No kernel may reach another device: no remote copies, remote signals or barrier semaphores. Data moves between devices by JAX's collectives and lax.ppermute only.
A program may use at most 128 MiB of HBM per device.

```python
import math
import jax
import jax.numpy as jnp
import numpy as np
from jax import lax

D = 2880
HQ = 64
KVH = 8
HD = 64
FF = 2880
TOPK = 4
STEPS = 2
LMAX = 512
EXPERTS = 32
COL_ROWS = 16
ROWS = 256
CAP = 12
N_DP = 16


def draw_prompt_lengths(key, part):
    first_key, second_key = jax.random.split(jax.random.fold_in(key, 7))
    lengths = jax.random.randint(first_key, (ROWS,), LMAX // 8, LMAX + 1)
    longest = jax.random.randint(second_key, (), 0, ROWS)
    return jnp.where(jnp.arange(ROWS) == longest, LMAX, lengths).astype(jnp.int32)


def block_levels(own_key, dims, cuts, smallest, top_value):
    factor_of, own = 1.0, jax.random.fold_in(own_key, 6)
    for dim, parts in cuts:
        steps = jnp.exp(jax.random.uniform(jax.random.fold_in(own, dim), (parts,), jnp.float32, smallest / len(cuts), top_value / len(cuts)))
        factor_of = factor_of * jnp.repeat(steps, dims[dim] // parts).reshape([-1 if axis == dim else 1 for axis in range(len(dims))])
    return factor_of


def assign_block(own_key, own, number, rows, count, top, reach, skew):
    ranking = jax.random.permutation(own_key, count)
    heavy_load, common = load_shares(count, rows * top, reach, skew, True), load_shares(count, rows * top, reach, skew, False)
    places = jnp.arange(count)

    def named(sizes, rotation):
        used = int((sizes > 0).sum())
        fixed = max(1, used // 4)
        moved = fixed + (places - fixed + rotation * (used - fixed)) % max(1, count - fixed)
        return jnp.zeros((count,), jnp.int32).at[ranking[jnp.where(places < fixed, places, moved)]].set(jnp.asarray(sizes, jnp.int32))

    sizes = jnp.where(number % 4 == 0, named(heavy_load, number // 4), named(common, number - number // 4 - 1))
    mixed = jax.random.permutation(jax.random.fold_in(own, 3), count)
    source_of, taker = mixed[0:count // 2 * 2:2], mixed[1:count // 2 * 2:2]
    slack = jnp.minimum(sizes[source_of] - 1, reach - sizes[taker]) // 2
    slack = jnp.where((source_of == ranking[0]) | (taker == ranking[0]) | (sizes[taker] == 0), 0, jnp.maximum(slack, 0))
    moved = jax.random.randint(jax.random.fold_in(own, 4), (count // 2,), 0, 1 << 20) % (slack + 1)
    sizes = sizes.at[source_of].add(-moved).at[taker].add(moved)
    members = jnp.searchsorted(jnp.cumsum(sizes), jnp.arange(rows * top), side="right").astype(jnp.int32)
    table = members.reshape(top, rows).T
    table = table[jax.random.permutation(jax.random.fold_in(own, 1), rows)]
    rotation = jax.random.randint(jax.random.fold_in(own, 2), (rows, 1), 0, top)
    return jnp.take_along_axis(table, (jnp.arange(top)[None, :] + rotation) % top, axis=1)


def load_shares(amount, total, reach, skew, full):
    weights = [(1 << 20) // math.isqrt(grade ** skew) + 1 for grade in range(1, amount + 1)]
    largest = reach if full else min(reach, max(-(-total // amount), total * weights[0] // sum(weights)))
    least = 1 if total - largest >= amount - 1 else 0
    given, surplus = [largest] + [least] * (amount - 1), total - largest - least * (amount - 1)
    while surplus > 0:
        movable = [i for i in range(1, amount) if given[i] < largest] or [i for i in range(1, amount) if given[i] < reach]
        pool, remaining = sum([weights[i] for i in movable]), surplus
        for i in movable:
            more = min(reach - given[i], max(1, remaining * weights[i] // pool), surplus)
            given[i] = given[i] + more
            surplus = surplus - more
    return np.array(given)


def centred(rng, extent, scale, most, cuts=(), kind=jnp.bfloat16):
    result = scale * jax.random.normal(rng, extent, jnp.float32)
    if cuts:
        result = result * block_levels(rng, extent, cuts, -0.22, 0.18)
    return jnp.clip(result, -most, most).astype(kind)


def setup_inputs(seed: int = 0) -> dict:
    arg_keys = jax.random.split(jax.random.key(seed), 15)
    hidden_in = centred(arg_keys[0], (ROWS, STEPS, D), 1.0, 6.0, ((0, 256),))
    queries = jnp.clip(jax.random.uniform(arg_keys[1], (ROWS, STEPS, HQ * HD), jnp.float32, -2.0, 2.0) * block_levels(arg_keys[1], (ROWS, STEPS, HQ * HD), ((0, 256),), -0.4, 0.0), -2.0, 2.0).astype(jnp.bfloat16)
    new_keys = jnp.clip(jax.random.uniform(arg_keys[2], (ROWS, STEPS, KVH * HD), jnp.float32, -2.0, 2.0) * block_levels(arg_keys[2], (ROWS, STEPS, KVH * HD), ((0, 256),), -0.4, 0.0), -2.0, 2.0).astype(jnp.bfloat16)
    new_values = centred(arg_keys[3], (ROWS, STEPS, KVH * HD), 1.0, 6.0, ((0, 256),))
    key_cache = jnp.clip(jax.random.uniform(arg_keys[4], (ROWS, LMAX, KVH * HD), jnp.float32, -2.0, 2.0) * block_levels(arg_keys[4], (ROWS, LMAX, KVH * HD), ((0, 256),), -0.4, 0.0), -2.0, 2.0).astype(jnp.bfloat16)
    value_cache = centred(arg_keys[5], (ROWS, LMAX, KVH * HD), 1.0, 6.0, ((0, 256),))
    prompt_lengths = draw_prompt_lengths(jax.random.fold_in(arg_keys[14], 71), 0)
    out_weight = centred(arg_keys[7], (HQ * HD, D), (HQ * HD // 16) ** -0.5, 0.375, ((0, 16),))
    norm_gain = jnp.clip(1.0 + 0.18 * jax.random.normal(arg_keys[8], (D,), jnp.float32), 0.1, 1.9)
    expert_ids_keys = jax.random.split(jax.random.fold_in(arg_keys[9], 1), ROWS * STEPS // (COL_ROWS * STEPS))
    expert_ids_turns = jax.random.permutation(jax.random.fold_in(arg_keys[9], 3), ROWS * STEPS // (COL_ROWS * STEPS))
    expert_ids = jax.vmap(lambda own, number: assign_block(jax.random.fold_in(arg_keys[9], 2), own, number, COL_ROWS * STEPS, EXPERTS, TOPK, CAP, 2))(expert_ids_keys, expert_ids_turns).reshape((ROWS, STEPS, TOPK))
    top_logits = centred(arg_keys[10], (ROWS, STEPS, TOPK), 1.0, 4.0, ((0, 16),))
    gate_weight = centred(arg_keys[11], (EXPERTS, D, FF), D ** -0.5, 0.109375, ((0, 16), (2, 16)))
    up_weight = centred(arg_keys[12], (EXPERTS, D, FF), D ** -0.5, 0.109375, ((0, 16), (2, 16)))
    down_weight = centred(arg_keys[13], (EXPERTS, FF, D), FF ** -0.5, 0.109375, ((0, 16), (1, 16)))
    return {"hidden_in": hidden_in, "queries": queries, "new_keys": new_keys, "new_values": new_values, "key_cache": key_cache, "value_cache": value_cache, "prompt_lengths": prompt_lengths, "out_weight": out_weight, "norm_gain": norm_gain, "expert_ids": expert_ids, "top_logits": top_logits, "gate_weight": gate_weight, "up_weight": up_weight, "down_weight": down_weight}


def attend_single(query_rows, fresh_keys, fresh_values, cache_keys, cache_values, length):
    step_count = query_rows.shape[0]
    cache_len = cache_keys.shape[0]
    keys_all = jnp.concatenate([cache_keys, fresh_keys], axis=0).astype(jnp.float32).reshape(cache_len + step_count, KVH, HD)
    values_all = jnp.concatenate([cache_values, fresh_values], axis=0).astype(jnp.float32).reshape(cache_len + step_count, KVH, HD)
    query_heads = query_rows.astype(jnp.float32).reshape(step_count, KVH, HQ // KVH, HD)
    scores = jnp.einsum('sgqe,kge->sgqk', query_heads, keys_all) * 0.125
    position = jnp.arange(cache_len + step_count, dtype=jnp.int32)
    step_ids = jnp.arange(step_count, dtype=jnp.int32)
    visible = (position[None, :] < length) | (position[None, :] >= cache_len) & (position[None, :] - cache_len <= step_ids[:, None])
    exp_scores = jnp.where(visible[:, None, None, :], jnp.exp(scores), jnp.zeros_like(scores))
    attn_probs = (exp_scores / lax.optimization_barrier(jnp.sum(exp_scores, axis=-1, keepdims=True))).astype(jnp.bfloat16)
    attended = jnp.einsum('sgqk,kge->sgqe', attn_probs.astype(jnp.float32), values_all)
    return attended.astype(jnp.bfloat16).reshape(step_count, HQ * HD)

def rms_normed(residual, norm_gain):
    inverse_rms = lax.rsqrt(lax.optimization_barrier(jnp.mean(residual * residual, axis=-1, keepdims=True)) + 1e-05)
    return (residual * inverse_rms * norm_gain).astype(jnp.bfloat16)

def swiglu_act(gate_vals, up_vals):
    return (gate_vals * jax.nn.sigmoid(1.702 * gate_vals) * (up_vals + 1.0)).astype(jnp.bfloat16)

def reference(hidden_in, queries, new_keys, new_values, key_cache, value_cache, prompt_lengths, out_weight, norm_gain, expert_ids, top_logits, gate_weight, up_weight, down_weight):
    attended = lax.map(lambda items: attend_single(*items), (queries, new_keys, new_values, key_cache, value_cache, prompt_lengths))
    flat_attn = attended.reshape(ROWS * STEPS, HQ * HD)
    projected = jnp.dot(flat_attn, out_weight, preferred_element_type=jnp.float32)
    residual = hidden_in.reshape(ROWS * STEPS, D).astype(jnp.float32) + projected
    normed = rms_normed(residual, norm_gain)
    flat_ids = expert_ids.reshape(ROWS * STEPS, TOPK)
    exp_logits = jnp.exp(top_logits.reshape(ROWS * STEPS, TOPK).astype(jnp.float32))
    mix_weights = exp_logits / lax.optimization_barrier(jnp.sum(exp_logits, axis=-1, keepdims=True))

    def expert_pass(running, inputs):
        gate_mat, up_mat, down_mat, expert_label = inputs
        gate_vals = jnp.dot(normed, gate_mat, preferred_element_type=jnp.float32)
        up_vals = jnp.dot(normed, up_mat, preferred_element_type=jnp.float32)
        activated = swiglu_act(gate_vals, up_vals)
        sliced = activated.astype(jnp.float32).reshape(ROWS * STEPS, N_DP, FF // N_DP)
        down_sliced = down_mat.astype(jnp.float32).reshape(N_DP, FF // N_DP, D)
        pieces = jnp.einsum('tjf,jfd->tjd', sliced, down_sliced).astype(jnp.bfloat16)
        expert_out = lax.optimization_barrier(jnp.sum(pieces.astype(jnp.float32), axis=1))
        token_share = lax.optimization_barrier(jnp.sum(jnp.where(flat_ids == expert_label, mix_weights, jnp.zeros_like(mix_weights)), axis=1))
        return (running + token_share[:, None] * expert_out, None)
    expert_labels = jnp.arange(EXPERTS, dtype=jnp.int32)
    moe_total = lax.scan(expert_pass, jnp.zeros((ROWS * STEPS, D), jnp.float32), (gate_weight, up_weight, down_weight, expert_labels))[0]
    return (residual + moe_total).astype(jnp.bfloat16).reshape(ROWS, STEPS, D)
```

```python
import functools

import jax
import jax.numpy as jnp
from jax import lax
from jax.experimental import pallas as pl
from jax.experimental.pallas import tpu as pltpu
from jax.sharding import Mesh
from jax.sharding import PartitionSpec as P

HQ = 64
KVH = 8
HD = 64
SWAP = [(0, 1), (1, 0)]
F32 = jnp.float32
BF16 = jnp.bfloat16


def params(mib=48):
    return pltpu.CompilerParams(vmem_limit_bytes=mib * 1024 * 1024)


def vmem():
    return pl.BlockSpec(memory_space=pltpu.VMEM)


def smem():
    return pl.BlockSpec(memory_space=pltpu.SMEM)


def attend_kernel(len_ref, q_ref, nk_ref, nv_ref, k_ref, v_ref, out_ref, rows_ref, flat_ref):
    steps = q_ref.shape[1]
    width = KVH * HD
    rows = HQ * steps
    per_group = rows // KVH
    q = q_ref[0].astype(F32) * 0.125
    for h in range(HQ):
        rows_ref[h * steps : (h + 1) * steps, :] = q[:, h * HD : (h + 1) * HD]
    q_rows = rows_ref[...]
    q_pair = jnp.concatenate([q_rows, q_rows], axis=1)
    q_wide = jnp.concatenate([q_pair] * (KVH // 2), axis=1)
    row_id = lax.broadcasted_iota(jnp.int32, (rows, width), 0)
    col_id = lax.broadcasted_iota(jnp.int32, (rows, width), 1)
    in_group = row_id // per_group == col_id // HD
    q_wide = jnp.where(in_group, q_wide, 0.0)
    q_bf = q_wide.astype(BF16)
    scores = lax.dot_general(
        q_bf, k_ref[0], (((1,), (1,)), ((), ())), preferred_element_type=F32
    )
    slot = lax.broadcasted_iota(jnp.int32, scores.shape, 1)
    weights = jnp.where(slot < len_ref[0], jnp.exp(scores), 0.0)
    total = jnp.sum(weights, axis=1, keepdims=True)
    nk = nk_ref[0].astype(F32)
    nv = nv_ref[0].astype(F32)
    step_id = lax.broadcasted_iota(jnp.int32, (rows, 1), 0) % steps
    fresh = []
    for s in range(steps):
        score = jnp.sum(q_wide * nk[s : s + 1, :], axis=1, keepdims=True)
        weight = jnp.where(step_id >= s, jnp.exp(score), 0.0)
        total = total + weight
        fresh.append(weight)
    probs = (weights / total).astype(BF16)
    mixed = jnp.dot(probs, v_ref[0], preferred_element_type=F32)
    for s in range(steps):
        mixed = mixed + (fresh[s] / total).astype(BF16).astype(F32) * nv[s : s + 1, :]
    mixed = jnp.where(in_group, mixed, 0.0)
    folded = mixed[:, :128]
    for i in range(1, width // 128):
        folded = folded + mixed[:, i * 128 : (i + 1) * 128]
    rows_ref[...] = folded[:, :HD] + folded[:, HD:]
    for h in range(HQ):
        flat_ref[:, h * HD : (h + 1) * HD] = rows_ref[h * steps : (h + 1) * steps, :]
    blocks = out_ref.shape[0]
    wide = HQ * HD // blocks
    for b in range(blocks):
        out_ref[b] = flat_ref[:, b * wide : (b + 1) * wide].astype(BF16)


def attend(length, q, nk, nv, k, v, blocks):
    steps = q.shape[1]
    return pl.pallas_call(
        attend_kernel,
        in_specs=[smem()] + [vmem()] * 5,
        out_specs=vmem(),
        out_shape=jax.ShapeDtypeStruct((blocks, steps, HQ * HD // blocks), BF16),
        scratch_shapes=[pltpu.VMEM((HQ * steps, HD), F32), pltpu.VMEM((steps, HQ * HD), F32)],
        compiler_params=params(),
        name="attend",
    )(length, q, nk, nv, k, v)


def norm_kernel(part_ref, hid_ref, gain_ref, route_ref, res_ref, out_ref):
    width = hid_ref.shape[2]
    res = hid_ref[0].astype(F32)
    for i in range(part_ref.shape[0]):
        res = res + part_ref[i].astype(F32)
    res_ref[...] = res
    scale = lax.rsqrt(jnp.sum(res * res, axis=1, keepdims=True) / width + 1e-05)
    normed = (res * scale * gain_ref[...]).astype(BF16).astype(F32)
    full = jnp.concatenate([normed, route_ref[...]], axis=1).astype(BF16)
    for i in range(out_ref.shape[0]):
        out_ref[i] = full


def norm(parts, hidden, gain, route):
    steps, width = hidden.shape[1:]
    copies = parts.shape[0]
    wide = width + route.shape[1]
    return pl.pallas_call(
        norm_kernel,
        in_specs=[vmem()] * 4,
        out_specs=[vmem(), vmem()],
        out_shape=[
            jax.ShapeDtypeStruct((steps, width), F32),
            jax.ShapeDtypeStruct((copies, steps, wide), BF16),
        ],
        compiler_params=params(),
        name="norm",
    )(parts, hidden, gain, route)


def experts_kernel(first_ref, x_ref, g0, g1, u0, u1, d0, d1, out_ref, acc_ref):
    step = pl.program_id(0)
    width = g0.shape[1]
    half = pl.num_programs(0) // 2

    def one(g_ref, u_ref, d_ref, label):
        x = x_ref[:, :width]
        gate = jnp.dot(x, g_ref[0], preferred_element_type=F32)
        up = jnp.dot(x, u_ref[0], preferred_element_type=F32)
        act = gate * jax.nn.sigmoid(1.702 * gate) * (up + 1.0)
        route = x_ref[:, width : width + 8].astype(F32)
        ids = route[:, 0:4]
        expo = jnp.exp(route[:, 4:8])
        chosen = jnp.where(ids == label.astype(F32), expo, 0.0)
        share = jnp.sum(chosen, axis=1, keepdims=True) / jnp.sum(expo, axis=1, keepdims=True)
        mixed = (act * share).astype(BF16)
        return jnp.dot(mixed, d_ref[0], preferred_element_type=F32)

    @pl.when(step == 0)
    def _():
        acc_ref[...] = one(g0, u0, d0, first_ref[0])

    @pl.when((step > 0) & (step < half))
    def _():
        acc_ref[...] += one(g0, u0, d0, first_ref[0] + step)

    @pl.when(step >= half)
    def _():
        acc_ref[...] += one(g1, u1, d1, first_ref[1] + step - half)

    @pl.when(step == pl.num_programs(0) - 1)
    def _():
        out_ref[...] = acc_ref[...].astype(BF16)


def experts(first, x, own, other):
    rows = x.shape[0]
    per, width, hidden = own[0].shape

    def early(i, *_):
        return (jnp.minimum(i, per - 1), 0, 0)

    def late(i, *_):
        return (jnp.maximum(i - per, 0), 0, 0)

    def spec(shape, index):
        return pl.BlockSpec((1,) + shape[1:], index)

    grid_spec = pltpu.PrefetchScalarGridSpec(
        num_scalar_prefetch=1,
        grid=(2 * per,),
        in_specs=[
            pl.BlockSpec(x.shape, lambda i, *_: (0, 0)),
            spec(own[0].shape, early),
            spec(own[0].shape, late),
            spec(own[1].shape, early),
            spec(own[1].shape, late),
            spec(own[2].shape, early),
            spec(own[2].shape, late),
        ],
        out_specs=pl.BlockSpec((rows, width), lambda i, *_: (0, 0)),
        scratch_shapes=[pltpu.VMEM((rows, width), F32)],
    )
    return pl.pallas_call(
        experts_kernel,
        grid_spec=grid_spec,
        out_shape=jax.ShapeDtypeStruct((rows, width), BF16),
        compiler_params=params(),
        name="experts",
    )(first, x, own[0], other[0], own[1], other[1], own[2], other[2])


def exchange(value, axis):
    return lax.all_to_all(value, axis, split_axis=0, concat_axis=0, tiled=True)


def on_device(
    hidden_in,
    queries,
    new_keys,
    new_values,
    key_cache,
    value_cache,
    prompt_lengths,
    out_weight,
    norm_gain,
    expert_ids,
    top_logits,
    gate_weight,
    up_weight,
    down_weight,
):
    rows, steps, width = hidden_in.shape
    nz = lax.axis_size("z")
    ndp = lax.axis_size(("x", "y"))
    z = lax.axis_index("z")
    c = lax.axis_index("c")
    d = lax.axis_index(("x", "y"))
    other_out = lax.ppermute(out_weight, "c", SWAP)
    other = [lax.ppermute(w, "c", SWAP) for w in (gate_weight, up_weight, down_weight)]
    own = [gate_weight, up_weight, down_weight]
    attended = attend(
        prompt_lengths, queries, new_keys, new_values, key_cache, value_cache, nz
    )
    feats = out_weight.shape[0]
    by_heads = exchange(attended, "z").reshape(nz * steps, 2 * feats)
    mine = lax.dynamic_slice_in_dim(by_heads, c * feats, feats, 1)
    theirs = lax.dynamic_slice_in_dim(by_heads, (1 - c) * feats, feats, 1)
    parts = jnp.dot(mine, out_weight, preferred_element_type=F32) + jnp.dot(
        theirs, other_out, preferred_element_type=F32
    )
    parts = exchange(parts.astype(BF16).reshape(nz, steps, width), "z")
    ids = lax.dynamic_index_in_dim(expert_ids, d, 0, False).astype(F32)
    logits = lax.dynamic_index_in_dim(top_logits, d, 0, False).astype(F32)
    route = jnp.pad(jnp.concatenate([ids, logits], axis=1), ((0, 0), (0, 56)))
    residual, sent = norm(parts, hidden_in, norm_gain[None], route)
    column = exchange(sent, "z").reshape(nz * steps, -1)
    copies = jnp.broadcast_to(column[None], (ndp,) + column.shape)
    tokens = exchange(copies, ("x", "y")).reshape(ndp * nz * steps, -1)
    per = gate_weight.shape[0]
    first = jnp.stack([(2 * z + c) * per, (2 * z + 1 - c) * per]).astype(jnp.int32)
    made = experts(first, tokens, own, other)
    back = exchange(made.reshape(ndp, nz * steps, width), ("x", "y"))
    column_sum = jnp.sum(back.astype(F32), axis=0).astype(BF16)
    final = exchange(column_sum.reshape(nz, steps, width), "z")
    out = residual + jnp.sum(final.astype(F32), axis=0)
    return out.astype(BF16)[None]


def solution(mesh):
    shape = dict(mesh.shape)
    side = int(round(shape["dp"] ** 0.5))
    fine = Mesh(
        mesh.devices.reshape(side, shape["dp"] // side, shape["expert"] // 2, 2),
        ("x", "y", "z", "c"),
    )
    row = ("z", "c", "x", "y")
    group = ("z", "c")
    dp = ("x", "y")
    placed = (
        P(row, None, None),
        P(row, None, None),
        P(row, None, None),
        P(row, None, None),
        P(row, None, None),
        P(row, None, None),
        P(row),
        P(group, None),
        P(),
        P(group, None, None),
        P(group, None, None),
        P(group, None, dp),
        P(group, None, dp),
        P(group, dp, None),
    )
    return jax.shard_map(
        on_device,
        mesh=fine,
        in_specs=placed,
        out_specs=P(row, None, None),
        check_vma=False,
    )
```

```python
import jax
import jax.numpy as jnp
from jax import lax
from jax.experimental import pallas as pl
from jax.experimental.pallas import tpu as pltpu
from jax.experimental.layout import Layout, with_layout_constraint
from jax.sharding import Mesh
from jax.sharding import PartitionSpec as P

HQ = 64
KVH = 8
HD = 64
SWAP = [(0, 1), (1, 0)]
F32 = jnp.float32
BF16 = jnp.bfloat16


def params(mib):
    return pltpu.CompilerParams(vmem_limit_bytes=mib * 1024 * 1024)


def vmem():
    return pl.BlockSpec(memory_space=pltpu.VMEM)


def hbm():
    return pl.BlockSpec(memory_space=pltpu.HBM)


def stay(*values):
    return [pltpu.with_memory_space_constraint(v, pltpu.HBM) for v in values]


def smem():
    return pl.BlockSpec(memory_space=pltpu.SMEM)


def attend_kernel(
    len_ref, q_hbm, nk_hbm, nv_hbm, k_hbm, v_hbm, out_ref,
    q_ref, nk_ref, nv_ref, k_ref, v_ref, rows_ref, flat_ref, sems,
):
    pairs = (
        (k_hbm, k_ref), (q_hbm, q_ref), (nk_hbm, nk_ref), (nv_hbm, nv_ref), (v_hbm, v_ref),
    )
    copies = [pltpu.make_async_copy(a, b, sems.at[i]) for i, (a, b) in enumerate(pairs)]
    for copy in copies:
        copy.start()
    steps = q_ref.shape[1]
    width = KVH * HD
    rows = HQ * steps
    per_group = rows // KVH
    copies[1].wait()
    q = q_ref[0].astype(F32) * 0.125
    for h in range(HQ):
        rows_ref[h * steps : (h + 1) * steps, :] = q[:, h * HD : (h + 1) * HD]
    q_rows = rows_ref[...]
    q_pair = jnp.concatenate([q_rows, q_rows], axis=1)
    q_wide = jnp.concatenate([q_pair] * (KVH // 2), axis=1)
    row_id = lax.broadcasted_iota(jnp.int32, (rows, width), 0)
    col_id = lax.broadcasted_iota(jnp.int32, (rows, width), 1)
    in_group = row_id // per_group == col_id // HD
    q_wide = jnp.where(in_group, q_wide, 0.0)
    q_bf = q_wide.astype(BF16)
    copies[0].wait()
    scores = lax.dot_general(
        q_bf, k_ref[0], (((1,), (1,)), ((), ())), preferred_element_type=F32
    )
    slot = lax.broadcasted_iota(jnp.int32, scores.shape, 1)
    weights = jnp.where(slot < len_ref[0], jnp.exp(scores), 0.0)
    total = jnp.sum(weights, axis=1, keepdims=True)
    copies[2].wait()
    copies[3].wait()
    nk = nk_ref[0].astype(F32)
    nv = nv_ref[0].astype(F32)
    step_id = lax.broadcasted_iota(jnp.int32, (rows, 1), 0) % steps
    fresh = []
    for s in range(steps):
        score = jnp.sum(q_wide * nk[s : s + 1, :], axis=1, keepdims=True)
        weight = jnp.where(step_id >= s, jnp.exp(score), 0.0)
        total = total + weight
        fresh.append(weight)
    probs = (weights / total).astype(BF16)
    copies[4].wait()
    mixed = jnp.dot(probs, v_ref[0], preferred_element_type=F32)
    for s in range(steps):
        mixed = mixed + (fresh[s] / total).astype(BF16).astype(F32) * nv[s : s + 1, :]
    mixed = jnp.where(in_group, mixed, 0.0)
    folded = mixed[:, :128]
    for i in range(1, width // 128):
        folded = folded + mixed[:, i * 128 : (i + 1) * 128]
    rows_ref[...] = folded[:, :HD] + folded[:, HD:]
    for h in range(HQ):
        flat_ref[:, h * HD : (h + 1) * HD] = rows_ref[h * steps : (h + 1) * steps, :]
    blocks = out_ref.shape[0]
    wide = HQ * HD // blocks
    for b in range(blocks):
        out_ref[b] = flat_ref[:, b * wide : (b + 1) * wide].astype(BF16)


def attend(length, q, nk, nv, k, v, blocks):
    steps = q.shape[1]
    return pl.pallas_call(
        attend_kernel,
        in_specs=[smem()] + [hbm()] * 5,
        out_specs=vmem(),
        out_shape=jax.ShapeDtypeStruct((blocks, steps, HQ * HD // blocks), BF16),
        scratch_shapes=[pltpu.VMEM(a.shape, BF16) for a in (q, nk, nv, k, v)]
        + [
            pltpu.VMEM((HQ * steps, HD), F32),
            pltpu.VMEM((steps, HQ * HD), F32),
            pltpu.SemaphoreType.DMA((5,)),
        ],
        compiler_params=params(12),
        name="attend",
    )(length, *stay(q, nk, nv, k, v))


def project_kernel(
    core_ref, x_ref, own_hbm, other_hbm, out_ref, rows_ref, own_ref, other_ref, sems
):
    copies = [
        pltpu.make_async_copy(own_hbm, own_ref, sems.at[0]),
        pltpu.make_async_copy(other_hbm, other_ref, sems.at[1]),
    ]
    for copy in copies:
        copy.start()
    blocks, steps, _ = x_ref.shape
    for i in range(blocks):
        rows_ref[i * steps : (i + 1) * steps, :] = x_ref[i].astype(F32)
    x = rows_ref[...].astype(BF16)
    feats = own_ref.shape[1]
    low, high = x[:, :feats], x[:, feats:]
    first = core_ref[0] == 0
    mine = jnp.where(first, low, high)
    theirs = jnp.where(first, high, low)
    dims = (((1,), (1,)), ((), ()))
    copies[0].wait()
    part = lax.dot_general(mine, own_ref[...], dims, preferred_element_type=F32)
    copies[1].wait()
    part = part + lax.dot_general(theirs, other_ref[...], dims, preferred_element_type=F32)
    for i in range(blocks):
        out_ref[i] = part[i * steps : (i + 1) * steps, :].astype(BF16)


def project(core, x, own, other):
    blocks, steps, feats = x.shape
    return pl.pallas_call(
        project_kernel,
        in_specs=[smem(), vmem(), hbm(), hbm()],
        out_specs=vmem(),
        out_shape=jax.ShapeDtypeStruct((blocks, steps, own.shape[0]), BF16),
        scratch_shapes=[
            pltpu.VMEM((blocks * steps, feats), F32),
            pltpu.VMEM(own.shape, BF16),
            pltpu.VMEM(own.shape, BF16),
            pltpu.SemaphoreType.DMA((2,)),
        ],
        compiler_params=params(12),
        name="project",
    )(core, x, *stay(own, other))


def norm_kernel(part_ref, hid_ref, gain_ref, route_ref, res_ref, out_ref):
    width = hid_ref.shape[2]
    res = hid_ref[0].astype(F32)
    for i in range(part_ref.shape[0]):
        res = res + part_ref[i].astype(F32)
    res_ref[...] = res
    scale = lax.rsqrt(jnp.sum(res * res, axis=1, keepdims=True) / width + 1e-05)
    normed = (res * scale * gain_ref[...]).astype(BF16).astype(F32)
    full = jnp.concatenate([normed, route_ref[...]], axis=1).astype(BF16)
    for i in range(out_ref.shape[0]):
        out_ref[i] = full


def norm(parts, hidden, gain, route):
    steps, width = hidden.shape[1:]
    copies = parts.shape[0]
    wide = width + route.shape[1]
    return pl.pallas_call(
        norm_kernel,
        in_specs=[vmem()] * 4,
        out_specs=[vmem(), vmem()],
        out_shape=[
            jax.ShapeDtypeStruct((steps, width), F32),
            jax.ShapeDtypeStruct((copies, steps, wide), BF16),
        ],
        compiler_params=params(12),
        name="norm",
    )(parts, hidden, gain, route)


def spread_kernel(x_ref, out_hbm, rows_ref, full_ref, sems):
    blocks, steps, _ = x_ref.shape
    for i in range(blocks):
        rows_ref[i * steps : (i + 1) * steps, :] = x_ref[i].astype(F32)
    full_ref[...] = rows_ref[...].astype(BF16)
    copies = [
        pltpu.make_async_copy(full_ref, out_hbm.at[i], sems.at[i])
        for i in range(out_hbm.shape[0])
    ]
    for copy in copies:
        copy.start()
    for copy in copies:
        copy.wait()


def spread(x, copies):
    blocks, steps, width = x.shape
    return pl.pallas_call(
        spread_kernel,
        in_specs=[vmem()],
        out_specs=hbm(),
        out_shape=jax.ShapeDtypeStruct((copies, blocks * steps, width), BF16),
        scratch_shapes=[
            pltpu.VMEM((blocks * steps, width), F32),
            pltpu.VMEM((blocks * steps, width), BF16),
            pltpu.SemaphoreType.DMA((copies,)),
        ],
        compiler_params=params(12),
        name="spread",
    )(x)


def experts_kernel(
    first_ref, x_ref, g0_hbm, u0_hbm, g1_hbm, u1_hbm, d0_hbm, d1_hbm, out_ref,
    g0, u0, g1, u1, d0, d1, sems,
):
    pairs = (
        (g0_hbm, g0), (u0_hbm, u0), (g1_hbm, g1), (u1_hbm, u1), (d0_hbm, d0), (d1_hbm, d1),
    )
    copies = [pltpu.make_async_copy(a, b, sems.at[i]) for i, (a, b) in enumerate(pairs)]
    for copy in copies:
        copy.start()
    per, _, width = g0.shape
    x = x_ref[:, :width]
    route = x_ref[:, width : width + 8].astype(F32)
    ids = route[:, 0:4]
    expo = jnp.exp(route[:, 4:8])
    total = jnp.sum(expo, axis=1, keepdims=True)
    dims = (((1,), (1,)), ((), ()))
    acts = []
    for side, (g_ref, u_ref) in enumerate(((g0, u0), (g1, u1))):
        copies[2 * side].wait()
        copies[1 + 2 * side].wait()
        for e in range(per):
            gate = lax.dot_general(x, g_ref[e], dims, preferred_element_type=F32)
            up = lax.dot_general(x, u_ref[e], dims, preferred_element_type=F32)
            act = gate * jax.nn.sigmoid(1.702 * gate) * (up + 1.0)
            label = (first_ref[side] + e).astype(F32)
            share = jnp.sum(jnp.where(ids == label, expo, 0.0), axis=1, keepdims=True) / total
            acts.append((act * share).astype(BF16))
    copies[4].wait()
    copies[5].wait()
    chunk = 768
    for start in range(0, width, chunk):
        stop = min(start + chunk, width)
        part = None
        for side, d_ref in enumerate((d0, d1)):
            for e in range(per):
                piece = jnp.dot(
                    acts[side * per + e], d_ref[e, :, start:stop], preferred_element_type=F32
                )
                part = piece if part is None else part + piece
        out_ref[:, start:stop] = part.astype(BF16)


def experts(first, x, own, other):
    width = own[0].shape[2]
    args = (own[0], own[1], other[0], other[1], own[2], other[2])
    return pl.pallas_call(
        experts_kernel,
        in_specs=[smem(), vmem()] + [hbm()] * 6,
        out_specs=vmem(),
        out_shape=jax.ShapeDtypeStruct((x.shape[0], width), BF16),
        scratch_shapes=[pltpu.VMEM(a.shape, BF16) for a in args]
        + [pltpu.SemaphoreType.DMA((len(args),))],
        compiler_params=params(32),
        name="experts",
    )(first, x, *stay(*args))


def row_major(value):
    return with_layout_constraint(value, Layout(major_to_minor=tuple(range(value.ndim))))


def exchange(value, axis):
    return lax.all_to_all(value, axis, split_axis=0, concat_axis=0, tiled=True)


def on_device(
    hidden_in,
    queries,
    new_keys,
    new_values,
    key_cache,
    value_cache,
    prompt_lengths,
    out_weight,
    norm_gain,
    expert_ids,
    top_logits,
    gate_weight,
    up_weight,
    down_weight,
):
    rows, steps, width = hidden_in.shape
    nz = lax.axis_size("z")
    ndp = lax.axis_size(("x", "y"))
    z = lax.axis_index("z")
    c = lax.axis_index("c")
    d = lax.axis_index(("x", "y"))
    out_rows = out_weight.T
    other_out = lax.ppermute(out_rows, "c", SWAP)
    weights = (gate_weight, up_weight, down_weight)
    swapped = [lax.ppermute(w, "c", SWAP) for w in weights]
    attended = attend(
        prompt_lengths, queries, new_keys, new_values, key_cache, value_cache, nz
    )
    attended, gate, up = lax.optimization_barrier((attended, gate_weight, up_weight))
    by_heads = exchange(attended, "z")
    gate, up = row_major(gate.swapaxes(1, 2)), row_major(up.swapaxes(1, 2))
    by_heads, gate, up = lax.optimization_barrier((by_heads, gate, up))
    parts = project(c[None], by_heads, out_rows, other_out)
    parts, down, far_down = lax.optimization_barrier((parts, down_weight, swapped[2]))
    parts = exchange(parts, "z")
    down, far_down = row_major(down), row_major(far_down)
    parts, down, far_down = lax.optimization_barrier((parts, down, far_down))
    ids = lax.dynamic_index_in_dim(expert_ids, d, 0, False).astype(F32)
    logits = lax.dynamic_index_in_dim(top_logits, d, 0, False).astype(F32)
    route = jnp.pad(jnp.concatenate([ids, logits], axis=1), ((0, 0), (0, 56)))
    residual, sent = norm(parts, hidden_in, norm_gain[None], route)
    sent, far_gate, far_up = lax.optimization_barrier((sent, swapped[0], swapped[1]))
    column = exchange(sent, "z")
    far_gate, far_up = row_major(far_gate.swapaxes(1, 2)), row_major(far_up.swapaxes(1, 2))
    column, far_gate, far_up = lax.optimization_barrier((column, far_gate, far_up))
    copies = spread(column, ndp)
    tokens = exchange(copies, ("x", "y")).reshape(ndp * nz * steps, -1)
    own = (gate, up, down)
    other = (far_gate, far_up, far_down)
    per = gate_weight.shape[0]
    first = jnp.stack([(2 * z + c) * per, (2 * z + 1 - c) * per]).astype(jnp.int32)
    made = experts(first, tokens, own, other)
    back = exchange(made.reshape(ndp, nz * steps, width), ("x", "y"))
    column_sum = jnp.sum(back.astype(F32), axis=0).astype(BF16)
    final = exchange(column_sum.reshape(nz, steps, width), "z")
    out = residual + jnp.sum(final.astype(F32), axis=0)
    return out.astype(BF16)[None]


def solution(mesh):
    shape = dict(mesh.shape)
    side = int(round(shape["dp"] ** 0.5))
    fine = Mesh(
        mesh.devices.reshape(side, shape["dp"] // side, shape["expert"] // 2, 2),
        ("x", "y", "z", "c"),
    )
    row = ("z", "c", "x", "y")
    group = ("z", "c")
    dp = ("x", "y")
    placed = (
        P(row, None, None),
        P(row, None, None),
        P(row, None, None),
        P(row, None, None),
        P(row, None, None),
        P(row, None, None),
        P(row),
        P(group, None),
        P(),
        P(group, None, None),
        P(group, None, None),
        P(group, None, dp),
        P(group, None, dp),
        P(group, dp, None),
    )
    return jax.shard_map(
        on_device,
        mesh=fine,
        in_specs=placed,
        out_specs=P(row, None, None),
        check_vma=False,
    )
```

```python
import jax
import jax.numpy as jnp
from jax import lax
from jax.experimental import pallas as pl
from jax.experimental.pallas import tpu as pltpu
from jax.sharding import Mesh
from jax.sharding import PartitionSpec as P

HQ = 64
KVH = 8
HD = 64
SWAP = [(0, 1), (1, 0)]
F32 = jnp.float32
BF16 = jnp.bfloat16


def params(mib):
    return pltpu.CompilerParams(vmem_limit_bytes=mib * 1024 * 1024)


def vmem():
    return pl.BlockSpec(memory_space=pltpu.VMEM)


def hbm():
    return pl.BlockSpec(memory_space=pltpu.HBM)


def stay(*values):
    return [pltpu.with_memory_space_constraint(v, pltpu.HBM) for v in values]


def smem():
    return pl.BlockSpec(memory_space=pltpu.SMEM)


def attend_kernel(
    len_ref, q_hbm, nk_hbm, nv_hbm, k_hbm, v_hbm, out_ref,
    q_ref, nk_ref, nv_ref, k_ref, v_ref, rows_ref, flat_ref, sems,
):
    pairs = (
        (k_hbm, k_ref), (q_hbm, q_ref), (nk_hbm, nk_ref), (nv_hbm, nv_ref), (v_hbm, v_ref),
    )
    copies = [pltpu.make_async_copy(a, b, sems.at[i]) for i, (a, b) in enumerate(pairs)]
    for copy in copies:
        copy.start()
    steps = q_ref.shape[1]
    width = KVH * HD
    rows = HQ * steps
    per_group = rows // KVH
    copies[1].wait()
    q = q_ref[0].astype(F32) * 0.125
    for h in range(HQ):
        rows_ref[h * steps : (h + 1) * steps, :] = q[:, h * HD : (h + 1) * HD]
    q_rows = rows_ref[...]
    q_pair = jnp.concatenate([q_rows, q_rows], axis=1)
    q_wide = jnp.concatenate([q_pair] * (KVH // 2), axis=1)
    row_id = lax.broadcasted_iota(jnp.int32, (rows, width), 0)
    col_id = lax.broadcasted_iota(jnp.int32, (rows, width), 1)
    in_group = row_id // per_group == col_id // HD
    q_wide = jnp.where(in_group, q_wide, 0.0)
    q_bf = q_wide.astype(BF16)
    copies[0].wait()
    scores = lax.dot_general(
        q_bf, k_ref[0], (((1,), (1,)), ((), ())), preferred_element_type=F32
    )
    slot = lax.broadcasted_iota(jnp.int32, scores.shape, 1)
    weights = jnp.where(slot < len_ref[0], jnp.exp(scores), 0.0)
    total = jnp.sum(weights, axis=1, keepdims=True)
    copies[2].wait()
    copies[3].wait()
    nk = nk_ref[0].astype(F32)
    nv = nv_ref[0].astype(F32)
    step_id = lax.broadcasted_iota(jnp.int32, (rows, 1), 0) % steps
    fresh = []
    for s in range(steps):
        score = jnp.sum(q_wide * nk[s : s + 1, :], axis=1, keepdims=True)
        weight = jnp.where(step_id >= s, jnp.exp(score), 0.0)
        total = total + weight
        fresh.append(weight)
    probs = (weights / total).astype(BF16)
    copies[4].wait()
    mixed = jnp.dot(probs, v_ref[0], preferred_element_type=F32)
    for s in range(steps):
        mixed = mixed + (fresh[s] / total).astype(BF16).astype(F32) * nv[s : s + 1, :]
    mixed = jnp.where(in_group, mixed, 0.0)
    folded = mixed[:, :128]
    for i in range(1, width // 128):
        folded = folded + mixed[:, i * 128 : (i + 1) * 128]
    rows_ref[...] = folded[:, :HD] + folded[:, HD:]
    for h in range(HQ):
        flat_ref[:, h * HD : (h + 1) * HD] = rows_ref[h * steps : (h + 1) * steps, :]
    blocks = out_ref.shape[0]
    wide = HQ * HD // blocks
    for b in range(blocks):
        out_ref[b] = flat_ref[:, b * wide : (b + 1) * wide].astype(BF16)


def attend(length, q, nk, nv, k, v, blocks):
    steps = q.shape[1]
    return pl.pallas_call(
        attend_kernel,
        in_specs=[smem()] + [hbm()] * 5,
        out_specs=vmem(),
        out_shape=jax.ShapeDtypeStruct((blocks, steps, HQ * HD // blocks), BF16),
        scratch_shapes=[pltpu.VMEM(a.shape, BF16) for a in (q, nk, nv, k, v)]
        + [
            pltpu.VMEM((HQ * steps, HD), F32),
            pltpu.VMEM((steps, HQ * HD), F32),
            pltpu.SemaphoreType.DMA((5,)),
        ],
        compiler_params=params(12),
        name="attend",
    )(length, *stay(q, nk, nv, k, v))


def project_kernel(
    place_ref, x_ref, hid_ref, route_ref, own_hbm, other_hbm, keep_ref, send_ref,
    rows_ref, own_ref, other_ref, sems,
):
    width, feats = own_ref.shape
    chunk = 640
    cuts = [(start, min(start + chunk, width)) for start in range(0, width, chunk)]
    copies = []
    for i, (start, stop) in enumerate(cuts):
        span = pl.ds(start, stop - start)
        copies.append(
            (
                pltpu.make_async_copy(own_hbm.at[span], own_ref.at[span], sems.at[2 * i]),
                pltpu.make_async_copy(other_hbm.at[span], other_ref.at[span], sems.at[2 * i + 1]),
            )
        )
        copies[-1][0].start()
        copies[-1][1].start()
    blocks, steps, _ = x_ref.shape
    for i in range(blocks):
        rows_ref[i * steps : (i + 1) * steps, :] = x_ref[i].astype(F32)
    x = rows_ref[...].astype(BF16)
    low, high = x[:, :feats], x[:, feats:]
    first = place_ref[1] == 0
    mine = jnp.where(first, low, high)
    theirs = jnp.where(first, high, low)
    extra = jnp.concatenate([hid_ref[0].astype(F32), route_ref[...]], axis=1)
    extra = jnp.concatenate([extra] * blocks, axis=0)
    block = lax.broadcasted_iota(jnp.int32, extra.shape, 0) // steps
    extra = jnp.where(block == place_ref[0], extra, 0.0)
    dims = (((1,), (1,)), ((), ()))
    for (start, stop), (first_copy, second_copy) in zip(cuts, copies):
        first_copy.wait()
        second_copy.wait()
        part = lax.dot_general(mine, own_ref[start:stop], dims, preferred_element_type=F32)
        part = part + lax.dot_general(
            theirs, other_ref[start:stop], dims, preferred_element_type=F32
        )
        part = part + extra[:, start:stop]
        keep_ref[:, start:stop] = part
        send_ref[:, start:stop] = part.astype(BF16)
    keep_ref[:, width:] = extra[:, width:]
    send_ref[:, width:] = extra[:, width:].astype(BF16)


def project(place, x, hidden, route, own, other):
    blocks, steps, feats = x.shape
    wide = own.shape[0] + route.shape[1]
    rows = blocks * steps
    return pl.pallas_call(
        project_kernel,
        in_specs=[smem(), vmem(), vmem(), vmem(), hbm(), hbm()],
        out_specs=[vmem(), vmem()],
        out_shape=[
            jax.ShapeDtypeStruct((rows, wide), F32),
            jax.ShapeDtypeStruct((rows, wide), BF16),
        ],
        scratch_shapes=[
            pltpu.VMEM((rows, feats), F32),
            pltpu.VMEM(own.shape, BF16),
            pltpu.VMEM(own.shape, BF16),
            pltpu.SemaphoreType.DMA((2 * pl.cdiv(own.shape[0], 640),)),
        ],
        compiler_params=params(12),
        name="project",
    )(place, x, hidden, route, *stay(own, other))


def pair_kernel(keep_ref, got_ref, out_ref):
    total = (keep_ref[...] + got_ref[...].astype(F32)).astype(BF16)
    for i in range(out_ref.shape[0]):
        out_ref[i] = total


def pair(keep, got, copies):
    return pl.pallas_call(
        pair_kernel,
        in_specs=[vmem(), vmem()],
        out_specs=vmem(),
        out_shape=jax.ShapeDtypeStruct((copies,) + keep.shape, BF16),
        compiler_params=params(12),
        name="pair",
    )(keep, got)


def norm_kernel(place_ref, part_ref, gain_ref, res_ref, out_ref):
    steps, width = res_ref.shape
    total = part_ref[0].astype(F32)
    for i in range(1, part_ref.shape[0]):
        total = total + part_ref[i].astype(F32)
    res = total[:, :width]
    own = jnp.zeros((steps, width), F32)
    for i in range(res.shape[0] // steps):
        own = own + jnp.where(place_ref[0] == i, res[i * steps : (i + 1) * steps, :], 0.0)
    res_ref[...] = own
    scale = lax.rsqrt(jnp.sum(res * res, axis=1, keepdims=True) / width + 1e-05)
    normed = (res * scale * gain_ref[...]).astype(BF16)
    full = jnp.concatenate([normed.astype(F32), total[:, width:]], axis=1).astype(BF16)
    for i in range(out_ref.shape[0]):
        out_ref[i] = full


def norm(place, parts, gain, copies, steps):
    _, rows, wide = parts.shape
    width = gain.shape[1]
    return pl.pallas_call(
        norm_kernel,
        in_specs=[smem(), vmem(), vmem()],
        out_specs=[vmem(), vmem()],
        out_shape=[
            jax.ShapeDtypeStruct((steps, width), F32),
            jax.ShapeDtypeStruct((copies, rows, wide), BF16),
        ],
        compiler_params=params(12),
        name="norm",
    )(place, parts, gain)


def experts_kernel(
    first_ref, x_ref, g0_hbm, u0_hbm, g1_hbm, u1_hbm, d0_hbm, d1_hbm, out_ref,
    w_ref, d_ref, act_ref, sems,
):
    rows, wide = g0_hbm.shape
    width = out_ref.shape[1]
    part = rows // 2
    pairs = (
        (g0_hbm, w_ref.at[0, pl.ds(0, rows)]), (u0_hbm, w_ref.at[0, pl.ds(rows, rows)]),
        (g1_hbm, w_ref.at[1, pl.ds(0, rows)]), (u1_hbm, w_ref.at[1, pl.ds(rows, rows)]),
        (d0_hbm, d_ref.at[pl.ds(0, rows)]), (d1_hbm, d_ref.at[pl.ds(rows, rows)]),
    )
    copies = [pltpu.make_async_copy(a, b, sems.at[i]) for i, (a, b) in enumerate(pairs)]
    for copy in copies:
        copy.start()
    x = x_ref[...]
    route = x_ref[:, width : width + 8].astype(F32)
    ids = route[:, 0:4]
    expo = jnp.exp(route[:, 4:8])
    total = jnp.sum(expo, axis=1, keepdims=True)
    column = lax.broadcasted_iota(jnp.int32, (x.shape[0], rows), 1)
    dims = (((1,), (1,)), ((), ()))
    for side in range(2):
        shares = []
        for e in range(2):
            label = (first_ref[side] + e).astype(F32)
            shares.append(
                jnp.sum(jnp.where(ids == label, expo, 0.0), axis=1, keepdims=True) / total
            )
        share = jnp.where(column < part, shares[0], shares[1])
        copies[2 * side].wait()
        copies[2 * side + 1].wait()
        both = lax.dot_general(x, w_ref[side], dims, preferred_element_type=F32)
        gate, up = both[:, :rows], both[:, rows:]
        act = gate * jax.nn.sigmoid(1.702 * gate) * (up + 1.0)
        act_ref[:, side * rows : (side + 1) * rows] = (act * share).astype(BF16)
    copies[4].wait()
    copies[5].wait()
    chunk = 768
    for start in range(0, width, chunk):
        stop = min(start + chunk, width)
        out_ref[:, start:stop] = jnp.dot(
            act_ref[...], d_ref[:, start:stop], preferred_element_type=F32
        ).astype(BF16)


def experts(first, x, own, other, width):
    rows, wide = own[0].shape
    args = (own[0], own[1], other[0], other[1], own[2], other[2])
    return pl.pallas_call(
        experts_kernel,
        in_specs=[smem(), vmem()] + [hbm()] * 6,
        out_specs=vmem(),
        out_shape=jax.ShapeDtypeStruct((x.shape[0], width), BF16),
        scratch_shapes=[
            pltpu.VMEM((2, 2 * rows, wide), BF16),
            pltpu.VMEM((2 * rows, wide), BF16),
            pltpu.VMEM((x.shape[0], 2 * rows), BF16),
            pltpu.SemaphoreType.DMA((len(args),)),
        ],
        compiler_params=params(32),
        name="experts",
    )(first, x, *stay(*args[:-1]), args[-1])


def stacked(value):
    per, rows, width = value.shape
    high, wide = rows + -rows % 64, width + -width % 128
    value = jnp.pad(value, ((0, 0), (0, high - rows), (0, wide - width)))
    return value.reshape(per * high, wide)


def exchange(value, axis):
    return lax.all_to_all(value, axis, split_axis=0, concat_axis=0, tiled=True)


def on_device(
    hidden_in,
    queries,
    new_keys,
    new_values,
    key_cache,
    value_cache,
    prompt_lengths,
    out_weight,
    norm_gain,
    expert_ids,
    top_logits,
    gate_weight,
    up_weight,
    down_weight,
):
    steps, width = hidden_in.shape[1:]
    zaxis = ("w", "v")
    dp = ("x", "y")
    nz = lax.axis_size(zaxis)
    ndp = lax.axis_size(dp)
    z = lax.axis_index(zaxis)
    c = lax.axis_index("c")
    d = lax.axis_index(dp)
    per = gate_weight.shape[0]
    out_rows = out_weight.T
    other_out = lax.ppermute(out_rows, "c", SWAP)
    attended = attend(
        prompt_lengths, queries, new_keys, new_values, key_cache, value_cache, nz
    )
    attended, gate = lax.optimization_barrier((attended, gate_weight))
    ids = lax.dynamic_index_in_dim(expert_ids, d, 0, False).astype(F32)
    logits = lax.dynamic_index_in_dim(top_logits, d, 0, False).astype(F32)
    route = jnp.pad(jnp.concatenate([ids, logits], axis=1), ((0, 0), (0, 56)))
    place = jnp.stack([z, c]).astype(jnp.int32)
    first = jnp.stack([(2 * z + c) * per, (2 * z + 1 - c) * per]).astype(jnp.int32)
    by_heads = exchange(attended, zaxis)
    gate = stacked(gate.swapaxes(1, 2))
    by_heads, gate, route, place, first = lax.optimization_barrier(
        (by_heads, gate, route, place, first)
    )
    far_gate = lax.ppermute(gate, "c", SWAP)
    keep, sent = project(place, by_heads, hidden_in, route, out_rows, other_out)
    sent, up = lax.optimization_barrier((sent, up_weight))
    got = lax.ppermute(sent, "v", SWAP)
    up = stacked(up.swapaxes(1, 2))
    got, up = lax.optimization_barrier((got, up))
    far_up = lax.ppermute(up, "c", SWAP)
    quads = pair(keep, got, nz // 2)
    quads, down = lax.optimization_barrier((quads, down_weight))
    parts = exchange(quads, "w")
    down = stacked(down)
    parts, down = lax.optimization_barrier((parts, down))
    far_down = lax.ppermute(down, "c", SWAP)
    residual, copies = norm(place, parts, norm_gain[None], ndp, steps)
    copies, far_gate, far_up, far_down = lax.optimization_barrier(
        (copies, far_gate, far_up, far_down)
    )
    tokens = exchange(copies, dp).reshape(ndp * nz * steps, -1)
    made = experts(first, tokens, (gate, up, down), (far_gate, far_up, far_down), width)
    back = exchange(made.reshape(ndp, nz * steps, width), dp)
    column_sum = jnp.sum(back.astype(F32), axis=0).astype(BF16)
    final = exchange(column_sum.reshape(nz, steps, width), zaxis)
    out = residual + jnp.sum(final.astype(F32), axis=0)
    return out.astype(BF16)[None]


def solution(mesh):
    shape = dict(mesh.shape)
    side = int(round(shape["dp"] ** 0.5))
    fine = Mesh(
        mesh.devices.reshape(side, shape["dp"] // side, shape["expert"] // 4, 2, 2),
        ("x", "y", "w", "v", "c"),
    )
    row = ("w", "v", "c", "x", "y")
    group = ("w", "v", "c")
    dp = ("x", "y")
    placed = (
        P(row, None, None),
        P(row, None, None),
        P(row, None, None),
        P(row, None, None),
        P(row, None, None),
        P(row, None, None),
        P(row),
        P(group, None),
        P(),
        P(group, None, None),
        P(group, None, None),
        P(group, None, dp),
        P(group, None, dp),
        P(group, dp, None),
    )
    return jax.shard_map(
        on_device,
        mesh=fine,
        in_specs=placed,
        out_specs=P(row, None, None),
        check_vma=False,
    )
```

```python
import jax
import jax.numpy as jnp
from jax import lax
from jax.experimental import pallas as pl
from jax.experimental.pallas import tpu as pltpu
from jax.experimental.layout import Layout, with_layout_constraint
from jax.sharding import Mesh
from jax.sharding import PartitionSpec as P

HQ = 64
KVH = 8
HD = 64
SWAP = [(0, 1), (1, 0)]
F32 = jnp.float32
BF16 = jnp.bfloat16


def params(mib):
    return pltpu.CompilerParams(vmem_limit_bytes=mib * 1024 * 1024)


def vmem():
    return pl.BlockSpec(memory_space=pltpu.VMEM)


def hbm():
    return pl.BlockSpec(memory_space=pltpu.HBM)


def stay(*values):
    return [pltpu.with_memory_space_constraint(v, pltpu.HBM) for v in values]


def smem():
    return pl.BlockSpec(memory_space=pltpu.SMEM)


def attend_kernel(
    len_ref, q_hbm, nk_hbm, nv_hbm, k_hbm, v_hbm, out_ref,
    q_ref, nk_ref, nv_ref, k_ref, v_ref, rows_ref, flat_ref, sems,
):
    pairs = (
        (k_hbm, k_ref), (q_hbm, q_ref), (nk_hbm, nk_ref), (nv_hbm, nv_ref), (v_hbm, v_ref),
    )
    copies = [pltpu.make_async_copy(a, b, sems.at[i]) for i, (a, b) in enumerate(pairs)]
    for copy in copies:
        copy.start()
    steps = q_ref.shape[1]
    width = KVH * HD
    rows = HQ * steps
    per_group = rows // KVH
    copies[1].wait()
    q = q_ref[0].astype(F32) * 0.125
    for h in range(HQ):
        rows_ref[h * steps : (h + 1) * steps, :] = q[:, h * HD : (h + 1) * HD]
    q_rows = rows_ref[...]
    q_pair = jnp.concatenate([q_rows, q_rows], axis=1)
    q_wide = jnp.concatenate([q_pair] * (KVH // 2), axis=1)
    row_id = lax.broadcasted_iota(jnp.int32, (rows, width), 0)
    col_id = lax.broadcasted_iota(jnp.int32, (rows, width), 1)
    in_group = row_id // per_group == col_id // HD
    q_wide = jnp.where(in_group, q_wide, 0.0)
    q_bf = q_wide.astype(BF16)
    copies[0].wait()
    scores = lax.dot_general(
        q_bf, k_ref[0], (((1,), (1,)), ((), ())), preferred_element_type=F32
    )
    slot = lax.broadcasted_iota(jnp.int32, scores.shape, 1)
    weights = jnp.where(slot < len_ref[0], jnp.exp(scores), 0.0)
    total = jnp.sum(weights, axis=1, keepdims=True)
    copies[2].wait()
    copies[3].wait()
    nk = nk_ref[0].astype(F32)
    nv = nv_ref[0].astype(F32)
    step_id = lax.broadcasted_iota(jnp.int32, (rows, 1), 0) % steps
    fresh = []
    for s in range(steps):
        score = jnp.sum(q_wide * nk[s : s + 1, :], axis=1, keepdims=True)
        weight = jnp.where(step_id >= s, jnp.exp(score), 0.0)
        total = total + weight
        fresh.append(weight)
    probs = (weights / total).astype(BF16)
    copies[4].wait()
    mixed = jnp.dot(probs, v_ref[0], preferred_element_type=F32)
    for s in range(steps):
        mixed = mixed + (fresh[s] / total).astype(BF16).astype(F32) * nv[s : s + 1, :]
    mixed = jnp.where(in_group, mixed, 0.0)
    folded = mixed[:, :128]
    for i in range(1, width // 128):
        folded = folded + mixed[:, i * 128 : (i + 1) * 128]
    rows_ref[...] = folded[:, :HD] + folded[:, HD:]
    for h in range(HQ):
        flat_ref[:, h * HD : (h + 1) * HD] = rows_ref[h * steps : (h + 1) * steps, :]
    blocks = out_ref.shape[0]
    wide = HQ * HD // blocks
    for b in range(blocks):
        out_ref[b] = flat_ref[:, b * wide : (b + 1) * wide].astype(BF16)


def attend(length, q, nk, nv, k, v, blocks):
    steps = q.shape[1]
    return pl.pallas_call(
        attend_kernel,
        in_specs=[smem()] + [hbm()] * 5,
        out_specs=vmem(),
        out_shape=jax.ShapeDtypeStruct((blocks, steps, HQ * HD // blocks), BF16),
        scratch_shapes=[pltpu.VMEM(a.shape, BF16) for a in (q, nk, nv, k, v)]
        + [
            pltpu.VMEM((HQ * steps, HD), F32),
            pltpu.VMEM((steps, HQ * HD), F32),
            pltpu.SemaphoreType.DMA((5,)),
        ],
        compiler_params=params(12),
        name="attend",
    )(length, *stay(q, nk, nv, k, v))


def project_kernel(
    place_ref, x_ref, hid_ref, route_ref, own_hbm, other_hbm, keep_ref, send_ref,
    rows_ref, own_ref, other_ref, sems,
):
    width, feats = own_ref.shape
    chunk = 640
    cuts = [(start, min(start + chunk, width)) for start in range(0, width, chunk)]
    copies = []
    for i, (start, stop) in enumerate(cuts):
        span = pl.ds(start, stop - start)
        copies.append(
            (
                pltpu.make_async_copy(own_hbm.at[span], own_ref.at[span], sems.at[2 * i]),
                pltpu.make_async_copy(other_hbm.at[span], other_ref.at[span], sems.at[2 * i + 1]),
            )
        )
        copies[-1][0].start()
        copies[-1][1].start()
    blocks, steps, _ = x_ref.shape
    for i in range(blocks):
        rows_ref[i * steps : (i + 1) * steps, :] = x_ref[i].astype(F32)
    x = rows_ref[...].astype(BF16)
    low, high = x[:, :feats], x[:, feats:]
    first = place_ref[1] == 0
    mine = jnp.where(first, low, high)
    theirs = jnp.where(first, high, low)
    extra = jnp.concatenate([hid_ref[0].astype(F32), route_ref[...]], axis=1)
    extra = jnp.concatenate([extra] * blocks, axis=0)
    block = lax.broadcasted_iota(jnp.int32, extra.shape, 0) // steps
    extra = jnp.where(block == place_ref[0], extra, 0.0)
    dims = (((1,), (1,)), ((), ()))
    for (start, stop), (first_copy, second_copy) in zip(cuts, copies):
        first_copy.wait()
        second_copy.wait()
        part = lax.dot_general(mine, own_ref[start:stop], dims, preferred_element_type=F32)
        part = part + lax.dot_general(
            theirs, other_ref[start:stop], dims, preferred_element_type=F32
        )
        part = part + extra[:, start:stop]
        keep_ref[:, start:stop] = part
        send_ref[:, start:stop] = part.astype(BF16)
    keep_ref[:, width:] = extra[:, width:]
    send_ref[:, width:] = extra[:, width:].astype(BF16)


def project(place, x, hidden, route, own, other):
    blocks, steps, feats = x.shape
    wide = own.shape[0] + route.shape[1]
    rows = blocks * steps
    return pl.pallas_call(
        project_kernel,
        in_specs=[smem(), vmem(), vmem(), vmem(), hbm(), hbm()],
        out_specs=[vmem(), vmem()],
        out_shape=[
            jax.ShapeDtypeStruct((rows, wide), F32),
            jax.ShapeDtypeStruct((rows, wide), BF16),
        ],
        scratch_shapes=[
            pltpu.VMEM((rows, feats), F32),
            pltpu.VMEM(own.shape, BF16),
            pltpu.VMEM(own.shape, BF16),
            pltpu.SemaphoreType.DMA((2 * pl.cdiv(own.shape[0], 640),)),
        ],
        compiler_params=params(12),
        name="project",
    )(place, x, hidden, route, *stay(own, other))


def pair_kernel(keep_ref, got_ref, out_ref):
    total = (keep_ref[...] + got_ref[...].astype(F32)).astype(BF16)
    for i in range(out_ref.shape[0]):
        out_ref[i] = total


def pair(keep, got, copies):
    return pl.pallas_call(
        pair_kernel,
        in_specs=[vmem(), vmem()],
        out_specs=vmem(),
        out_shape=jax.ShapeDtypeStruct((copies,) + keep.shape, BF16),
        compiler_params=params(12),
        name="pair",
    )(keep, got)


def norm_kernel(place_ref, part_ref, gain_ref, res_ref, out_ref):
    steps, width = res_ref.shape
    total = part_ref[0].astype(F32)
    for i in range(1, part_ref.shape[0]):
        total = total + part_ref[i].astype(F32)
    res = total[:, :width]
    own = jnp.zeros((steps, width), F32)
    for i in range(res.shape[0] // steps):
        own = own + jnp.where(place_ref[0] == i, res[i * steps : (i + 1) * steps, :], 0.0)
    res_ref[...] = own
    scale = lax.rsqrt(jnp.sum(res * res, axis=1, keepdims=True) / width + 1e-05)
    normed = (res * scale * gain_ref[...]).astype(BF16)
    full = jnp.concatenate([normed.astype(F32), total[:, width:]], axis=1).astype(BF16)
    for i in range(out_ref.shape[0]):
        out_ref[i] = full


def norm(place, parts, gain, copies, steps):
    _, rows, wide = parts.shape
    width = gain.shape[1]
    return pl.pallas_call(
        norm_kernel,
        in_specs=[smem(), vmem(), vmem()],
        out_specs=[vmem(), vmem()],
        out_shape=[
            jax.ShapeDtypeStruct((steps, width), F32),
            jax.ShapeDtypeStruct((copies, rows, wide), BF16),
        ],
        compiler_params=params(12),
        name="norm",
    )(place, parts, gain)


def experts_kernel(
    first_ref, x_ref, g0_hbm, u0_hbm, g1_hbm, u1_hbm, d0_hbm, d1_hbm, out_ref,
    g0, u0, g1, u1, d0, d1, sems,
):
    pairs = (
        (g0_hbm, g0), (u0_hbm, u0), (g1_hbm, g1), (u1_hbm, u1), (d0_hbm, d0), (d1_hbm, d1),
    )
    per, _, width = g0.shape
    copies = []
    for i, (a, b) in enumerate(pairs):
        copies.append(
            [pltpu.make_async_copy(a.at[e], b.at[e], sems.at[i, e]) for e in range(per)]
        )
    for side in (0, 2):
        for e in range(per):
            copies[side][e].start()
            copies[side + 1][e].start()
    for i in (4, 5):
        for e in range(per):
            copies[i][e].start()
    x = x_ref[:, :width]
    route = x_ref[:, width : width + 8].astype(F32)
    ids = route[:, 0:4]
    expo = jnp.exp(route[:, 4:8])
    total = jnp.sum(expo, axis=1, keepdims=True)
    dims = (((1,), (1,)), ((), ()))
    acts = []
    for side, (g_ref, u_ref) in enumerate(((g0, u0), (g1, u1))):
        for e in range(per):
            copies[2 * side][e].wait()
            gate = lax.dot_general(x, g_ref[e], dims, preferred_element_type=F32)
            copies[2 * side + 1][e].wait()
            up = lax.dot_general(x, u_ref[e], dims, preferred_element_type=F32)
            act = gate * jax.nn.sigmoid(1.702 * gate) * (up + 1.0)
            label = (first_ref[side] + e).astype(F32)
            share = jnp.sum(jnp.where(ids == label, expo, 0.0), axis=1, keepdims=True) / total
            acts.append((act * share).astype(BF16))
    for i in (4, 5):
        for e in range(per):
            copies[i][e].wait()
    chunk = 768
    for start in range(0, width, chunk):
        stop = min(start + chunk, width)
        part = None
        for side, d_ref in enumerate((d0, d1)):
            for e in range(per):
                piece = jnp.dot(
                    acts[side * per + e], d_ref[e, :, start:stop], preferred_element_type=F32
                )
                part = piece if part is None else part + piece
        out_ref[:, start:stop] = part.astype(BF16)


def experts(first, x, own, other):
    width = own[0].shape[2]
    args = (own[0], own[1], other[0], other[1], own[2], other[2])
    return pl.pallas_call(
        experts_kernel,
        in_specs=[smem(), vmem()] + [hbm()] * 6,
        out_specs=vmem(),
        out_shape=jax.ShapeDtypeStruct((x.shape[0], width), BF16),
        scratch_shapes=[pltpu.VMEM(a.shape, BF16) for a in args]
        + [pltpu.SemaphoreType.DMA((len(args), own[0].shape[0]))],
        compiler_params=params(32),
        name="experts",
    )(first, x, *stay(*args))


def row_major(value):
    return with_layout_constraint(value, Layout(major_to_minor=tuple(range(value.ndim))))


def exchange(value, axis):
    return lax.all_to_all(value, axis, split_axis=0, concat_axis=0, tiled=True)


def on_device(
    hidden_in,
    queries,
    new_keys,
    new_values,
    key_cache,
    value_cache,
    prompt_lengths,
    out_weight,
    norm_gain,
    expert_ids,
    top_logits,
    gate_weight,
    up_weight,
    down_weight,
):
    steps, width = hidden_in.shape[1:]
    zaxis = ("w", "v")
    dp = ("x", "y")
    nz = lax.axis_size(zaxis)
    ndp = lax.axis_size(dp)
    z = lax.axis_index(zaxis)
    c = lax.axis_index("c")
    d = lax.axis_index(dp)
    per = gate_weight.shape[0]
    out_rows = out_weight.T
    other_out = lax.ppermute(out_rows, "c", SWAP)
    weights = [gate_weight, up_weight, down_weight]
    weights += [lax.ppermute(w, "c", SWAP) for w in weights]
    attended = attend(
        prompt_lengths, queries, new_keys, new_values, key_cache, value_cache, nz
    )
    ids = lax.dynamic_index_in_dim(expert_ids, d, 0, False).astype(F32)
    logits = lax.dynamic_index_in_dim(top_logits, d, 0, False).astype(F32)
    route = jnp.pad(jnp.concatenate([ids, logits], axis=1), ((0, 0), (0, 56)))
    place = jnp.stack([z, c]).astype(jnp.int32)
    first = jnp.stack([(2 * z + c) * per, (2 * z + 1 - c) * per]).astype(jnp.int32)
    gain = norm_gain[None]
    attended, route, place, first, gain = lax.optimization_barrier(
        (attended, route, place, first, gain)
    )
    by_heads = exchange(attended, zaxis)
    keep, sent = project(place, by_heads, hidden_in, route, out_rows, other_out)
    got = lax.ppermute(sent, "v", SWAP)
    quads = pair(keep, got, nz // 2)
    parts = exchange(quads, "w")
    residual, copies = norm(place, parts, gain, ndp, steps)
    copies, *weights = lax.optimization_barrier((copies, *weights))
    tokens = exchange(copies, dp)
    relaid = [
        row_major(w if i % 3 == 2 else w.swapaxes(1, 2)) for i, w in enumerate(weights)
    ]
    tokens, *relaid = lax.optimization_barrier((tokens, *relaid))
    tokens = tokens.reshape(ndp * nz * steps, -1)
    made = experts(first, tokens, relaid[:3], relaid[3:])
    back = exchange(made.reshape(ndp, nz * steps, width), dp)
    column_sum = jnp.sum(back.astype(F32), axis=0).astype(BF16)
    final = exchange(column_sum.reshape(nz, steps, width), zaxis)
    out = residual + jnp.sum(final.astype(F32), axis=0)
    return out.astype(BF16)[None]


def solution(mesh):
    shape = dict(mesh.shape)
    side = int(round(shape["dp"] ** 0.5))
    fine = Mesh(
        mesh.devices.reshape(side, shape["dp"] // side, shape["expert"] // 4, 2, 2),
        ("x", "y", "w", "v", "c"),
    )
    row = ("w", "v", "c", "x", "y")
    group = ("w", "v", "c")
    dp = ("x", "y")
    placed = (
        P(row, None, None),
        P(row, None, None),
        P(row, None, None),
        P(row, None, None),
        P(row, None, None),
        P(row, None, None),
        P(row),
        P(group, None),
        P(),
        P(group, None, None),
        P(group, None, None),
        P(group, None, dp),
        P(group, None, dp),
        P(group, dp, None),
    )
    return jax.shard_map(
        on_device,
        mesh=fine,
        in_specs=placed,
        out_specs=P(row, None, None),
        check_vma=False,
    )
```

```python
import jax
import jax.numpy as jnp
from jax import lax
from jax.experimental import pallas as pl
from jax.experimental.pallas import tpu as pltpu
from jax.experimental.layout import Layout, with_layout_constraint
from jax.sharding import Mesh
from jax.sharding import PartitionSpec as P

HQ = 64
KVH = 8
HD = 64
SWAP = [(0, 1), (1, 0)]
F32 = jnp.float32
BF16 = jnp.bfloat16


def params(mib):
    return pltpu.CompilerParams(vmem_limit_bytes=mib * 1024 * 1024)


def vmem():
    return pl.BlockSpec(memory_space=pltpu.VMEM)


def hbm():
    return pl.BlockSpec(memory_space=pltpu.HBM)


def stay(*values):
    return [pltpu.with_memory_space_constraint(v, pltpu.HBM) for v in values]


def smem():
    return pl.BlockSpec(memory_space=pltpu.SMEM)


def attend_kernel(
    len_ref, q_hbm, nk_hbm, nv_hbm, k_hbm, v_hbm, out_ref,
    q_ref, nk_ref, nv_ref, k_ref, v_ref, rows_ref, flat_ref, sems,
):
    pairs = (
        (k_hbm, k_ref), (q_hbm, q_ref), (nk_hbm, nk_ref), (nv_hbm, nv_ref), (v_hbm, v_ref),
    )
    copies = [pltpu.make_async_copy(a, b, sems.at[i]) for i, (a, b) in enumerate(pairs)]
    for copy in copies:
        copy.start()
    steps = q_ref.shape[1]
    width = KVH * HD
    rows = HQ * steps
    per_group = rows // KVH
    copies[1].wait()
    q = q_ref[0].astype(F32) * 0.125
    for h in range(HQ):
        rows_ref[h * steps : (h + 1) * steps, :] = q[:, h * HD : (h + 1) * HD]
    q_rows = rows_ref[...]
    q_pair = jnp.concatenate([q_rows, q_rows], axis=1)
    q_wide = jnp.concatenate([q_pair] * (KVH // 2), axis=1)
    row_id = lax.broadcasted_iota(jnp.int32, (rows, width), 0)
    col_id = lax.broadcasted_iota(jnp.int32, (rows, width), 1)
    in_group = row_id // per_group == col_id // HD
    q_wide = jnp.where(in_group, q_wide, 0.0)
    q_bf = q_wide.astype(BF16)
    copies[0].wait()
    scores = lax.dot_general(
        q_bf, k_ref[0], (((1,), (1,)), ((), ())), preferred_element_type=F32
    )
    slot = lax.broadcasted_iota(jnp.int32, scores.shape, 1)
    weights = jnp.where(slot < len_ref[0], jnp.exp(scores), 0.0)
    total = jnp.sum(weights, axis=1, keepdims=True)
    copies[2].wait()
    copies[3].wait()
    nk = nk_ref[0].astype(F32)
    nv = nv_ref[0].astype(F32)
    step_id = lax.broadcasted_iota(jnp.int32, (rows, 1), 0) % steps
    fresh = []
    for s in range(steps):
        score = jnp.sum(q_wide * nk[s : s + 1, :], axis=1, keepdims=True)
        weight = jnp.where(step_id >= s, jnp.exp(score), 0.0)
        total = total + weight
        fresh.append(weight)
    probs = (weights / total).astype(BF16)
    copies[4].wait()
    mixed = jnp.dot(probs, v_ref[0], preferred_element_type=F32)
    for s in range(steps):
        mixed = mixed + (fresh[s] / total).astype(BF16).astype(F32) * nv[s : s + 1, :]
    mixed = jnp.where(in_group, mixed, 0.0)
    folded = mixed[:, :128]
    for i in range(1, width // 128):
        folded = folded + mixed[:, i * 128 : (i + 1) * 128]
    rows_ref[...] = folded[:, :HD] + folded[:, HD:]
    for h in range(HQ):
        flat_ref[:, h * HD : (h + 1) * HD] = rows_ref[h * steps : (h + 1) * steps, :]
    blocks = out_ref.shape[0]
    wide = HQ * HD // blocks
    for b in range(blocks):
        out_ref[b] = flat_ref[:, b * wide : (b + 1) * wide].astype(BF16)


def attend(length, q, nk, nv, k, v, blocks):
    steps = q.shape[1]
    return pl.pallas_call(
        attend_kernel,
        in_specs=[smem()] + [hbm()] * 5,
        out_specs=vmem(),
        out_shape=jax.ShapeDtypeStruct((blocks, steps, HQ * HD // blocks), BF16),
        scratch_shapes=[pltpu.VMEM(a.shape, BF16) for a in (q, nk, nv, k, v)]
        + [
            pltpu.VMEM((HQ * steps, HD), F32),
            pltpu.VMEM((steps, HQ * HD), F32),
            pltpu.SemaphoreType.DMA((5,)),
        ],
        compiler_params=params(12),
        name="attend",
    )(length, *stay(q, nk, nv, k, v))


def project_kernel(
    place_ref, x_ref, hid_hbm, ids_hbm, logits_hbm, own_hbm, other_hbm, keep_ref, send_ref,
    rows_ref, hid_ref, ids_ref, logits_ref, own_ref, other_ref, sems,
):
    width, feats = own_ref.shape
    chunk = 640
    cuts = [(start, min(start + chunk, width)) for start in range(0, width, chunk)]
    small = [
        pltpu.make_async_copy(hid_hbm, hid_ref, sems.at[0]),
        pltpu.make_async_copy(ids_hbm, ids_ref, sems.at[1]),
        pltpu.make_async_copy(logits_hbm, logits_ref, sems.at[2]),
    ]
    copies = []
    for i, (start, stop) in enumerate(cuts):
        span = pl.ds(start, stop - start)
        copies.append(
            (
                pltpu.make_async_copy(own_hbm.at[span], own_ref.at[span], sems.at[2 * i + 3]),
                pltpu.make_async_copy(other_hbm.at[span], other_ref.at[span], sems.at[2 * i + 4]),
            )
        )
    for copy in small:
        copy.start()
    for pair_copies in copies:
        pair_copies[0].start()
        pair_copies[1].start()
    blocks, steps, _ = x_ref.shape
    for i in range(blocks):
        rows_ref[i * steps : (i + 1) * steps, :] = x_ref[i].astype(F32)
    x = rows_ref[...].astype(BF16)
    low, high = x[:, :feats], x[:, feats:]
    first = place_ref[1] == 0
    mine = jnp.where(first, low, high)
    theirs = jnp.where(first, high, low)
    for copy in small:
        copy.wait()
    spare = keep_ref.shape[1] - width
    lane = lax.broadcasted_iota(jnp.int32, (1, spare), 1)
    routes = []
    for ref in (ids_ref, logits_ref):
        held = ref[...].astype(F32)
        row = lax.broadcasted_iota(jnp.int32, held.shape, 2)
        routes.append(
            jnp.sum(jnp.where(row == place_ref[2], held, 0.0), axis=2, keepdims=True)
        )
    top = routes[0].shape[1]
    lines = []
    for s in range(steps):
        line = jnp.zeros((1, spare), F32)
        for i, values in enumerate(routes):
            for k in range(top):
                line = jnp.where(lane == i * top + k, values[s, k : k + 1, :], line)
        lines.append(line)
    route = jnp.concatenate(lines, axis=0)
    extra = jnp.concatenate([hid_ref[0].astype(F32), route], axis=1)
    extra = jnp.concatenate([extra] * blocks, axis=0)
    block = lax.broadcasted_iota(jnp.int32, extra.shape, 0) // steps
    extra = jnp.where(block == place_ref[0], extra, 0.0)
    dims = (((1,), (1,)), ((), ()))
    for (start, stop), (first_copy, second_copy) in zip(cuts, copies):
        first_copy.wait()
        second_copy.wait()
        part = lax.dot_general(mine, own_ref[start:stop], dims, preferred_element_type=F32)
        part = part + lax.dot_general(
            theirs, other_ref[start:stop], dims, preferred_element_type=F32
        )
        part = part + extra[:, start:stop]
        keep_ref[:, start:stop] = part
        send_ref[:, start:stop] = part.astype(BF16)
    keep_ref[:, width:] = extra[:, width:]
    send_ref[:, width:] = extra[:, width:].astype(BF16)


def project(place, x, hidden, ids, logits, own, other):
    blocks, steps, feats = x.shape
    wide = own.shape[0] + -own.shape[0] % 128
    rows = blocks * steps
    return pl.pallas_call(
        project_kernel,
        in_specs=[smem(), vmem()] + [hbm()] * 5,
        out_specs=[vmem(), vmem()],
        out_shape=[
            jax.ShapeDtypeStruct((rows, wide), F32),
            jax.ShapeDtypeStruct((rows, wide), BF16),
        ],
        scratch_shapes=[
            pltpu.VMEM((rows, feats), F32),
            pltpu.VMEM(hidden.shape, BF16),
            pltpu.VMEM(ids.shape, jnp.int32),
            pltpu.VMEM(logits.shape, BF16),
            pltpu.VMEM(own.shape, BF16),
            pltpu.VMEM(own.shape, BF16),
            pltpu.SemaphoreType.DMA((2 * pl.cdiv(own.shape[0], 640) + 3,)),
        ],
        compiler_params=params(12),
        name="project",
    )(place, x, *stay(hidden, ids, logits, own), other)


def pair_kernel(keep_ref, got_ref, out_ref):
    total = (keep_ref[...] + got_ref[...].astype(F32)).astype(BF16)
    for i in range(out_ref.shape[0]):
        out_ref[i] = total


def pair(keep, got, copies):
    return pl.pallas_call(
        pair_kernel,
        in_specs=[vmem(), vmem()],
        out_specs=vmem(),
        out_shape=jax.ShapeDtypeStruct((copies,) + keep.shape, BF16),
        compiler_params=params(12),
        name="pair",
    )(keep, got)


def norm_kernel(place_ref, part_ref, gain_ref, res_ref, out_hbm, full_ref, sems):
    steps, width = res_ref.shape
    total = part_ref[0].astype(F32)
    for i in range(1, part_ref.shape[0]):
        total = total + part_ref[i].astype(F32)
    res = total[:, :width]
    scale = lax.rsqrt(jnp.sum(res * res, axis=1, keepdims=True) / width + 1e-05)
    normed = (res * scale * gain_ref[...]).astype(BF16)
    full_ref[...] = jnp.concatenate([normed.astype(F32), total[:, width:]], axis=1).astype(BF16)
    copies = [
        pltpu.make_async_copy(full_ref, out_hbm.at[i], sems.at[i])
        for i in range(out_hbm.shape[0])
    ]
    for copy in copies:
        copy.start()
    own = jnp.zeros((steps, width), F32)
    for i in range(res.shape[0] // steps):
        own = own + jnp.where(place_ref[0] == i, res[i * steps : (i + 1) * steps, :], 0.0)
    res_ref[...] = own
    for copy in copies:
        copy.wait()


def norm(place, parts, gain, copies, steps):
    _, rows, wide = parts.shape
    width = gain.shape[1]
    return pl.pallas_call(
        norm_kernel,
        in_specs=[smem(), vmem(), vmem()],
        out_specs=[vmem(), hbm()],
        out_shape=[
            jax.ShapeDtypeStruct((steps, width), F32),
            jax.ShapeDtypeStruct((copies, rows, wide), BF16),
        ],
        scratch_shapes=[pltpu.VMEM((rows, wide), BF16), pltpu.SemaphoreType.DMA((copies,))],
        compiler_params=params(12),
        name="norm",
    )(place, parts, gain)


def experts_kernel(
    first_ref, x_ref, g0_hbm, u0_hbm, g1_hbm, u1_hbm, d0_hbm, d1_hbm, out_ref,
    g0, u0, g1, u1, d0, d1, sems,
):
    pairs = (
        (g0_hbm, g0), (u0_hbm, u0), (g1_hbm, g1), (u1_hbm, u1), (d0_hbm, d0), (d1_hbm, d1),
    )
    per, _, width = g0.shape
    copies = [pltpu.make_async_copy(a, b, sems.at[i]) for i, (a, b) in enumerate(pairs)]
    for copy in copies:
        copy.start()
    x = x_ref[:, :width]
    route = x_ref[:, width : width + 8].astype(F32)
    ids = route[:, 0:4]
    expo = jnp.exp(route[:, 4:8])
    total = jnp.sum(expo, axis=1, keepdims=True)
    dims = (((1,), (1,)), ((), ()))
    acts = []
    for side, (g_ref, u_ref) in enumerate(((g0, u0), (g1, u1))):
        copies[2 * side].wait()
        gates = [
            lax.dot_general(x, g_ref[e], dims, preferred_element_type=F32) for e in range(per)
        ]
        copies[2 * side + 1].wait()
        for e in range(per):
            gate = gates[e]
            up = lax.dot_general(x, u_ref[e], dims, preferred_element_type=F32)
            act = gate * jax.nn.sigmoid(1.702 * gate) * (up + 1.0)
            label = (first_ref[side] + e).astype(F32)
            share = jnp.sum(jnp.where(ids == label, expo, 0.0), axis=1, keepdims=True) / total
            acts.append((act * share).astype(BF16))
    copies[4].wait()
    copies[5].wait()
    chunk = 768
    for start in range(0, width, chunk):
        stop = min(start + chunk, width)
        part = None
        for side, d_ref in enumerate((d0, d1)):
            for e in range(per):
                piece = jnp.dot(
                    acts[side * per + e], d_ref[e, :, start:stop], preferred_element_type=F32
                )
                part = piece if part is None else part + piece
        out_ref[:, start:stop] = part.astype(BF16)


def experts(first, x, own, other):
    width = own[0].shape[2]
    args = (own[0], own[1], other[0], other[1], own[2], other[2])
    return pl.pallas_call(
        experts_kernel,
        in_specs=[smem(), vmem()] + [hbm()] * 6,
        out_specs=vmem(),
        out_shape=jax.ShapeDtypeStruct((x.shape[0], width), BF16),
        scratch_shapes=[pltpu.VMEM(a.shape, BF16) for a in args]
        + [pltpu.SemaphoreType.DMA((len(args),))],
        compiler_params=params(32),
        name="experts",
    )(first, x, *stay(*args))


def row_major(value):
    return with_layout_constraint(value, Layout(major_to_minor=tuple(range(value.ndim))))


def exchange(value, axis):
    return lax.all_to_all(value, axis, split_axis=0, concat_axis=0, tiled=True)


def on_device(
    hidden_in,
    queries,
    new_keys,
    new_values,
    key_cache,
    value_cache,
    prompt_lengths,
    out_weight,
    norm_gain,
    expert_ids,
    top_logits,
    gate_weight,
    up_weight,
    down_weight,
):
    steps, width = hidden_in.shape[1:]
    zaxis = ("w", "v")
    dp = ("x", "y")
    nz = lax.axis_size(zaxis)
    ndp = lax.axis_size(dp)
    z = lax.axis_index(zaxis)
    c = lax.axis_index("c")
    d = lax.axis_index(dp)
    per = gate_weight.shape[0]
    out_rows = out_weight.T
    other_out = lax.ppermute(out_rows, "c", SWAP)
    weights = [gate_weight, up_weight, down_weight]
    weights += [lax.ppermute(w, "c", SWAP) for w in weights]
    attended = attend(
        prompt_lengths, queries, new_keys, new_values, key_cache, value_cache, nz
    )
    place = jnp.stack([z, c, d]).astype(jnp.int32)
    first = jnp.stack([(2 * z + c) * per, (2 * z + 1 - c) * per]).astype(jnp.int32)
    attended, place, first = lax.optimization_barrier((attended, place, first))
    by_heads = exchange(attended, zaxis)
    ids, logits = expert_ids.transpose(1, 2, 0), top_logits.transpose(1, 2, 0)
    keep, sent = project(place, by_heads, hidden_in, ids, logits, out_rows, other_out)
    sent, gain = lax.optimization_barrier((sent, norm_gain))
    got = lax.ppermute(sent, "v", SWAP)
    got, gain = lax.optimization_barrier((got, gain[None]))
    quads = pair(keep, got, nz // 2)
    parts = exchange(quads, "w")
    residual, copies = norm(place, parts, gain, ndp, steps)
    copies, *weights = lax.optimization_barrier((copies, *weights))
    tokens = exchange(copies, dp)
    relaid = [
        row_major(w if i % 3 == 2 else w.swapaxes(1, 2)) for i, w in enumerate(weights)
    ]
    tokens, *relaid = lax.optimization_barrier((tokens, *relaid))
    tokens = tokens.reshape(ndp * nz * steps, -1)
    made = experts(first, tokens, relaid[:3], relaid[3:])
    back = exchange(made.reshape(ndp, nz * steps, width), dp)
    column_sum = jnp.sum(back.astype(F32), axis=0).astype(BF16)
    final = exchange(column_sum.reshape(nz, steps, width), zaxis)
    out = residual + jnp.sum(final.astype(F32), axis=0)
    return out.astype(BF16)[None]


def solution(mesh):
    shape = dict(mesh.shape)
    side = int(round(shape["dp"] ** 0.5))
    fine = Mesh(
        mesh.devices.reshape(side, shape["dp"] // side, shape["expert"] // 4, 2, 2),
        ("x", "y", "w", "v", "c"),
    )
    row = ("w", "v", "c", "x", "y")
    group = ("w", "v", "c")
    dp = ("x", "y")
    placed = (
        P(row, None, None),
        P(row, None, None),
        P(row, None, None),
        P(row, None, None),
        P(row, None, None),
        P(row, None, None),
        P(row),
        P(group, None),
        P(),
        P(group, None, None),
        P(group, None, None),
        P(group, None, dp),
        P(group, None, dp),
        P(group, dp, None),
    )
    return jax.shard_map(
        on_device,
        mesh=fine,
        in_specs=placed,
        out_specs=P(row, None, None),
        check_vma=False,
    )
```

```python
import jax
import jax.numpy as jnp
from jax import lax
from jax.experimental import pallas as pl
from jax.experimental.pallas import tpu as pltpu
from jax.experimental.layout import Layout, with_layout_constraint
from jax.sharding import Mesh
from jax.sharding import PartitionSpec as P

HQ = 64
KVH = 8
HD = 64
SWAP = [(0, 1), (1, 0)]
F32 = jnp.float32
BF16 = jnp.bfloat16


def params(mib):
    return pltpu.CompilerParams(vmem_limit_bytes=mib * 1024 * 1024)


def vmem():
    return pl.BlockSpec(memory_space=pltpu.VMEM)


def hbm():
    return pl.BlockSpec(memory_space=pltpu.HBM)


def stay(*values):
    return [pltpu.with_memory_space_constraint(v, pltpu.HBM) for v in values]


def smem():
    return pl.BlockSpec(memory_space=pltpu.SMEM)


def attend_kernel(
    len_ref, q_hbm, nk_hbm, nv_hbm, k_hbm, v_hbm, w_hbm, out_ref, w_ref,
    q_ref, nk_ref, nv_ref, k_ref, v_ref, rows_ref, flat_ref, sems,
):
    pairs = (
        (k_hbm, k_ref), (q_hbm, q_ref), (nk_hbm, nk_ref), (nv_hbm, nv_ref), (v_hbm, v_ref),
        (w_hbm, w_ref),
    )
    copies = [pltpu.make_async_copy(a, b, sems.at[i]) for i, (a, b) in enumerate(pairs)]
    for copy in copies:
        copy.start()
    steps = q_ref.shape[1]
    width = KVH * HD
    rows = HQ * steps
    per_group = rows // KVH
    copies[1].wait()
    q = q_ref[0].astype(F32) * 0.125
    for h in range(HQ):
        rows_ref[h * steps : (h + 1) * steps, :] = q[:, h * HD : (h + 1) * HD]
    q_rows = rows_ref[...]
    q_pair = jnp.concatenate([q_rows, q_rows], axis=1)
    q_wide = jnp.concatenate([q_pair] * (KVH // 2), axis=1)
    row_id = lax.broadcasted_iota(jnp.int32, (rows, width), 0)
    col_id = lax.broadcasted_iota(jnp.int32, (rows, width), 1)
    in_group = row_id // per_group == col_id // HD
    q_wide = jnp.where(in_group, q_wide, 0.0)
    q_bf = q_wide.astype(BF16)
    copies[0].wait()
    scores = lax.dot_general(
        q_bf, k_ref[0], (((1,), (1,)), ((), ())), preferred_element_type=F32
    )
    slot = lax.broadcasted_iota(jnp.int32, scores.shape, 1)
    weights = jnp.where(slot < len_ref[0], jnp.exp(scores), 0.0)
    total = jnp.sum(weights, axis=1, keepdims=True)
    copies[2].wait()
    copies[3].wait()
    nk = nk_ref[0].astype(F32)
    nv = nv_ref[0].astype(F32)
    step_id = lax.broadcasted_iota(jnp.int32, (rows, 1), 0) % steps
    fresh = []
    for s in range(steps):
        score = jnp.sum(q_wide * nk[s : s + 1, :], axis=1, keepdims=True)
        weight = jnp.where(step_id >= s, jnp.exp(score), 0.0)
        total = total + weight
        fresh.append(weight)
    probs = (weights / total).astype(BF16)
    copies[4].wait()
    mixed = jnp.dot(probs, v_ref[0], preferred_element_type=F32)
    for s in range(steps):
        mixed = mixed + (fresh[s] / total).astype(BF16).astype(F32) * nv[s : s + 1, :]
    mixed = jnp.where(in_group, mixed, 0.0)
    folded = mixed[:, :128]
    for i in range(1, width // 128):
        folded = folded + mixed[:, i * 128 : (i + 1) * 128]
    rows_ref[...] = folded[:, :HD] + folded[:, HD:]
    for h in range(HQ):
        flat_ref[:, h * HD : (h + 1) * HD] = rows_ref[h * steps : (h + 1) * steps, :]
    blocks = out_ref.shape[0]
    wide = HQ * HD // blocks
    for b in range(blocks):
        out_ref[b] = flat_ref[:, b * wide : (b + 1) * wide].astype(BF16)
    copies[5].wait()


def attend(length, q, nk, nv, k, v, w, blocks):
    steps = q.shape[1]
    return pl.pallas_call(
        attend_kernel,
        in_specs=[smem()] + [hbm()] * 6,
        out_specs=[vmem(), vmem()],
        out_shape=[
            jax.ShapeDtypeStruct((blocks, steps, HQ * HD // blocks), BF16),
            jax.ShapeDtypeStruct(w.shape, BF16),
        ],
        scratch_shapes=[pltpu.VMEM(a.shape, BF16) for a in (q, nk, nv, k, v)]
        + [
            pltpu.VMEM((HQ * steps, HD), F32),
            pltpu.VMEM((steps, HQ * HD), F32),
            pltpu.SemaphoreType.DMA((6,)),
        ],
        compiler_params=params(12),
        name="attend",
    )(length, *stay(q, nk, nv, k, v, w))


def project_kernel(
    place_ref, x_ref, own_ref, other_ref, hid_hbm, ids_hbm, logits_hbm, keep_ref, send_ref,
    rows_ref, hid_ref, ids_ref, logits_ref, sems,
):
    width, feats = own_ref.shape
    chunk = 640
    cuts = [(start, min(start + chunk, width)) for start in range(0, width, chunk)]
    small = [
        pltpu.make_async_copy(hid_hbm, hid_ref, sems.at[0]),
        pltpu.make_async_copy(ids_hbm, ids_ref, sems.at[1]),
        pltpu.make_async_copy(logits_hbm, logits_ref, sems.at[2]),
    ]
    for copy in small:
        copy.start()
    blocks, steps, _ = x_ref.shape
    for i in range(blocks):
        rows_ref[i * steps : (i + 1) * steps, :] = x_ref[i].astype(F32)
    x = rows_ref[...].astype(BF16)
    low, high = x[:, :feats], x[:, feats:]
    first = place_ref[1] == 0
    mine = jnp.where(first, low, high)
    theirs = jnp.where(first, high, low)
    for copy in small:
        copy.wait()
    spare = keep_ref.shape[1] - width
    lane = lax.broadcasted_iota(jnp.int32, (1, spare), 1)
    routes = []
    for ref in (ids_ref, logits_ref):
        held = ref[...].astype(F32)
        row = lax.broadcasted_iota(jnp.int32, held.shape, 2)
        routes.append(
            jnp.sum(jnp.where(row == place_ref[2], held, 0.0), axis=2, keepdims=True)
        )
    top = routes[0].shape[1]
    lines = []
    for s in range(steps):
        line = jnp.zeros((1, spare), F32)
        for i, values in enumerate(routes):
            for k in range(top):
                line = jnp.where(lane == i * top + k, values[s, k : k + 1, :], line)
        lines.append(line)
    route = jnp.concatenate(lines, axis=0)
    extra = jnp.concatenate([hid_ref[0].astype(F32), route], axis=1)
    extra = jnp.concatenate([extra] * blocks, axis=0)
    block = lax.broadcasted_iota(jnp.int32, extra.shape, 0) // steps
    extra = jnp.where(block == place_ref[0], extra, 0.0)
    dims = (((1,), (1,)), ((), ()))
    for start, stop in cuts:
        part = lax.dot_general(mine, own_ref[start:stop], dims, preferred_element_type=F32)
        part = part + lax.dot_general(
            theirs, other_ref[start:stop], dims, preferred_element_type=F32
        )
        part = part + extra[:, start:stop]
        keep_ref[:, start:stop] = part
        send_ref[:, start:stop] = part.astype(BF16)
    keep_ref[:, width:] = extra[:, width:]
    send_ref[:, width:] = extra[:, width:].astype(BF16)


def project(place, x, hidden, ids, logits, own, other):
    blocks, steps, feats = x.shape
    wide = own.shape[0] + -own.shape[0] % 128
    rows = blocks * steps
    return pl.pallas_call(
        project_kernel,
        in_specs=[smem(), vmem(), vmem(), vmem()] + [hbm()] * 3,
        out_specs=[vmem(), vmem()],
        out_shape=[
            jax.ShapeDtypeStruct((rows, wide), F32),
            jax.ShapeDtypeStruct((rows, wide), BF16),
        ],
        scratch_shapes=[
            pltpu.VMEM((rows, feats), F32),
            pltpu.VMEM(hidden.shape, BF16),
            pltpu.VMEM(ids.shape, jnp.int32),
            pltpu.VMEM(logits.shape, BF16),
            pltpu.SemaphoreType.DMA((3,)),
        ],
        compiler_params=params(12),
        name="project",
    )(place, x, own, other, *stay(hidden, ids, logits))


def pair_kernel(keep_ref, got_ref, out_ref):
    total = (keep_ref[...] + got_ref[...].astype(F32)).astype(BF16)
    for i in range(out_ref.shape[0]):
        out_ref[i] = total


def pair(keep, got, copies):
    return pl.pallas_call(
        pair_kernel,
        in_specs=[vmem(), vmem()],
        out_specs=vmem(),
        out_shape=jax.ShapeDtypeStruct((copies,) + keep.shape, BF16),
        compiler_params=params(12),
        name="pair",
    )(keep, got)


def norm_kernel(place_ref, part_ref, gain_ref, res_ref, out_hbm, full_ref, sems):
    steps, width = res_ref.shape
    total = part_ref[0].astype(F32)
    for i in range(1, part_ref.shape[0]):
        total = total + part_ref[i].astype(F32)
    res = total[:, :width]
    scale = lax.rsqrt(jnp.sum(res * res, axis=1, keepdims=True) / width + 1e-05)
    normed = (res * scale * gain_ref[...]).astype(BF16)
    full_ref[...] = jnp.concatenate([normed.astype(F32), total[:, width:]], axis=1).astype(BF16)
    copies = [
        pltpu.make_async_copy(full_ref, out_hbm.at[i], sems.at[i])
        for i in range(out_hbm.shape[0])
    ]
    for copy in copies:
        copy.start()
    own = jnp.zeros((steps, width), F32)
    for i in range(res.shape[0] // steps):
        own = own + jnp.where(place_ref[0] == i, res[i * steps : (i + 1) * steps, :], 0.0)
    res_ref[...] = own
    for copy in copies:
        copy.wait()


def norm(place, parts, gain, copies, steps):
    _, rows, wide = parts.shape
    width = gain.shape[1]
    return pl.pallas_call(
        norm_kernel,
        in_specs=[smem(), vmem(), vmem()],
        out_specs=[vmem(), hbm()],
        out_shape=[
            jax.ShapeDtypeStruct((steps, width), F32),
            jax.ShapeDtypeStruct((copies, rows, wide), BF16),
        ],
        scratch_shapes=[pltpu.VMEM((rows, wide), BF16), pltpu.SemaphoreType.DMA((copies,))],
        compiler_params=params(12),
        name="norm",
    )(place, parts, gain)


def experts_kernel(
    first_ref, x_ref, g0_hbm, u0_hbm, g1_hbm, u1_hbm, d0_hbm, d1_hbm, out_ref,
    g0, u0, g1, u1, d0, d1, sems,
):
    pairs = (
        (g0_hbm, g0), (u0_hbm, u0), (g1_hbm, g1), (u1_hbm, u1), (d0_hbm, d0), (d1_hbm, d1),
    )
    per, _, width = g0.shape
    copies = [pltpu.make_async_copy(a, b, sems.at[i]) for i, (a, b) in enumerate(pairs)]
    for copy in copies:
        copy.start()
    x = x_ref[:, :width]
    route = x_ref[:, width : width + 8].astype(F32)
    ids = route[:, 0:4]
    expo = jnp.exp(route[:, 4:8])
    total = jnp.sum(expo, axis=1, keepdims=True)
    dims = (((1,), (1,)), ((), ()))
    acts = []
    for side, (g_ref, u_ref) in enumerate(((g0, u0), (g1, u1))):
        copies[2 * side].wait()
        gates = [
            lax.dot_general(x, g_ref[e], dims, preferred_element_type=F32) for e in range(per)
        ]
        copies[2 * side + 1].wait()
        for e in range(per):
            gate = gates[e]
            up = lax.dot_general(x, u_ref[e], dims, preferred_element_type=F32)
            act = gate * jax.nn.sigmoid(1.702 * gate) * (up + 1.0)
            label = (first_ref[side] + e).astype(F32)
            share = jnp.sum(jnp.where(ids == label, expo, 0.0), axis=1, keepdims=True) / total
            acts.append((act * share).astype(BF16))
    copies[4].wait()
    copies[5].wait()
    chunk = 768
    for start in range(0, width, chunk):
        stop = min(start + chunk, width)
        part = None
        for side, d_ref in enumerate((d0, d1)):
            for e in range(per):
                piece = jnp.dot(
                    acts[side * per + e], d_ref[e, :, start:stop], preferred_element_type=F32
                )
                part = piece if part is None else part + piece
        out_ref[:, start:stop] = part.astype(BF16)


def experts(first, x, own, other):
    width = own[0].shape[2]
    args = (own[0], own[1], other[0], other[1], own[2], other[2])
    return pl.pallas_call(
        experts_kernel,
        in_specs=[smem(), vmem()] + [hbm()] * 6,
        out_specs=vmem(),
        out_shape=jax.ShapeDtypeStruct((x.shape[0], width), BF16),
        scratch_shapes=[pltpu.VMEM(a.shape, BF16) for a in args]
        + [pltpu.SemaphoreType.DMA((len(args),))],
        compiler_params=params(32),
        name="experts",
    )(first, x, *stay(*args))


def row_major(value):
    return with_layout_constraint(value, Layout(major_to_minor=tuple(range(value.ndim))))


def exchange(value, axis):
    return lax.all_to_all(value, axis, split_axis=0, concat_axis=0, tiled=True)


def on_device(
    hidden_in,
    queries,
    new_keys,
    new_values,
    key_cache,
    value_cache,
    prompt_lengths,
    out_weight,
    norm_gain,
    expert_ids,
    top_logits,
    gate_weight,
    up_weight,
    down_weight,
):
    steps, width = hidden_in.shape[1:]
    zaxis = ("w", "v")
    dp = ("x", "y")
    nz = lax.axis_size(zaxis)
    ndp = lax.axis_size(dp)
    z = lax.axis_index(zaxis)
    c = lax.axis_index("c")
    d = lax.axis_index(dp)
    per = gate_weight.shape[0]
    out_rows = out_weight.T
    other_out = lax.ppermute(out_rows, "c", SWAP)
    far_down, far_gate, far_up = (
        lax.ppermute(w, "c", SWAP) for w in (down_weight, gate_weight, up_weight)
    )
    attended, own_out = attend(
        prompt_lengths, queries, new_keys, new_values, key_cache, value_cache, out_rows, nz
    )
    place = jnp.stack([z, c, d]).astype(jnp.int32)
    first = jnp.stack([(2 * z + c) * per, (2 * z + 1 - c) * per]).astype(jnp.int32)
    attended, place, first = lax.optimization_barrier((attended, place, first))
    by_heads = exchange(attended, zaxis)
    ids, logits = expert_ids.transpose(1, 2, 0), top_logits.transpose(1, 2, 0)
    keep, sent = project(place, by_heads, hidden_in, ids, logits, own_out, other_out)
    sent, gain, down, far_down = lax.optimization_barrier(
        (sent, norm_gain, down_weight, far_down)
    )
    got = lax.ppermute(sent, "v", SWAP)
    got, gain, down, far_down = lax.optimization_barrier(
        (got, gain[None], row_major(down), row_major(far_down))
    )
    quads = pair(keep, got, nz // 2)
    parts = exchange(quads, "w")
    residual, copies = norm(place, parts, gain, ndp, steps)
    copies, *weights = lax.optimization_barrier(
        (copies, gate_weight, up_weight, far_gate, far_up)
    )
    tokens = exchange(copies, dp)
    relaid = [row_major(w.swapaxes(1, 2)) for w in weights]
    tokens, gate, up, far_gate, far_up = lax.optimization_barrier((tokens, *relaid))
    tokens = tokens.reshape(ndp * nz * steps, -1)
    made = experts(first, tokens, (gate, up, down), (far_gate, far_up, far_down))
    back = exchange(made.reshape(ndp, nz * steps, width), dp)
    column_sum = jnp.sum(back.astype(F32), axis=0).astype(BF16)
    final = exchange(column_sum.reshape(nz, steps, width), zaxis)
    out = residual + jnp.sum(final.astype(F32), axis=0)
    return out.astype(BF16)[None]


def solution(mesh):
    shape = dict(mesh.shape)
    side = int(round(shape["dp"] ** 0.5))
    fine = Mesh(
        mesh.devices.reshape(side, shape["dp"] // side, shape["expert"] // 4, 2, 2),
        ("x", "y", "w", "v", "c"),
    )
    row = ("w", "v", "c", "x", "y")
    group = ("w", "v", "c")
    dp = ("x", "y")
    placed = (
        P(row, None, None),
        P(row, None, None),
        P(row, None, None),
        P(row, None, None),
        P(row, None, None),
        P(row, None, None),
        P(row),
        P(group, None),
        P(),
        P(group, None, None),
        P(group, None, None),
        P(group, None, dp),
        P(group, None, dp),
        P(group, dp, None),
    )
    return jax.shard_map(
        on_device,
        mesh=fine,
        in_specs=placed,
        out_specs=P(row, None, None),
        check_vma=False,
    )
```

```python
import jax
import jax.numpy as jnp
from jax import lax
from jax.experimental import pallas as pl
from jax.experimental.pallas import tpu as pltpu
from jax.experimental.layout import Layout, with_layout_constraint
from jax.sharding import Mesh
from jax.sharding import PartitionSpec as P

HQ = 64
KVH = 8
HD = 64
SWAP = [(0, 1), (1, 0)]
F32 = jnp.float32
BF16 = jnp.bfloat16


def params(mib):
    return pltpu.CompilerParams(vmem_limit_bytes=mib * 1024 * 1024)


def vmem():
    return pl.BlockSpec(memory_space=pltpu.VMEM)


def hbm():
    return pl.BlockSpec(memory_space=pltpu.HBM)


def stay(*values):
    return [pltpu.with_memory_space_constraint(v, pltpu.HBM) for v in values]


def smem():
    return pl.BlockSpec(memory_space=pltpu.SMEM)


def attend_kernel(
    len_ref, q_hbm, nk_hbm, nv_hbm, k_hbm, v_hbm, w_hbm, out_ref, w_ref,
    q_ref, nk_ref, nv_ref, k_ref, v_ref, rows_ref, flat_ref, sems,
):
    pairs = (
        (k_hbm, k_ref), (q_hbm, q_ref), (nk_hbm, nk_ref), (nv_hbm, nv_ref), (v_hbm, v_ref),
        (w_hbm, w_ref),
    )
    copies = [pltpu.make_async_copy(a, b, sems.at[i]) for i, (a, b) in enumerate(pairs)]
    for copy in copies:
        copy.start()
    steps = q_ref.shape[1]
    width = KVH * HD
    rows = HQ * steps
    per_group = rows // KVH
    copies[1].wait()
    q = q_ref[0].astype(F32) * 0.125
    for h in range(HQ):
        rows_ref[h * steps : (h + 1) * steps, :] = q[:, h * HD : (h + 1) * HD]
    q_rows = rows_ref[...]
    q_pair = jnp.concatenate([q_rows, q_rows], axis=1)
    q_wide = jnp.concatenate([q_pair] * (KVH // 2), axis=1)
    row_id = lax.broadcasted_iota(jnp.int32, (rows, width), 0)
    col_id = lax.broadcasted_iota(jnp.int32, (rows, width), 1)
    in_group = row_id // per_group == col_id // HD
    q_wide = jnp.where(in_group, q_wide, 0.0)
    q_bf = q_wide.astype(BF16)
    copies[0].wait()
    scores = lax.dot_general(
        q_bf, k_ref[0], (((1,), (1,)), ((), ())), preferred_element_type=F32
    )
    slot = lax.broadcasted_iota(jnp.int32, scores.shape, 1)
    weights = jnp.where(slot < len_ref[0], jnp.exp(scores), 0.0)
    total = jnp.sum(weights, axis=1, keepdims=True)
    copies[2].wait()
    copies[3].wait()
    nk = nk_ref[0].astype(F32)
    nv = nv_ref[0].astype(F32)
    step_id = lax.broadcasted_iota(jnp.int32, (rows, 1), 0) % steps
    fresh = []
    for s in range(steps):
        score = jnp.sum(q_wide * nk[s : s + 1, :], axis=1, keepdims=True)
        weight = jnp.where(step_id >= s, jnp.exp(score), 0.0)
        total = total + weight
        fresh.append(weight)
    probs = (weights / total).astype(BF16)
    copies[4].wait()
    mixed = jnp.dot(probs, v_ref[0], preferred_element_type=F32)
    for s in range(steps):
        mixed = mixed + (fresh[s] / total).astype(BF16).astype(F32) * nv[s : s + 1, :]
    mixed = jnp.where(in_group, mixed, 0.0)
    folded = mixed[:, :128]
    for i in range(1, width // 128):
        folded = folded + mixed[:, i * 128 : (i + 1) * 128]
    rows_ref[...] = folded[:, :HD] + folded[:, HD:]
    for h in range(HQ):
        flat_ref[:, h * HD : (h + 1) * HD] = rows_ref[h * steps : (h + 1) * steps, :]
    blocks = out_ref.shape[0]
    wide = HQ * HD // blocks
    for b in range(blocks):
        out_ref[b] = flat_ref[:, b * wide : (b + 1) * wide].astype(BF16)
    copies[5].wait()


def attend(length, q, nk, nv, k, v, w, blocks):
    steps = q.shape[1]
    return pl.pallas_call(
        attend_kernel,
        in_specs=[smem()] + [hbm()] * 6,
        out_specs=[vmem(), vmem()],
        out_shape=[
            jax.ShapeDtypeStruct((blocks, steps, HQ * HD // blocks), BF16),
            jax.ShapeDtypeStruct(w.shape, BF16),
        ],
        scratch_shapes=[pltpu.VMEM(a.shape, BF16) for a in (q, nk, nv, k, v)]
        + [
            pltpu.VMEM((HQ * steps, HD), F32),
            pltpu.VMEM((steps, HQ * HD), F32),
            pltpu.SemaphoreType.DMA((6,)),
        ],
        compiler_params=params(12),
        name="attend",
    )(length, *stay(q, nk, nv, k, v, w))


def project_kernel(
    place_ref, x_ref, own_ref, other_ref, hid_hbm, ids_hbm, logits_hbm, out_hbm,
    send_ref, rows_ref, hid_ref, ids_ref, logits_ref, sems,
):
    width, feats = own_ref.shape
    chunk = 640
    cuts = [(start, min(start + chunk, width)) for start in range(0, width, chunk)]
    small = [
        pltpu.make_async_copy(hid_hbm, hid_ref, sems.at[0]),
        pltpu.make_async_copy(ids_hbm, ids_ref, sems.at[1]),
        pltpu.make_async_copy(logits_hbm, logits_ref, sems.at[2]),
    ]
    for copy in small:
        copy.start()
    blocks, steps, _ = x_ref.shape
    for i in range(blocks):
        rows_ref[i * steps : (i + 1) * steps, :] = x_ref[i].astype(F32)
    x = rows_ref[...].astype(BF16)
    low, high = x[:, :feats], x[:, feats:]
    first = place_ref[1] == 0
    mine = jnp.where(first, low, high)
    theirs = jnp.where(first, high, low)
    for copy in small:
        copy.wait()
    spare = send_ref.shape[1] - width
    lane = lax.broadcasted_iota(jnp.int32, (1, spare), 1)
    routes = []
    for ref in (ids_ref, logits_ref):
        held = ref[...].astype(F32)
        row = lax.broadcasted_iota(jnp.int32, held.shape, 2)
        routes.append(
            jnp.sum(jnp.where(row == place_ref[2], held, 0.0), axis=2, keepdims=True)
        )
    top = routes[0].shape[1]
    lines = []
    for s in range(steps):
        line = jnp.zeros((1, spare), F32)
        for i, values in enumerate(routes):
            for k in range(top):
                line = jnp.where(lane == i * top + k, values[s, k : k + 1, :], line)
        lines.append(line)
    route = jnp.concatenate(lines, axis=0)
    extra = jnp.concatenate([hid_ref[0].astype(F32), route], axis=1)
    extra = jnp.concatenate([extra] * blocks, axis=0)
    block = lax.broadcasted_iota(jnp.int32, extra.shape, 0) // steps
    extra = jnp.where(block == place_ref[0], extra, 0.0)
    dims = (((1,), (1,)), ((), ()))
    for start, stop in cuts:
        part = lax.dot_general(mine, own_ref[start:stop], dims, preferred_element_type=F32)
        part = part + lax.dot_general(
            theirs, other_ref[start:stop], dims, preferred_element_type=F32
        )
        send_ref[:, start:stop] = (part + extra[:, start:stop]).astype(BF16)
    send_ref[:, width:] = extra[:, width:].astype(BF16)
    out = [
        pltpu.make_async_copy(send_ref, out_hbm.at[i], sems.at[3 + i]) for i in range(blocks)
    ]
    for copy in out:
        copy.start()
    for copy in out:
        copy.wait()


def project(place, x, hidden, ids, logits, own, other):
    blocks, steps, feats = x.shape
    wide = own.shape[0] + -own.shape[0] % 128
    rows = blocks * steps
    return pl.pallas_call(
        project_kernel,
        in_specs=[smem(), vmem(), vmem(), vmem()] + [hbm()] * 3,
        out_specs=hbm(),
        out_shape=jax.ShapeDtypeStruct((blocks, rows, wide), BF16),
        scratch_shapes=[
            pltpu.VMEM((rows, wide), BF16),
            pltpu.VMEM((rows, feats), F32),
            pltpu.VMEM(hidden.shape, BF16),
            pltpu.VMEM(ids.shape, jnp.int32),
            pltpu.VMEM(logits.shape, BF16),
            pltpu.SemaphoreType.DMA((3 + blocks,)),
        ],
        compiler_params=params(12),
        name="project",
    )(place, x, own, other, *stay(hidden, ids, logits))


def norm_kernel(place_ref, part_ref, gain_ref, res_ref, out_hbm, full_ref, sems):
    steps, width = res_ref.shape
    total = part_ref[0].astype(F32)
    for i in range(1, part_ref.shape[0]):
        total = total + part_ref[i].astype(F32)
    res = total[:, :width]
    scale = lax.rsqrt(jnp.sum(res * res, axis=1, keepdims=True) / width + 1e-05)
    normed = (res * scale * gain_ref[...]).astype(BF16)
    full_ref[...] = jnp.concatenate([normed.astype(F32), total[:, width:]], axis=1).astype(BF16)
    copies = [
        pltpu.make_async_copy(full_ref, out_hbm.at[i], sems.at[i])
        for i in range(out_hbm.shape[0])
    ]
    for copy in copies:
        copy.start()
    own = jnp.zeros((steps, width), F32)
    for i in range(res.shape[0] // steps):
        own = own + jnp.where(place_ref[0] == i, res[i * steps : (i + 1) * steps, :], 0.0)
    res_ref[...] = own
    for copy in copies:
        copy.wait()


def norm(place, parts, gain, copies, steps):
    _, rows, wide = parts.shape
    width = gain.shape[1]
    return pl.pallas_call(
        norm_kernel,
        in_specs=[smem(), vmem(), vmem()],
        out_specs=[vmem(), hbm()],
        out_shape=[
            jax.ShapeDtypeStruct((steps, width), F32),
            jax.ShapeDtypeStruct((copies, rows, wide), BF16),
        ],
        scratch_shapes=[pltpu.VMEM((rows, wide), BF16), pltpu.SemaphoreType.DMA((copies,))],
        compiler_params=params(12),
        name="norm",
    )(place, parts, gain)


def experts_kernel(
    first_ref, x_ref, g0_hbm, u0_hbm, g1_hbm, u1_hbm, d0_hbm, d1_hbm, out_ref,
    g0, u0, g1, u1, d0, d1, sems,
):
    pairs = (
        (g0_hbm, g0), (u0_hbm, u0), (g1_hbm, g1), (u1_hbm, u1), (d0_hbm, d0), (d1_hbm, d1),
    )
    per, _, width = g0.shape
    copies = [pltpu.make_async_copy(a, b, sems.at[i]) for i, (a, b) in enumerate(pairs)]
    for copy in copies:
        copy.start()
    x = x_ref[:, :width]
    route = x_ref[:, width : width + 8].astype(F32)
    ids = route[:, 0:4]
    expo = jnp.exp(route[:, 4:8])
    total = jnp.sum(expo, axis=1, keepdims=True)
    dims = (((1,), (1,)), ((), ()))
    acts = []
    for side, (g_ref, u_ref) in enumerate(((g0, u0), (g1, u1))):
        copies[2 * side].wait()
        gates = [
            lax.dot_general(x, g_ref[e], dims, preferred_element_type=F32) for e in range(per)
        ]
        copies[2 * side + 1].wait()
        for e in range(per):
            gate = gates[e]
            up = lax.dot_general(x, u_ref[e], dims, preferred_element_type=F32)
            act = gate * jax.nn.sigmoid(1.702 * gate) * (up + 1.0)
            label = (first_ref[side] + e).astype(F32)
            share = jnp.sum(jnp.where(ids == label, expo, 0.0), axis=1, keepdims=True) / total
            acts.append((act * share).astype(BF16))
    copies[4].wait()
    copies[5].wait()
    chunk = 768
    for start in range(0, width, chunk):
        stop = min(start + chunk, width)
        part = None
        for side, d_ref in enumerate((d0, d1)):
            for e in range(per):
                piece = jnp.dot(
                    acts[side * per + e], d_ref[e, :, start:stop], preferred_element_type=F32
                )
                part = piece if part is None else part + piece
        out_ref[:, start:stop] = part.astype(BF16)


def experts(first, x, own, other):
    width = own[0].shape[2]
    args = (own[0], own[1], other[0], other[1], own[2], other[2])
    return pl.pallas_call(
        experts_kernel,
        in_specs=[smem(), vmem()] + [hbm()] * 6,
        out_specs=vmem(),
        out_shape=jax.ShapeDtypeStruct((x.shape[0], width), BF16),
        scratch_shapes=[pltpu.VMEM(a.shape, BF16) for a in args]
        + [pltpu.SemaphoreType.DMA((len(args),))],
        compiler_params=params(32),
        name="experts",
    )(first, x, *stay(*args))


def row_major(value):
    return with_layout_constraint(value, Layout(major_to_minor=tuple(range(value.ndim))))


def exchange(value, axis):
    return lax.all_to_all(value, axis, split_axis=0, concat_axis=0, tiled=True)


def on_device(
    hidden_in,
    queries,
    new_keys,
    new_values,
    key_cache,
    value_cache,
    prompt_lengths,
    out_weight,
    norm_gain,
    expert_ids,
    top_logits,
    gate_weight,
    up_weight,
    down_weight,
):
    steps, width = hidden_in.shape[1:]
    zaxis = ("w", "v")
    dp = ("x", "y")
    nz = lax.axis_size(zaxis)
    ndp = lax.axis_size(dp)
    z = lax.axis_index(zaxis)
    c = lax.axis_index("c")
    d = lax.axis_index(dp)
    per = gate_weight.shape[0]
    out_rows = out_weight.T
    other_out = lax.ppermute(out_rows, "c", SWAP)
    far_down = lax.ppermute(down_weight, "c", SWAP)
    attended, own_out = attend(
        prompt_lengths, queries, new_keys, new_values, key_cache, value_cache, out_rows, nz
    )
    place = jnp.stack([z, c, d]).astype(jnp.int32)
    first = jnp.stack([(2 * z + c) * per, (2 * z + 1 - c) * per]).astype(jnp.int32)
    attended, place, first = lax.optimization_barrier((attended, place, first))
    by_heads = exchange(attended, zaxis)
    ids, logits = expert_ids.transpose(1, 2, 0), top_logits.transpose(1, 2, 0)
    sent = project(place, by_heads, hidden_in, ids, logits, own_out, other_out)
    sent, gain, gate, up, down, far_down = lax.optimization_barrier(
        (sent, norm_gain, gate_weight, up_weight, down_weight, far_down)
    )
    far_gate, far_up = lax.ppermute(gate, "c", SWAP), lax.ppermute(up, "c", SWAP)
    parts = exchange(sent, zaxis)
    parts, gain, down, far_down = lax.optimization_barrier(
        (parts, gain[None], row_major(down), row_major(far_down))
    )
    residual, copies = norm(place, parts, gain, ndp, steps)
    copies, *weights = lax.optimization_barrier(
        (copies, gate, up, far_gate, far_up)
    )
    tokens = exchange(copies, dp)
    relaid = [row_major(w.swapaxes(1, 2)) for w in weights]
    tokens, gate, up, far_gate, far_up = lax.optimization_barrier((tokens, *relaid))
    tokens = tokens.reshape(ndp * nz * steps, -1)
    made = experts(first, tokens, (gate, up, down), (far_gate, far_up, far_down))
    back = exchange(made.reshape(ndp, nz * steps, width), dp)
    column_sum = jnp.sum(back.astype(F32), axis=0).astype(BF16)
    final = exchange(column_sum.reshape(nz, steps, width), zaxis)
    out = residual + jnp.sum(final.astype(F32), axis=0)
    return out.astype(BF16)[None]


def solution(mesh):
    shape = dict(mesh.shape)
    side = int(round(shape["dp"] ** 0.5))
    fine = Mesh(
        mesh.devices.reshape(side, shape["dp"] // side, shape["expert"] // 4, 2, 2),
        ("x", "y", "w", "v", "c"),
    )
    row = ("w", "v", "c", "x", "y")
    group = ("w", "v", "c")
    dp = ("x", "y")
    placed = (
        P(row, None, None),
        P(row, None, None),
        P(row, None, None),
        P(row, None, None),
        P(row, None, None),
        P(row, None, None),
        P(row),
        P(group, None),
        P(),
        P(group, None, None),
        P(group, None, None),
        P(group, None, dp),
        P(group, None, dp),
        P(group, dp, None),
    )
    return jax.shard_map(
        on_device,
        mesh=fine,
        in_specs=placed,
        out_specs=P(row, None, None),
        check_vma=False,
    )
```

```python
import jax
import jax.numpy as jnp
from jax import lax
from jax.experimental import pallas as pl
from jax.experimental.pallas import tpu as pltpu
from jax.experimental.layout import Layout, with_layout_constraint
from jax.sharding import Mesh
from jax.sharding import PartitionSpec as P

HQ = 64
KVH = 8
HD = 64
SWAP = [(0, 1), (1, 0)]
F32 = jnp.float32
BF16 = jnp.bfloat16


def params(mib):
    return pltpu.CompilerParams(vmem_limit_bytes=mib * 1024 * 1024)


def vmem():
    return pl.BlockSpec(memory_space=pltpu.VMEM)


def hbm():
    return pl.BlockSpec(memory_space=pltpu.HBM)


def stay(*values):
    return [pltpu.with_memory_space_constraint(v, pltpu.HBM) for v in values]


def smem():
    return pl.BlockSpec(memory_space=pltpu.SMEM)


def attend_kernel(
    len_ref, q_hbm, nk_hbm, nv_hbm, k_hbm, v_hbm, w_hbm, out_ref, w_ref,
    q_ref, nk_ref, nv_ref, k_ref, v_ref, rows_ref, flat_ref, sems,
):
    pairs = (
        (k_hbm, k_ref), (q_hbm, q_ref), (nk_hbm, nk_ref), (nv_hbm, nv_ref), (v_hbm, v_ref),
        (w_hbm, w_ref),
    )
    copies = [pltpu.make_async_copy(a, b, sems.at[i]) for i, (a, b) in enumerate(pairs)]
    for copy in copies:
        copy.start()
    steps = q_ref.shape[1]
    width = KVH * HD
    rows = HQ * steps
    per_group = rows // KVH
    copies[1].wait()
    q = q_ref[0].astype(F32) * 0.125
    for h in range(HQ):
        rows_ref[h * steps : (h + 1) * steps, :] = q[:, h * HD : (h + 1) * HD]
    q_rows = rows_ref[...]
    q_pair = jnp.concatenate([q_rows, q_rows], axis=1)
    q_wide = jnp.concatenate([q_pair] * (KVH // 2), axis=1)
    row_id = lax.broadcasted_iota(jnp.int32, (rows, width), 0)
    col_id = lax.broadcasted_iota(jnp.int32, (rows, width), 1)
    in_group = row_id // per_group == col_id // HD
    q_wide = jnp.where(in_group, q_wide, 0.0)
    q_bf = q_wide.astype(BF16)
    copies[0].wait()
    scores = lax.dot_general(
        q_bf, k_ref[0], (((1,), (1,)), ((), ())), preferred_element_type=F32
    )
    slot = lax.broadcasted_iota(jnp.int32, scores.shape, 1)
    weights = jnp.where(slot < len_ref[0], jnp.exp(scores), 0.0)
    total = jnp.sum(weights, axis=1, keepdims=True)
    copies[2].wait()
    copies[3].wait()
    nk = nk_ref[0].astype(F32)
    nv = nv_ref[0].astype(F32)
    step_id = lax.broadcasted_iota(jnp.int32, (rows, 1), 0) % steps
    fresh = []
    for s in range(steps):
        score = jnp.sum(q_wide * nk[s : s + 1, :], axis=1, keepdims=True)
        weight = jnp.where(step_id >= s, jnp.exp(score), 0.0)
        total = total + weight
        fresh.append(weight)
    probs = (weights / total).astype(BF16)
    copies[4].wait()
    mixed = jnp.dot(probs, v_ref[0], preferred_element_type=F32)
    for s in range(steps):
        mixed = mixed + (fresh[s] / total).astype(BF16).astype(F32) * nv[s : s + 1, :]
    mixed = jnp.where(in_group, mixed, 0.0)
    folded = mixed[:, :128]
    for i in range(1, width // 128):
        folded = folded + mixed[:, i * 128 : (i + 1) * 128]
    rows_ref[...] = folded[:, :HD] + folded[:, HD:]
    for h in range(HQ):
        flat_ref[:, h * HD : (h + 1) * HD] = rows_ref[h * steps : (h + 1) * steps, :]
    blocks = out_ref.shape[0]
    wide = HQ * HD // blocks
    for b in range(blocks):
        out_ref[b] = flat_ref[:, b * wide : (b + 1) * wide].astype(BF16)
    copies[5].wait()


def attend(length, q, nk, nv, k, v, w, blocks):
    steps = q.shape[1]
    return pl.pallas_call(
        attend_kernel,
        in_specs=[smem()] + [hbm()] * 6,
        out_specs=[vmem(), vmem()],
        out_shape=[
            jax.ShapeDtypeStruct((blocks, steps, HQ * HD // blocks), BF16),
            jax.ShapeDtypeStruct(w.shape, BF16),
        ],
        scratch_shapes=[pltpu.VMEM(a.shape, BF16) for a in (q, nk, nv, k, v)]
        + [
            pltpu.VMEM((HQ * steps, HD), F32),
            pltpu.VMEM((steps, HQ * HD), F32),
            pltpu.SemaphoreType.DMA((6,)),
        ],
        compiler_params=params(12),
        name="attend",
    )(length, *stay(q, nk, nv, k, v, w))


def project_kernel(
    place_ref, x_ref, own_ref, other_ref, hid_hbm, ids_hbm, logits_hbm, keep_ref, send_ref,
    rows_ref, hid_ref, ids_ref, logits_ref, sems,
):
    width, feats = own_ref.shape
    chunk = 640
    cuts = [(start, min(start + chunk, width)) for start in range(0, width, chunk)]
    small = [
        pltpu.make_async_copy(hid_hbm, hid_ref, sems.at[0]),
        pltpu.make_async_copy(ids_hbm, ids_ref, sems.at[1]),
        pltpu.make_async_copy(logits_hbm, logits_ref, sems.at[2]),
    ]
    for copy in small:
        copy.start()
    blocks, steps, _ = x_ref.shape
    for i in range(blocks):
        rows_ref[i * steps : (i + 1) * steps, :] = x_ref[i].astype(F32)
    x = rows_ref[...].astype(BF16)
    low, high = x[:, :feats], x[:, feats:]
    first = place_ref[1] == 0
    mine = jnp.where(first, low, high)
    theirs = jnp.where(first, high, low)
    for copy in small:
        copy.wait()
    spare = keep_ref.shape[1] - width
    lane = lax.broadcasted_iota(jnp.int32, (1, spare), 1)
    routes = []
    for ref in (ids_ref, logits_ref):
        held = ref[...].astype(F32)
        row = lax.broadcasted_iota(jnp.int32, held.shape, 2)
        routes.append(
            jnp.sum(jnp.where(row == place_ref[2], held, 0.0), axis=2, keepdims=True)
        )
    top = routes[0].shape[1]
    lines = []
    for s in range(steps):
        line = jnp.zeros((1, spare), F32)
        for i, values in enumerate(routes):
            for k in range(top):
                line = jnp.where(lane == i * top + k, values[s, k : k + 1, :], line)
        lines.append(line)
    route = jnp.concatenate(lines, axis=0)
    extra = jnp.concatenate([hid_ref[0].astype(F32), route], axis=1)
    extra = jnp.concatenate([extra] * blocks, axis=0)
    block = lax.broadcasted_iota(jnp.int32, extra.shape, 0) // steps
    extra = jnp.where(block == place_ref[0], extra, 0.0)
    dims = (((1,), (1,)), ((), ()))
    for start, stop in cuts:
        part = lax.dot_general(mine, own_ref[start:stop], dims, preferred_element_type=F32)
        part = part + lax.dot_general(
            theirs, other_ref[start:stop], dims, preferred_element_type=F32
        )
        part = part + extra[:, start:stop]
        keep_ref[:, start:stop] = part
        send_ref[:, start:stop] = part.astype(BF16)
    keep_ref[:, width:] = extra[:, width:]
    send_ref[:, width:] = extra[:, width:].astype(BF16)


def project(place, x, hidden, ids, logits, own, other):
    blocks, steps, feats = x.shape
    wide = own.shape[0] + -own.shape[0] % 128
    rows = blocks * steps
    return pl.pallas_call(
        project_kernel,
        in_specs=[smem(), vmem(), vmem(), vmem()] + [hbm()] * 3,
        out_specs=[vmem(), vmem()],
        out_shape=[
            jax.ShapeDtypeStruct((rows, wide), F32),
            jax.ShapeDtypeStruct((rows, wide), BF16),
        ],
        scratch_shapes=[
            pltpu.VMEM((rows, feats), F32),
            pltpu.VMEM(hidden.shape, BF16),
            pltpu.VMEM(ids.shape, jnp.int32),
            pltpu.VMEM(logits.shape, BF16),
            pltpu.SemaphoreType.DMA((3,)),
        ],
        compiler_params=params(12),
        name="project",
    )(place, x, own, other, *stay(hidden, ids, logits))


def join_kernel(keep_ref, got_ref, next_ref, send_ref):
    total = keep_ref[...] + got_ref[...].astype(F32)
    next_ref[...] = total
    send_ref[...] = total.astype(BF16)


def join(keep, got):
    return pl.pallas_call(
        join_kernel,
        in_specs=[vmem(), vmem()],
        out_specs=[vmem(), vmem()],
        out_shape=[
            jax.ShapeDtypeStruct(keep.shape, F32),
            jax.ShapeDtypeStruct(keep.shape, BF16),
        ],
        compiler_params=params(12),
        name="join",
    )(keep, got)


def norm_kernel(place_ref, keep_ref, got_ref, gain_ref, res_ref, out_hbm, full_ref, sems):
    steps, width = res_ref.shape
    total = keep_ref[...] + got_ref[...].astype(F32)
    res = total[:, :width]
    scale = lax.rsqrt(jnp.sum(res * res, axis=1, keepdims=True) / width + 1e-05)
    normed = (res * scale * gain_ref[...]).astype(BF16)
    full_ref[...] = jnp.concatenate([normed.astype(F32), total[:, width:]], axis=1).astype(BF16)
    copies = [
        pltpu.make_async_copy(full_ref, out_hbm.at[i], sems.at[i])
        for i in range(out_hbm.shape[0])
    ]
    for copy in copies:
        copy.start()
    own = jnp.zeros((steps, width), F32)
    for i in range(res.shape[0] // steps):
        own = own + jnp.where(place_ref[0] == i, res[i * steps : (i + 1) * steps, :], 0.0)
    res_ref[...] = own
    for copy in copies:
        copy.wait()


def norm(place, keep, got, gain, copies, steps):
    rows, wide = keep.shape
    width = gain.shape[1]
    return pl.pallas_call(
        norm_kernel,
        in_specs=[smem(), vmem(), vmem(), vmem()],
        out_specs=[vmem(), hbm()],
        out_shape=[
            jax.ShapeDtypeStruct((steps, width), F32),
            jax.ShapeDtypeStruct((copies, rows, wide), BF16),
        ],
        scratch_shapes=[pltpu.VMEM((rows, wide), BF16), pltpu.SemaphoreType.DMA((copies,))],
        compiler_params=params(12),
        name="norm",
    )(place, keep, got, gain)


def experts_kernel(
    first_ref, x_ref, g0_hbm, u0_hbm, g1_hbm, u1_hbm, d0_hbm, d1_hbm, out_ref,
    g0, u0, g1, u1, d0, d1, sems,
):
    pairs = (
        (g0_hbm, g0), (u0_hbm, u0), (g1_hbm, g1), (u1_hbm, u1), (d0_hbm, d0), (d1_hbm, d1),
    )
    per, _, width = g0.shape
    copies = [pltpu.make_async_copy(a, b, sems.at[i]) for i, (a, b) in enumerate(pairs)]
    for copy in copies:
        copy.start()
    x = x_ref[:, :width]
    route = x_ref[:, width : width + 8].astype(F32)
    ids = route[:, 0:4]
    expo = jnp.exp(route[:, 4:8])
    total = jnp.sum(expo, axis=1, keepdims=True)
    dims = (((1,), (1,)), ((), ()))
    acts = []
    for side, (g_ref, u_ref) in enumerate(((g0, u0), (g1, u1))):
        copies[2 * side].wait()
        gates = [
            lax.dot_general(x, g_ref[e], dims, preferred_element_type=F32) for e in range(per)
        ]
        copies[2 * side + 1].wait()
        for e in range(per):
            gate = gates[e]
            up = lax.dot_general(x, u_ref[e], dims, preferred_element_type=F32)
            act = gate * jax.nn.sigmoid(1.702 * gate) * (up + 1.0)
            label = (first_ref[side] + e).astype(F32)
            share = jnp.sum(jnp.where(ids == label, expo, 0.0), axis=1, keepdims=True) / total
            acts.append((act * share).astype(BF16))
    copies[4].wait()
    copies[5].wait()
    chunk = 768
    for start in range(0, width, chunk):
        stop = min(start + chunk, width)
        part = None
        for side, d_ref in enumerate((d0, d1)):
            for e in range(per):
                piece = jnp.dot(
                    acts[side * per + e], d_ref[e, :, start:stop], preferred_element_type=F32
                )
                part = piece if part is None else part + piece
        out_ref[:, start:stop] = part.astype(BF16)


def experts(first, x, own, other):
    width = own[0].shape[2]
    args = (own[0], own[1], other[0], other[1], own[2], other[2])
    return pl.pallas_call(
        experts_kernel,
        in_specs=[smem(), vmem()] + [hbm()] * 6,
        out_specs=vmem(),
        out_shape=jax.ShapeDtypeStruct((x.shape[0], width), BF16),
        scratch_shapes=[pltpu.VMEM(a.shape, BF16) for a in args]
        + [pltpu.SemaphoreType.DMA((len(args),))],
        compiler_params=params(32),
        name="experts",
    )(first, x, *stay(*args))


def row_major(value):
    return with_layout_constraint(value, Layout(major_to_minor=tuple(range(value.ndim))))


def exchange(value, axis):
    return lax.all_to_all(value, axis, split_axis=0, concat_axis=0, tiled=True)


def on_device(
    hidden_in,
    queries,
    new_keys,
    new_values,
    key_cache,
    value_cache,
    prompt_lengths,
    out_weight,
    norm_gain,
    expert_ids,
    top_logits,
    gate_weight,
    up_weight,
    down_weight,
):
    steps, width = hidden_in.shape[1:]
    zaxis = ("w", "v")
    dp = ("x", "y")
    nz = lax.axis_size(zaxis)
    ndp = lax.axis_size(dp)
    z = lax.axis_index(zaxis)
    c = lax.axis_index("c")
    d = lax.axis_index(dp)
    per = gate_weight.shape[0]
    out_rows = out_weight.T
    other_out = lax.ppermute(out_rows, "c", SWAP)
    far_down = lax.ppermute(down_weight, "c", SWAP)
    attended, own_out = attend(
        prompt_lengths, queries, new_keys, new_values, key_cache, value_cache, out_rows, nz
    )
    place = jnp.stack([z, c, d]).astype(jnp.int32)
    first = jnp.stack([(2 * z + c) * per, (2 * z + 1 - c) * per]).astype(jnp.int32)
    attended, place, first = lax.optimization_barrier((attended, place, first))
    by_heads = exchange(attended, zaxis)
    ids, logits = expert_ids.transpose(1, 2, 0), top_logits.transpose(1, 2, 0)
    keep, sent = project(place, by_heads, hidden_in, ids, logits, own_out, other_out)
    sent, gain, down, gate, up = lax.optimization_barrier(
        (sent, norm_gain, down_weight, gate_weight, up_weight)
    )
    got = lax.ppermute(sent, "v", SWAP)
    far_gate, far_up = lax.ppermute(gate, "c", SWAP), lax.ppermute(up, "c", SWAP)
    got, gain, down = lax.optimization_barrier((got, gain[None], row_major(down)))
    keep, sent = join(keep, got)
    sent, far_down = lax.optimization_barrier((sent, far_down))
    got = lax.ppermute(sent, "w", [(i, i ^ 1) for i in range(nz // 2)])
    got, far_down = lax.optimization_barrier((got, row_major(far_down)))
    keep, sent = join(keep, got)
    sent, gate, up = lax.optimization_barrier((sent, gate, up))
    got = lax.ppermute(sent, "w", [(i, i ^ 2) for i in range(nz // 2)])
    got, gate, up = lax.optimization_barrier(
        (got, row_major(gate.swapaxes(1, 2)), row_major(up.swapaxes(1, 2)))
    )
    residual, copies = norm(place, keep, got, gain, ndp, steps)
    copies, far_gate, far_up = lax.optimization_barrier((copies, far_gate, far_up))
    tokens = exchange(copies, dp)
    tokens, far_gate, far_up = lax.optimization_barrier(
        (tokens, row_major(far_gate.swapaxes(1, 2)), row_major(far_up.swapaxes(1, 2)))
    )
    tokens = tokens.reshape(ndp * nz * steps, -1)
    made = experts(first, tokens, (gate, up, down), (far_gate, far_up, far_down))
    back = exchange(made.reshape(ndp, nz * steps, width), dp)
    column_sum = jnp.sum(back.astype(F32), axis=0).astype(BF16)
    final = exchange(column_sum.reshape(nz, steps, width), zaxis)
    out = residual + jnp.sum(final.astype(F32), axis=0)
    return out.astype(BF16)[None]


def solution(mesh):
    shape = dict(mesh.shape)
    side = int(round(shape["dp"] ** 0.5))
    fine = Mesh(
        mesh.devices.reshape(side, shape["dp"] // side, shape["expert"] // 4, 2, 2),
        ("x", "y", "w", "v", "c"),
    )
    row = ("w", "v", "c", "x", "y")
    group = ("w", "v", "c")
    dp = ("x", "y")
    placed = (
        P(row, None, None),
        P(row, None, None),
        P(row, None, None),
        P(row, None, None),
        P(row, None, None),
        P(row, None, None),
        P(row),
        P(group, None),
        P(),
        P(group, None, None),
        P(group, None, None),
        P(group, None, dp),
        P(group, None, dp),
        P(group, dp, None),
    )
    return jax.shard_map(
        on_device,
        mesh=fine,
        in_specs=placed,
        out_specs=P(row, None, None),
        check_vma=False,
    )
```

```python
import jax
import jax.numpy as jnp
from jax import lax
from jax.experimental import pallas as pl
from jax.experimental.pallas import tpu as pltpu
from jax.experimental.layout import Layout, with_layout_constraint
from jax.sharding import Mesh
from jax.sharding import PartitionSpec as P

HQ = 64
KVH = 8
HD = 64
SWAP = [(0, 1), (1, 0)]
F32 = jnp.float32
BF16 = jnp.bfloat16


def params(mib):
    return pltpu.CompilerParams(vmem_limit_bytes=mib * 1024 * 1024)


def vmem():
    return pl.BlockSpec(memory_space=pltpu.VMEM)


def hbm():
    return pl.BlockSpec(memory_space=pltpu.HBM)


def stay(*values):
    return [pltpu.with_memory_space_constraint(v, pltpu.HBM) for v in values]


def smem():
    return pl.BlockSpec(memory_space=pltpu.SMEM)


def attend_kernel(
    len_ref, q_hbm, nk_hbm, nv_hbm, k_hbm, v_hbm, w_hbm, out_ref, w_ref,
    q_ref, nk_ref, nv_ref, k_ref, v_ref, rows_ref, flat_ref, sems,
):
    pairs = (
        (k_hbm, k_ref), (q_hbm, q_ref), (nk_hbm, nk_ref), (nv_hbm, nv_ref), (v_hbm, v_ref),
        (w_hbm, w_ref),
    )
    copies = [pltpu.make_async_copy(a, b, sems.at[i]) for i, (a, b) in enumerate(pairs)]
    for copy in copies:
        copy.start()
    steps = q_ref.shape[1]
    width = KVH * HD
    rows = HQ * steps
    per_group = rows // KVH
    copies[1].wait()
    q = q_ref[0].astype(F32) * 0.125
    for h in range(HQ):
        rows_ref[h * steps : (h + 1) * steps, :] = q[:, h * HD : (h + 1) * HD]
    q_rows = rows_ref[...]
    q_pair = jnp.concatenate([q_rows, q_rows], axis=1)
    q_wide = jnp.concatenate([q_pair] * (KVH // 2), axis=1)
    row_id = lax.broadcasted_iota(jnp.int32, (rows, width), 0)
    col_id = lax.broadcasted_iota(jnp.int32, (rows, width), 1)
    in_group = row_id // per_group == col_id // HD
    q_wide = jnp.where(in_group, q_wide, 0.0)
    q_bf = q_wide.astype(BF16)
    copies[0].wait()
    scores = lax.dot_general(
        q_bf, k_ref[0], (((1,), (1,)), ((), ())), preferred_element_type=F32
    )
    slot = lax.broadcasted_iota(jnp.int32, scores.shape, 1)
    weights = jnp.where(slot < len_ref[0], jnp.exp(scores), 0.0)
    total = jnp.sum(weights, axis=1, keepdims=True)
    copies[2].wait()
    copies[3].wait()
    nk = nk_ref[0].astype(F32)
    nv = nv_ref[0].astype(F32)
    step_id = lax.broadcasted_iota(jnp.int32, (rows, 1), 0) % steps
    fresh = []
    for s in range(steps):
        score = jnp.sum(q_wide * nk[s : s + 1, :], axis=1, keepdims=True)
        weight = jnp.where(step_id >= s, jnp.exp(score), 0.0)
        total = total + weight
        fresh.append(weight)
    probs = (weights / total).astype(BF16)
    copies[4].wait()
    mixed = jnp.dot(probs, v_ref[0], preferred_element_type=F32)
    for s in range(steps):
        mixed = mixed + (fresh[s] / total).astype(BF16).astype(F32) * nv[s : s + 1, :]
    mixed = jnp.where(in_group, mixed, 0.0)
    folded = mixed[:, :128]
    for i in range(1, width // 128):
        folded = folded + mixed[:, i * 128 : (i + 1) * 128]
    rows_ref[...] = folded[:, :HD] + folded[:, HD:]
    for h in range(HQ):
        flat_ref[:, h * HD : (h + 1) * HD] = rows_ref[h * steps : (h + 1) * steps, :]
    blocks = out_ref.shape[0]
    wide = HQ * HD // blocks
    for b in range(blocks):
        out_ref[b] = flat_ref[:, b * wide : (b + 1) * wide].astype(BF16)
    copies[5].wait()


def attend(length, q, nk, nv, k, v, w, blocks):
    steps = q.shape[1]
    return pl.pallas_call(
        attend_kernel,
        in_specs=[smem()] + [hbm()] * 6,
        out_specs=[vmem(), vmem()],
        out_shape=[
            jax.ShapeDtypeStruct((blocks, steps, HQ * HD // blocks), BF16),
            jax.ShapeDtypeStruct(w.shape, BF16),
        ],
        scratch_shapes=[pltpu.VMEM(a.shape, BF16) for a in (q, nk, nv, k, v)]
        + [
            pltpu.VMEM((HQ * steps, HD), F32),
            pltpu.VMEM((steps, HQ * HD), F32),
            pltpu.SemaphoreType.DMA((6,)),
        ],
        compiler_params=params(12),
        name="attend",
    )(length, *stay(q, nk, nv, k, v, w))


def project_kernel(
    place_ref, x_ref, own_ref, other_ref, hid_hbm, ids_hbm, logits_hbm, keep_ref, send_ref,
    rows_ref, hid_ref, ids_ref, logits_ref, sems,
):
    width, feats = own_ref.shape
    chunk = 640
    cuts = [(start, min(start + chunk, width)) for start in range(0, width, chunk)]
    small = [
        pltpu.make_async_copy(hid_hbm, hid_ref, sems.at[0]),
        pltpu.make_async_copy(ids_hbm, ids_ref, sems.at[1]),
        pltpu.make_async_copy(logits_hbm, logits_ref, sems.at[2]),
    ]
    for copy in small:
        copy.start()
    blocks, steps, _ = x_ref.shape
    for i in range(blocks):
        rows_ref[i * steps : (i + 1) * steps, :] = x_ref[i].astype(F32)
    x = rows_ref[...].astype(BF16)
    low, high = x[:, :feats], x[:, feats:]
    first = place_ref[1] == 0
    mine = jnp.where(first, low, high)
    theirs = jnp.where(first, high, low)
    for copy in small:
        copy.wait()
    spare = keep_ref.shape[1] - width
    lane = lax.broadcasted_iota(jnp.int32, (1, spare), 1)
    routes = []
    for ref in (ids_ref, logits_ref):
        held = ref[...].astype(F32)
        row = lax.broadcasted_iota(jnp.int32, held.shape, 2)
        routes.append(
            jnp.sum(jnp.where(row == place_ref[2], held, 0.0), axis=2, keepdims=True)
        )
    top = routes[0].shape[1]
    lines = []
    for s in range(steps):
        line = jnp.zeros((1, spare), F32)
        for i, values in enumerate(routes):
            for k in range(top):
                line = jnp.where(lane == i * top + k, values[s, k : k + 1, :], line)
        lines.append(line)
    route = jnp.concatenate(lines, axis=0)
    extra = jnp.concatenate([hid_ref[0].astype(F32), route], axis=1)
    extra = jnp.concatenate([extra] * blocks, axis=0)
    block = lax.broadcasted_iota(jnp.int32, extra.shape, 0) // steps
    extra = jnp.where(block == place_ref[0], extra, 0.0)
    dims = (((1,), (1,)), ((), ()))
    for start, stop in cuts:
        part = lax.dot_general(mine, own_ref[start:stop], dims, preferred_element_type=F32)
        part = part + lax.dot_general(
            theirs, other_ref[start:stop], dims, preferred_element_type=F32
        )
        part = part + extra[:, start:stop]
        keep_ref[:, start:stop] = part
        send_ref[:, start:stop] = part.astype(BF16)
    keep_ref[:, width:] = extra[:, width:]
    send_ref[:, width:] = extra[:, width:].astype(BF16)


def project(place, x, hidden, ids, logits, own, other):
    blocks, steps, feats = x.shape
    wide = own.shape[0] + -own.shape[0] % 128
    rows = blocks * steps
    return pl.pallas_call(
        project_kernel,
        in_specs=[smem(), vmem(), vmem(), vmem()] + [hbm()] * 3,
        out_specs=[vmem(), vmem()],
        out_shape=[
            jax.ShapeDtypeStruct((rows, wide), F32),
            jax.ShapeDtypeStruct((rows, wide), BF16),
        ],
        scratch_shapes=[
            pltpu.VMEM((rows, feats), F32),
            pltpu.VMEM(hidden.shape, BF16),
            pltpu.VMEM(ids.shape, jnp.int32),
            pltpu.VMEM(logits.shape, BF16),
            pltpu.SemaphoreType.DMA((3,)),
        ],
        compiler_params=params(12),
        name="project",
    )(place, x, own, other, *stay(hidden, ids, logits))


def join_kernel(keep_ref, got_ref, next_ref, send_ref):
    total = keep_ref[...] + got_ref[...].astype(F32)
    next_ref[...] = total
    send_ref[...] = total.astype(BF16)


def join(keep, got):
    return pl.pallas_call(
        join_kernel,
        in_specs=[vmem(), vmem()],
        out_specs=[vmem(), vmem()],
        out_shape=[
            jax.ShapeDtypeStruct(keep.shape, F32),
            jax.ShapeDtypeStruct(keep.shape, BF16),
        ],
        compiler_params=params(12),
        name="join",
    )(keep, got)


def norm_kernel(
    place_ref, keep_ref, near_ref, back_ref, far_ref, gain_ref, res_ref, out_hbm, full_ref, sems
):
    steps, width = res_ref.shape
    total = keep_ref[...]
    for ref in (near_ref, back_ref, far_ref):
        total = total + ref[...].astype(F32)
    res = total[:, :width]
    scale = lax.rsqrt(jnp.sum(res * res, axis=1, keepdims=True) / width + 1e-05)
    normed = (res * scale * gain_ref[...]).astype(BF16)
    full_ref[...] = jnp.concatenate([normed.astype(F32), total[:, width:]], axis=1).astype(BF16)
    copies = [
        pltpu.make_async_copy(full_ref, out_hbm.at[i], sems.at[i])
        for i in range(out_hbm.shape[0])
    ]
    for copy in copies:
        copy.start()
    own = jnp.zeros((steps, width), F32)
    for i in range(res.shape[0] // steps):
        own = own + jnp.where(place_ref[0] == i, res[i * steps : (i + 1) * steps, :], 0.0)
    res_ref[...] = own
    for copy in copies:
        copy.wait()


def norm(place, keep, got, gain, copies, steps):
    rows, wide = keep.shape
    width = gain.shape[1]
    return pl.pallas_call(
        norm_kernel,
        in_specs=[smem()] + [vmem()] * 5,
        out_specs=[vmem(), hbm()],
        out_shape=[
            jax.ShapeDtypeStruct((steps, width), F32),
            jax.ShapeDtypeStruct((copies, rows, wide), BF16),
        ],
        scratch_shapes=[pltpu.VMEM((rows, wide), BF16), pltpu.SemaphoreType.DMA((copies,))],
        compiler_params=params(12),
        name="norm",
    )(place, keep, *got, gain)


def experts_kernel(
    first_ref, x_ref, g0_hbm, u0_hbm, g1_hbm, u1_hbm, d0_hbm, d1_hbm, out_ref,
    g0, u0, g1, u1, d0, d1, sems,
):
    pairs = (
        (g0_hbm, g0), (u0_hbm, u0), (g1_hbm, g1), (u1_hbm, u1), (d0_hbm, d0), (d1_hbm, d1),
    )
    per, _, width = g0.shape
    copies = [pltpu.make_async_copy(a, b, sems.at[i]) for i, (a, b) in enumerate(pairs)]
    for copy in copies:
        copy.start()
    x = x_ref[:, :width]
    route = x_ref[:, width : width + 8].astype(F32)
    ids = route[:, 0:4]
    expo = jnp.exp(route[:, 4:8])
    total = jnp.sum(expo, axis=1, keepdims=True)
    dims = (((1,), (1,)), ((), ()))
    acts = []
    for side, (g_ref, u_ref) in enumerate(((g0, u0), (g1, u1))):
        copies[2 * side].wait()
        gates = [
            lax.dot_general(x, g_ref[e], dims, preferred_element_type=F32) for e in range(per)
        ]
        copies[2 * side + 1].wait()
        for e in range(per):
            gate = gates[e]
            up = lax.dot_general(x, u_ref[e], dims, preferred_element_type=F32)
            act = gate * jax.nn.sigmoid(1.702 * gate) * (up + 1.0)
            label = (first_ref[side] + e).astype(F32)
            share = jnp.sum(jnp.where(ids == label, expo, 0.0), axis=1, keepdims=True) / total
            acts.append((act * share).astype(BF16))
    copies[4].wait()
    copies[5].wait()
    chunk = 768
    for start in range(0, width, chunk):
        stop = min(start + chunk, width)
        part = None
        for side, d_ref in enumerate((d0, d1)):
            for e in range(per):
                piece = jnp.dot(
                    acts[side * per + e], d_ref[e, :, start:stop], preferred_element_type=F32
                )
                part = piece if part is None else part + piece
        out_ref[:, start:stop] = part.astype(BF16)


def experts(first, x, own, other):
    width = own[0].shape[2]
    args = (own[0], own[1], other[0], other[1], own[2], other[2])
    return pl.pallas_call(
        experts_kernel,
        in_specs=[smem(), vmem()] + [hbm()] * 6,
        out_specs=vmem(),
        out_shape=jax.ShapeDtypeStruct((x.shape[0], width), BF16),
        scratch_shapes=[pltpu.VMEM(a.shape, BF16) for a in args]
        + [pltpu.SemaphoreType.DMA((len(args),))],
        compiler_params=params(32),
        name="experts",
    )(first, x, *stay(*args))


def row_major(value):
    return with_layout_constraint(value, Layout(major_to_minor=tuple(range(value.ndim))))


def exchange(value, axis):
    return lax.all_to_all(value, axis, split_axis=0, concat_axis=0, tiled=True)


def on_device(
    hidden_in,
    queries,
    new_keys,
    new_values,
    key_cache,
    value_cache,
    prompt_lengths,
    out_weight,
    norm_gain,
    expert_ids,
    top_logits,
    gate_weight,
    up_weight,
    down_weight,
):
    steps, width = hidden_in.shape[1:]
    zaxis = ("w", "v")
    dp = ("x", "y")
    nz = lax.axis_size(zaxis)
    ndp = lax.axis_size(dp)
    z = lax.axis_index(zaxis)
    c = lax.axis_index("c")
    d = lax.axis_index(dp)
    per = gate_weight.shape[0]
    out_rows = out_weight.T
    other_out = lax.ppermute(out_rows, "c", SWAP)
    far_down = lax.ppermute(down_weight, "c", SWAP)
    attended, own_out = attend(
        prompt_lengths, queries, new_keys, new_values, key_cache, value_cache, out_rows, nz
    )
    place = jnp.stack([z, c, d]).astype(jnp.int32)
    first = jnp.stack([(2 * z + c) * per, (2 * z + 1 - c) * per]).astype(jnp.int32)
    attended, place, first = lax.optimization_barrier((attended, place, first))
    by_heads = exchange(attended, zaxis)
    ids, logits = expert_ids.transpose(1, 2, 0), top_logits.transpose(1, 2, 0)
    keep, sent = project(place, by_heads, hidden_in, ids, logits, own_out, other_out)
    sent, gain, down, gate, up = lax.optimization_barrier(
        (sent, norm_gain, down_weight, gate_weight, up_weight)
    )
    got = lax.ppermute(sent, "v", SWAP)
    far_gate, far_up = lax.ppermute(gate, "c", SWAP), lax.ppermute(up, "c", SWAP)
    got, gain, down = lax.optimization_barrier((got, gain[None], row_major(down)))
    keep, sent = join(keep, got)
    sent, far_down, gate, up = lax.optimization_barrier((sent, far_down, gate, up))
    quarter = nz // 2
    got = [
        lax.ppermute(sent, "w", [(i, (i + k) % quarter) for i in range(quarter)])
        for k in range(1, quarter)
    ]
    far_down, gate, up = (
        row_major(far_down),
        row_major(gate.swapaxes(1, 2)),
        row_major(up.swapaxes(1, 2)),
    )
    far_down, gate, up, *got = lax.optimization_barrier((far_down, gate, up, *got))
    residual, copies = norm(place, keep, got, gain, ndp, steps)
    copies, far_gate, far_up = lax.optimization_barrier((copies, far_gate, far_up))
    tokens = exchange(copies, dp)
    tokens, far_gate, far_up = lax.optimization_barrier(
        (tokens, row_major(far_gate.swapaxes(1, 2)), row_major(far_up.swapaxes(1, 2)))
    )
    tokens = tokens.reshape(ndp * nz * steps, -1)
    made = experts(first, tokens, (gate, up, down), (far_gate, far_up, far_down))
    back = exchange(made.reshape(ndp, nz * steps, width), dp)
    column_sum = jnp.sum(back.astype(F32), axis=0).astype(BF16)
    final = exchange(column_sum.reshape(nz, steps, width), zaxis)
    out = residual + jnp.sum(final.astype(F32), axis=0)
    return out.astype(BF16)[None]


def solution(mesh):
    shape = dict(mesh.shape)
    side = int(round(shape["dp"] ** 0.5))
    fine = Mesh(
        mesh.devices.reshape(side, shape["dp"] // side, shape["expert"] // 4, 2, 2),
        ("x", "y", "w", "v", "c"),
    )
    row = ("w", "v", "c", "x", "y")
    group = ("w", "v", "c")
    dp = ("x", "y")
    placed = (
        P(row, None, None),
        P(row, None, None),
        P(row, None, None),
        P(row, None, None),
        P(row, None, None),
        P(row, None, None),
        P(row),
        P(group, None),
        P(),
        P(group, None, None),
        P(group, None, None),
        P(group, None, dp),
        P(group, None, dp),
        P(group, dp, None),
    )
    return jax.shard_map(
        on_device,
        mesh=fine,
        in_specs=placed,
        out_specs=P(row, None, None),
        check_vma=False,
    )
```

```python
import jax
import jax.numpy as jnp
from jax import lax
from jax.experimental import pallas as pl
from jax.experimental.pallas import tpu as pltpu
from jax.experimental.layout import Layout, with_layout_constraint
from jax.sharding import Mesh
from jax.sharding import PartitionSpec as P

HQ = 64
KVH = 8
HD = 64
SWAP = [(0, 1), (1, 0)]
F32 = jnp.float32
BF16 = jnp.bfloat16


def params(mib):
    return pltpu.CompilerParams(vmem_limit_bytes=mib * 1024 * 1024)


def vmem():
    return pl.BlockSpec(memory_space=pltpu.VMEM)


def hbm():
    return pl.BlockSpec(memory_space=pltpu.HBM)


def stay(*values):
    return [pltpu.with_memory_space_constraint(v, pltpu.HBM) for v in values]


def smem():
    return pl.BlockSpec(memory_space=pltpu.SMEM)


def attend_kernel(
    len_ref, q_hbm, nk_hbm, nv_hbm, k_hbm, v_hbm, w_hbm, out_ref, w_ref,
    q_ref, nk_ref, nv_ref, k_ref, v_ref, rows_ref, flat_ref, sems,
):
    pairs = (
        (k_hbm, k_ref), (q_hbm, q_ref), (nk_hbm, nk_ref), (nv_hbm, nv_ref), (v_hbm, v_ref),
        (w_hbm, w_ref),
    )
    copies = [pltpu.make_async_copy(a, b, sems.at[i]) for i, (a, b) in enumerate(pairs)]
    for copy in copies:
        copy.start()
    steps = q_ref.shape[1]
    width = KVH * HD
    rows = HQ * steps
    per_group = rows // KVH
    copies[1].wait()
    q = q_ref[0].astype(F32) * 0.125
    for h in range(HQ):
        rows_ref[h * steps : (h + 1) * steps, :] = q[:, h * HD : (h + 1) * HD]
    q_rows = rows_ref[...]
    q_pair = jnp.concatenate([q_rows, q_rows], axis=1)
    q_wide = jnp.concatenate([q_pair] * (KVH // 2), axis=1)
    row_id = lax.broadcasted_iota(jnp.int32, (rows, width), 0)
    col_id = lax.broadcasted_iota(jnp.int32, (rows, width), 1)
    in_group = row_id // per_group == col_id // HD
    q_wide = jnp.where(in_group, q_wide, 0.0)
    q_bf = q_wide.astype(BF16)
    copies[0].wait()
    scores = lax.dot_general(
        q_bf, k_ref[0], (((1,), (1,)), ((), ())), preferred_element_type=F32
    )
    slot = lax.broadcasted_iota(jnp.int32, scores.shape, 1)
    weights = jnp.where(slot < len_ref[0], jnp.exp(scores), 0.0)
    total = jnp.sum(weights, axis=1, keepdims=True)
    copies[2].wait()
    copies[3].wait()
    nk = nk_ref[0].astype(F32)
    nv = nv_ref[0].astype(F32)
    step_id = lax.broadcasted_iota(jnp.int32, (rows, 1), 0) % steps
    fresh = []
    for s in range(steps):
        score = jnp.sum(q_wide * nk[s : s + 1, :], axis=1, keepdims=True)
        weight = jnp.where(step_id >= s, jnp.exp(score), 0.0)
        total = total + weight
        fresh.append(weight)
    probs = (weights / total).astype(BF16)
    copies[4].wait()
    mixed = jnp.dot(probs, v_ref[0], preferred_element_type=F32)
    for s in range(steps):
        mixed = mixed + (fresh[s] / total).astype(BF16).astype(F32) * nv[s : s + 1, :]
    mixed = jnp.where(in_group, mixed, 0.0)
    folded = mixed[:, :128]
    for i in range(1, width // 128):
        folded = folded + mixed[:, i * 128 : (i + 1) * 128]
    rows_ref[...] = folded[:, :HD] + folded[:, HD:]
    for h in range(HQ):
        flat_ref[:, h * HD : (h + 1) * HD] = rows_ref[h * steps : (h + 1) * steps, :]
    blocks = out_ref.shape[0]
    wide = HQ * HD // blocks
    for b in range(blocks):
        out_ref[b] = flat_ref[:, b * wide : (b + 1) * wide].astype(BF16)
    copies[5].wait()


def attend(length, q, nk, nv, k, v, w, blocks):
    steps = q.shape[1]
    return pl.pallas_call(
        attend_kernel,
        in_specs=[smem()] + [hbm()] * 6,
        out_specs=[vmem(), vmem()],
        out_shape=[
            jax.ShapeDtypeStruct((blocks, steps, HQ * HD // blocks), BF16),
            jax.ShapeDtypeStruct(w.shape, BF16),
        ],
        scratch_shapes=[pltpu.VMEM(a.shape, BF16) for a in (q, nk, nv, k, v)]
        + [
            pltpu.VMEM((HQ * steps, HD), F32),
            pltpu.VMEM((steps, HQ * HD), F32),
            pltpu.SemaphoreType.DMA((6,)),
        ],
        compiler_params=params(12),
        name="attend",
    )(length, *stay(q, nk, nv, k, v, w))


def project_kernel(
    place_ref, x_ref, own_ref, other_ref, hid_hbm, ids_hbm, logits_hbm, keep_ref, send_ref,
    rows_ref, hid_ref, ids_ref, logits_ref, sems,
):
    width, feats = own_ref.shape
    chunk = 640
    cuts = [(start, min(start + chunk, width)) for start in range(0, width, chunk)]
    small = [
        pltpu.make_async_copy(hid_hbm, hid_ref, sems.at[0]),
        pltpu.make_async_copy(ids_hbm, ids_ref, sems.at[1]),
        pltpu.make_async_copy(logits_hbm, logits_ref, sems.at[2]),
    ]
    for copy in small:
        copy.start()
    blocks, steps, _ = x_ref.shape
    for i in range(blocks):
        rows_ref[i * steps : (i + 1) * steps, :] = x_ref[i].astype(F32)
    x = rows_ref[...].astype(BF16)
    low, high = x[:, :feats], x[:, feats:]
    first = place_ref[1] == 0
    mine = jnp.where(first, low, high)
    theirs = jnp.where(first, high, low)
    for copy in small:
        copy.wait()
    spare = keep_ref.shape[1] - width
    lane = lax.broadcasted_iota(jnp.int32, (1, spare), 1)
    routes = []
    for ref in (ids_ref, logits_ref):
        held = ref[...].astype(F32)
        row = lax.broadcasted_iota(jnp.int32, held.shape, 2)
        routes.append(
            jnp.sum(jnp.where(row == place_ref[2], held, 0.0), axis=2, keepdims=True)
        )
    top = routes[0].shape[1]
    lines = []
    for s in range(steps):
        line = jnp.zeros((1, spare), F32)
        for i, values in enumerate(routes):
            for k in range(top):
                line = jnp.where(lane == i * top + k, values[s, k : k + 1, :], line)
        lines.append(line)
    route = jnp.concatenate(lines, axis=0)
    extra = jnp.concatenate([hid_ref[0].astype(F32), route], axis=1)
    extra = jnp.concatenate([extra] * blocks, axis=0)
    block = lax.broadcasted_iota(jnp.int32, extra.shape, 0) // steps
    extra = jnp.where(block == place_ref[0], extra, 0.0)
    dims = (((1,), (1,)), ((), ()))
    for start, stop in cuts:
        part = lax.dot_general(mine, own_ref[start:stop], dims, preferred_element_type=F32)
        part = part + lax.dot_general(
            theirs, other_ref[start:stop], dims, preferred_element_type=F32
        )
        part = part + extra[:, start:stop]
        keep_ref[:, start:stop] = part
        send_ref[:, start:stop] = part.astype(BF16)
    keep_ref[:, width:] = extra[:, width:]
    send_ref[:, width:] = extra[:, width:].astype(BF16)


def project(place, x, hidden, ids, logits, own, other):
    blocks, steps, feats = x.shape
    wide = own.shape[0] + -own.shape[0] % 128
    rows = blocks * steps
    return pl.pallas_call(
        project_kernel,
        in_specs=[smem(), vmem(), vmem(), vmem()] + [hbm()] * 3,
        out_specs=[vmem(), vmem()],
        out_shape=[
            jax.ShapeDtypeStruct((rows, wide), F32),
            jax.ShapeDtypeStruct((rows, wide), BF16),
        ],
        scratch_shapes=[
            pltpu.VMEM((rows, feats), F32),
            pltpu.VMEM(hidden.shape, BF16),
            pltpu.VMEM(ids.shape, jnp.int32),
            pltpu.VMEM(logits.shape, BF16),
            pltpu.SemaphoreType.DMA((3,)),
        ],
        compiler_params=params(12),
        name="project",
    )(place, x, own, other, *stay(hidden, ids, logits))


def join_kernel(keep_ref, got_ref, next_ref, send_ref):
    total = keep_ref[...] + got_ref[...].astype(F32)
    next_ref[...] = total
    send_ref[...] = total.astype(BF16)


def join(keep, got):
    return pl.pallas_call(
        join_kernel,
        in_specs=[vmem(), vmem()],
        out_specs=[vmem(), vmem()],
        out_shape=[
            jax.ShapeDtypeStruct(keep.shape, F32),
            jax.ShapeDtypeStruct(keep.shape, BF16),
        ],
        compiler_params=params(12),
        name="join",
    )(keep, got)


def norm_kernel(
    place_ref, keep_ref, near_ref, back_ref, far_ref, gain_ref, res_ref, out_hbm, full_ref, sems
):
    steps, width = res_ref.shape
    total = keep_ref[...]
    for ref in (near_ref, back_ref, far_ref):
        total = total + ref[...].astype(F32)
    res = total[:, :width]
    scale = lax.rsqrt(jnp.sum(res * res, axis=1, keepdims=True) / width + 1e-05)
    normed = (res * scale * gain_ref[...]).astype(BF16)
    full_ref[...] = jnp.concatenate([normed.astype(F32), total[:, width:]], axis=1).astype(BF16)
    copies = [
        pltpu.make_async_copy(full_ref, out_hbm.at[i], sems.at[i])
        for i in range(out_hbm.shape[0])
    ]
    for copy in copies:
        copy.start()
    own = jnp.zeros((steps, width), F32)
    for i in range(res.shape[0] // steps):
        own = own + jnp.where(place_ref[0] == i, res[i * steps : (i + 1) * steps, :], 0.0)
    res_ref[...] = own
    for copy in copies:
        copy.wait()


def norm(place, keep, got, gain, copies, steps):
    rows, wide = keep.shape
    width = gain.shape[1]
    return pl.pallas_call(
        norm_kernel,
        in_specs=[smem()] + [vmem()] * 5,
        out_specs=[vmem(), hbm()],
        out_shape=[
            jax.ShapeDtypeStruct((steps, width), F32),
            jax.ShapeDtypeStruct((copies, rows, wide), BF16),
        ],
        scratch_shapes=[pltpu.VMEM((rows, wide), BF16), pltpu.SemaphoreType.DMA((copies,))],
        compiler_params=params(12),
        name="norm",
    )(place, keep, *got, gain)


def experts_kernel(
    first_ref, x_ref, g0_hbm, u0_hbm, g1_hbm, u1_hbm, d0_hbm, d1_hbm, out_ref,
    g0, u0, g1, u1, d0, d1, sems,
):
    pairs = (
        (g0_hbm, g0), (u0_hbm, u0), (g1_hbm, g1), (u1_hbm, u1), (d0_hbm, d0), (d1_hbm, d1),
    )
    per, _, width = g0.shape
    copies = [pltpu.make_async_copy(a, b, sems.at[i]) for i, (a, b) in enumerate(pairs)]
    for copy in copies:
        copy.start()
    x = x_ref[:, :width]
    route = x_ref[:, width : width + 8].astype(F32)
    ids = route[:, 0:4]
    expo = jnp.exp(route[:, 4:8])
    total = jnp.sum(expo, axis=1, keepdims=True)
    dims = (((1,), (1,)), ((), ()))
    acts = []
    for side, (g_ref, u_ref) in enumerate(((g0, u0), (g1, u1))):
        copies[2 * side].wait()
        gates = [
            lax.dot_general(x, g_ref[e], dims, preferred_element_type=F32) for e in range(per)
        ]
        copies[2 * side + 1].wait()
        for e in range(per):
            gate = gates[e]
            up = lax.dot_general(x, u_ref[e], dims, preferred_element_type=F32)
            act = gate * jax.nn.sigmoid(1.702 * gate) * (up + 1.0)
            label = (first_ref[side] + e).astype(F32)
            share = jnp.sum(jnp.where(ids == label, expo, 0.0), axis=1, keepdims=True) / total
            acts.append((act * share).astype(BF16))
    copies[4].wait()
    copies[5].wait()
    chunk = 1536
    for start in range(0, width, chunk):
        stop = min(start + chunk, width)
        part = None
        for side, d_ref in enumerate((d0, d1)):
            for e in range(per):
                piece = jnp.dot(
                    acts[side * per + e], d_ref[e, :, start:stop], preferred_element_type=F32
                )
                part = piece if part is None else part + piece
        out_ref[:, start:stop] = part.astype(BF16)


def experts(first, x, own, other):
    width = own[0].shape[2]
    args = (own[0], own[1], other[0], other[1], own[2], other[2])
    return pl.pallas_call(
        experts_kernel,
        in_specs=[smem(), vmem()] + [hbm()] * 6,
        out_specs=vmem(),
        out_shape=jax.ShapeDtypeStruct((x.shape[0], width), BF16),
        scratch_shapes=[pltpu.VMEM(a.shape, BF16) for a in args]
        + [pltpu.SemaphoreType.DMA((len(args),))],
        compiler_params=params(32),
        name="experts",
    )(first, x, *stay(*args))


def row_major(value):
    return with_layout_constraint(value, Layout(major_to_minor=tuple(range(value.ndim))))


def exchange(value, axis):
    return lax.all_to_all(value, axis, split_axis=0, concat_axis=0, tiled=True)


def on_device(
    hidden_in,
    queries,
    new_keys,
    new_values,
    key_cache,
    value_cache,
    prompt_lengths,
    out_weight,
    norm_gain,
    expert_ids,
    top_logits,
    gate_weight,
    up_weight,
    down_weight,
):
    steps, width = hidden_in.shape[1:]
    zaxis = ("w", "v")
    dp = ("x", "y")
    nz = lax.axis_size(zaxis)
    ndp = lax.axis_size(dp)
    z = lax.axis_index(zaxis)
    c = lax.axis_index("c")
    d = lax.axis_index(dp)
    per = gate_weight.shape[0]
    out_rows = out_weight.T
    other_out = lax.ppermute(out_rows, "c", SWAP)
    far_down, far_gate, far_up = (
        lax.ppermute(w, "c", SWAP) for w in (down_weight, gate_weight, up_weight)
    )
    attended, own_out = attend(
        prompt_lengths, queries, new_keys, new_values, key_cache, value_cache, out_rows, nz
    )
    place = jnp.stack([z, c, d]).astype(jnp.int32)
    first = jnp.stack([(2 * z + c) * per, (2 * z + 1 - c) * per]).astype(jnp.int32)
    attended, place, first = lax.optimization_barrier((attended, place, first))
    by_heads = exchange(attended, zaxis)
    ids, logits = expert_ids.transpose(1, 2, 0), top_logits.transpose(1, 2, 0)
    keep, sent = project(place, by_heads, hidden_in, ids, logits, own_out, other_out)
    sent, gain, down = lax.optimization_barrier((sent, norm_gain, down_weight))
    got = lax.ppermute(sent, "v", SWAP)
    got, gain, down = lax.optimization_barrier((got, gain[None], row_major(down)))
    keep, sent = join(keep, got)
    sent, far_down = lax.optimization_barrier((sent, far_down))
    quarter = nz // 2
    got = [
        lax.ppermute(sent, "w", [(i, (i + k) % quarter) for i in range(quarter)])
        for k in range(1, quarter)
    ]
    far_down, *got = lax.optimization_barrier((row_major(far_down), *got))
    residual, copies = norm(place, keep, got, gain, ndp, steps)
    copies, *weights = lax.optimization_barrier(
        (copies, gate_weight, up_weight, far_gate, far_up)
    )
    tokens = exchange(copies, dp)
    relaid = [row_major(w.swapaxes(1, 2)) for w in weights]
    tokens, gate, up, far_gate, far_up = lax.optimization_barrier((tokens, *relaid))
    tokens = tokens.reshape(ndp * nz * steps, -1)
    made = experts(first, tokens, (gate, up, down), (far_gate, far_up, far_down))
    back = exchange(made.reshape(ndp, nz * steps, width), dp)
    column_sum = jnp.sum(back.astype(F32), axis=0).astype(BF16)
    final = exchange(column_sum.reshape(nz, steps, width), zaxis)
    out = residual + jnp.sum(final.astype(F32), axis=0)
    return out.astype(BF16)[None]


def solution(mesh):
    shape = dict(mesh.shape)
    side = int(round(shape["dp"] ** 0.5))
    fine = Mesh(
        mesh.devices.reshape(side, shape["dp"] // side, shape["expert"] // 4, 2, 2),
        ("x", "y", "w", "v", "c"),
    )
    row = ("w", "v", "c", "x", "y")
    group = ("w", "v", "c")
    dp = ("x", "y")
    placed = (
        P(row, None, None),
        P(row, None, None),
        P(row, None, None),
        P(row, None, None),
        P(row, None, None),
        P(row, None, None),
        P(row),
        P(group, None),
        P(),
        P(group, None, None),
        P(group, None, None),
        P(group, None, dp),
        P(group, None, dp),
        P(group, dp, None),
    )
    return jax.shard_map(
        on_device,
        mesh=fine,
        in_specs=placed,
        out_specs=P(row, None, None),
        check_vma=False,
    )
```

```python
import jax
import jax.numpy as jnp
from jax import lax
from jax.experimental import pallas as pl
from jax.experimental.pallas import tpu as pltpu
from jax.experimental.layout import Layout, with_layout_constraint
from jax.sharding import Mesh
from jax.sharding import PartitionSpec as P

HQ = 64
KVH = 8
HD = 64
SWAP = [(0, 1), (1, 0)]
F32 = jnp.float32
BF16 = jnp.bfloat16


def params(mib):
    return pltpu.CompilerParams(vmem_limit_bytes=mib * 1024 * 1024)


def vmem():
    return pl.BlockSpec(memory_space=pltpu.VMEM)


def hbm():
    return pl.BlockSpec(memory_space=pltpu.HBM)


def stay(*values):
    return [pltpu.with_memory_space_constraint(v, pltpu.HBM) for v in values]


def smem():
    return pl.BlockSpec(memory_space=pltpu.SMEM)


def attend_kernel(
    len_ref, place_ref, q_hbm, nk_hbm, nv_hbm, k_hbm, v_hbm, w_hbm, hid_hbm, ids_hbm, logits_hbm,
    out_ref, w_ref, extra_ref, hid_ref, ids_ref, logits_ref, q_ref, nk_ref, nv_ref, k_ref, v_ref, rows_ref, flat_ref, sems,
):
    pairs = (
        (k_hbm, k_ref), (q_hbm, q_ref), (nk_hbm, nk_ref), (nv_hbm, nv_ref), (v_hbm, v_ref),
        (w_hbm, w_ref), (hid_hbm, hid_ref), (ids_hbm, ids_ref), (logits_hbm, logits_ref),
    )
    copies = [pltpu.make_async_copy(a, b, sems.at[i]) for i, (a, b) in enumerate(pairs)]
    for i in (1, 0, 6, 7, 8, 2, 3, 4, 5):
        copies[i].start()
    steps = q_ref.shape[1]
    width = KVH * HD
    rows = HQ * steps
    per_group = rows // KVH
    copies[1].wait()
    q = q_ref[0].astype(F32) * 0.125
    for h in range(HQ):
        rows_ref[h * steps : (h + 1) * steps, :] = q[:, h * HD : (h + 1) * HD]
    q_rows = rows_ref[...]
    q_pair = jnp.concatenate([q_rows, q_rows], axis=1)
    q_wide = jnp.concatenate([q_pair] * (KVH // 2), axis=1)
    row_id = lax.broadcasted_iota(jnp.int32, (rows, width), 0)
    col_id = lax.broadcasted_iota(jnp.int32, (rows, width), 1)
    in_group = row_id // per_group == col_id // HD
    q_wide = jnp.where(in_group, q_wide, 0.0)
    q_bf = q_wide.astype(BF16)
    for i in (6, 7, 8):
        copies[i].wait()
    spare = extra_ref.shape[1] - hid_ref.shape[2]
    lane = lax.broadcasted_iota(jnp.int32, (1, spare), 1)
    routes = []
    for ref in (ids_ref, logits_ref):
        held = ref[...].astype(F32)
        row = lax.broadcasted_iota(jnp.int32, held.shape, 2)
        routes.append(
            jnp.sum(jnp.where(row == place_ref[2], held, 0.0), axis=2, keepdims=True)
        )
    top = routes[0].shape[1]
    lines = []
    for s in range(steps):
        line = jnp.zeros((1, spare), F32)
        for i, values in enumerate(routes):
            for k in range(top):
                line = jnp.where(lane == i * top + k, values[s, k : k + 1, :], line)
        lines.append(line)
    route = jnp.concatenate(lines, axis=0)
    extra_ref[...] = jnp.concatenate([hid_ref[0].astype(F32), route], axis=1)
    copies[0].wait()
    scores = lax.dot_general(
        q_bf, k_ref[0], (((1,), (1,)), ((), ())), preferred_element_type=F32
    )
    slot = lax.broadcasted_iota(jnp.int32, scores.shape, 1)
    weights = jnp.where(slot < len_ref[0], jnp.exp(scores), 0.0)
    total = jnp.sum(weights, axis=1, keepdims=True)
    copies[2].wait()
    copies[3].wait()
    nk = nk_ref[0].astype(F32)
    nv = nv_ref[0].astype(F32)
    step_id = lax.broadcasted_iota(jnp.int32, (rows, 1), 0) % steps
    fresh = []
    for s in range(steps):
        score = jnp.sum(q_wide * nk[s : s + 1, :], axis=1, keepdims=True)
        weight = jnp.where(step_id >= s, jnp.exp(score), 0.0)
        total = total + weight
        fresh.append(weight)
    probs = (weights / total).astype(BF16)
    copies[4].wait()
    mixed = jnp.dot(probs, v_ref[0], preferred_element_type=F32)
    for s in range(steps):
        mixed = mixed + (fresh[s] / total).astype(BF16).astype(F32) * nv[s : s + 1, :]
    mixed = jnp.where(in_group, mixed, 0.0)
    folded = mixed[:, :128]
    for i in range(1, width // 128):
        folded = folded + mixed[:, i * 128 : (i + 1) * 128]
    rows_ref[...] = folded[:, :HD] + folded[:, HD:]
    for h in range(HQ):
        flat_ref[:, h * HD : (h + 1) * HD] = rows_ref[h * steps : (h + 1) * steps, :]
    blocks = out_ref.shape[0]
    wide = HQ * HD // blocks
    for b in range(blocks):
        out_ref[b] = flat_ref[:, b * wide : (b + 1) * wide].astype(BF16)
    copies[5].wait()


def attend(length, place, q, nk, nv, k, v, w, hidden, ids, logits, blocks):
    steps = q.shape[1]
    width = hidden.shape[2]
    args = (q, nk, nv, k, v, w, hidden, ids, logits)
    return pl.pallas_call(
        attend_kernel,
        in_specs=[smem(), smem()] + [hbm()] * len(args),
        out_specs=[vmem(), vmem(), vmem()],
        out_shape=[
            jax.ShapeDtypeStruct((blocks, steps, HQ * HD // blocks), BF16),
            jax.ShapeDtypeStruct(w.shape, BF16),
            jax.ShapeDtypeStruct((steps, width + -width % 128), F32),
        ],
        scratch_shapes=[pltpu.VMEM(a.shape, a.dtype) for a in (hidden, ids, logits)]
        + [pltpu.VMEM(a.shape, BF16) for a in (q, nk, nv, k, v)]
        + [
            pltpu.VMEM((HQ * steps, HD), F32),
            pltpu.VMEM((steps, HQ * HD), F32),
            pltpu.SemaphoreType.DMA((len(args),)),
        ],
        compiler_params=params(12),
        name="attend",
    )(length, place, *stay(*args))


def project_kernel(
    place_ref, x_ref, line_ref, own_ref, other_ref, keep_ref, send_ref, rows_ref
):
    width, feats = own_ref.shape
    chunk = 640
    blocks, steps, _ = x_ref.shape
    for i in range(blocks):
        rows_ref[i * steps : (i + 1) * steps, :] = x_ref[i].astype(F32)
    x = rows_ref[...].astype(BF16)
    low, high = x[:, :feats], x[:, feats:]
    first = place_ref[1] == 0
    mine = jnp.where(first, low, high)
    theirs = jnp.where(first, high, low)
    extra = jnp.concatenate([line_ref[...]] * blocks, axis=0)
    block = lax.broadcasted_iota(jnp.int32, extra.shape, 0) // steps
    extra = jnp.where(block == place_ref[0], extra, 0.0)
    dims = (((1,), (1,)), ((), ()))
    for start in range(0, width, chunk):
        stop = min(start + chunk, width)
        part = lax.dot_general(mine, own_ref[start:stop], dims, preferred_element_type=F32)
        part = part + lax.dot_general(
            theirs, other_ref[start:stop], dims, preferred_element_type=F32
        )
        part = part + extra[:, start:stop]
        keep_ref[:, start:stop] = part
        send_ref[:, start:stop] = part.astype(BF16)
    keep_ref[:, width:] = extra[:, width:]
    send_ref[:, width:] = extra[:, width:].astype(BF16)


def project(place, x, line, own, other):
    blocks, steps, feats = x.shape
    rows = blocks * steps
    return pl.pallas_call(
        project_kernel,
        in_specs=[smem()] + [vmem()] * 4,
        out_specs=[vmem(), vmem()],
        out_shape=[
            jax.ShapeDtypeStruct((rows, line.shape[1]), F32),
            jax.ShapeDtypeStruct((rows, line.shape[1]), BF16),
        ],
        scratch_shapes=[pltpu.VMEM((rows, feats), F32)],
        compiler_params=params(12),
        name="project",
    )(place, x, line, own, other)


def join_kernel(keep_ref, got_ref, next_ref, send_ref):
    total = keep_ref[...] + got_ref[...].astype(F32)
    next_ref[...] = total
    send_ref[...] = total.astype(BF16)


def join(keep, got):
    return pl.pallas_call(
        join_kernel,
        in_specs=[vmem(), vmem()],
        out_specs=[vmem(), vmem()],
        out_shape=[
            jax.ShapeDtypeStruct(keep.shape, F32),
            jax.ShapeDtypeStruct(keep.shape, BF16),
        ],
        compiler_params=params(12),
        name="join",
    )(keep, got)


def norm_kernel(
    place_ref, keep_ref, near_ref, back_ref, far_ref, gain_ref, res_ref, out_hbm, full_ref, sems
):
    steps, width = res_ref.shape
    total = keep_ref[...]
    for ref in (near_ref, back_ref, far_ref):
        total = total + ref[...].astype(F32)
    res = total[:, :width]
    scale = lax.rsqrt(jnp.sum(res * res, axis=1, keepdims=True) / width + 1e-05)
    normed = (res * scale * gain_ref[...]).astype(BF16)
    full_ref[...] = jnp.concatenate([normed.astype(F32), total[:, width:]], axis=1).astype(BF16)
    copies = [
        pltpu.make_async_copy(full_ref, out_hbm.at[i], sems.at[i])
        for i in range(out_hbm.shape[0])
    ]
    for copy in copies:
        copy.start()
    own = jnp.zeros((steps, width), F32)
    for i in range(res.shape[0] // steps):
        own = own + jnp.where(place_ref[0] == i, res[i * steps : (i + 1) * steps, :], 0.0)
    res_ref[...] = own
    for copy in copies:
        copy.wait()


def norm(place, keep, got, gain, copies, steps):
    rows, wide = keep.shape
    width = gain.shape[1]
    return pl.pallas_call(
        norm_kernel,
        in_specs=[smem()] + [vmem()] * 5,
        out_specs=[vmem(), hbm()],
        out_shape=[
            jax.ShapeDtypeStruct((steps, width), F32),
            jax.ShapeDtypeStruct((copies, rows, wide), BF16),
        ],
        scratch_shapes=[pltpu.VMEM((rows, wide), BF16), pltpu.SemaphoreType.DMA((copies,))],
        compiler_params=params(12),
        name="norm",
    )(place, keep, *got, gain)


def experts_kernel(
    first_ref, x_ref, g0_hbm, u0_hbm, g1_hbm, u1_hbm, d0_hbm, d1_hbm, out_ref,
    g0, u0, g1, u1, d0, d1, sems,
):
    pairs = (
        (g0_hbm, g0), (u0_hbm, u0), (g1_hbm, g1), (u1_hbm, u1), (d0_hbm, d0), (d1_hbm, d1),
    )
    per, _, width = g0.shape
    copies = [pltpu.make_async_copy(a, b, sems.at[i]) for i, (a, b) in enumerate(pairs)]
    for copy in copies:
        copy.start()
    x = x_ref[:, :width]
    route = x_ref[:, width : width + 8].astype(F32)
    ids = route[:, 0:4]
    expo = jnp.exp(route[:, 4:8])
    total = jnp.sum(expo, axis=1, keepdims=True)
    dims = (((1,), (1,)), ((), ()))
    acts = []
    for side, (g_ref, u_ref) in enumerate(((g0, u0), (g1, u1))):
        copies[2 * side].wait()
        gates = [
            lax.dot_general(x, g_ref[e], dims, preferred_element_type=F32) for e in range(per)
        ]
        copies[2 * side + 1].wait()
        for e in range(per):
            gate = gates[e]
            up = lax.dot_general(x, u_ref[e], dims, preferred_element_type=F32)
            act = gate * jax.nn.sigmoid(1.702 * gate) * (up + 1.0)
            label = (first_ref[side] + e).astype(F32)
            share = jnp.sum(jnp.where(ids == label, expo, 0.0), axis=1, keepdims=True) / total
            acts.append((act * share).astype(BF16))
    copies[4].wait()
    copies[5].wait()
    part = None
    for side, d_ref in enumerate((d0, d1)):
        for e in range(per):
            piece = jnp.dot(acts[side * per + e], d_ref[e], preferred_element_type=F32)
            part = piece if part is None else part + piece
    out_ref[...] = part.astype(BF16)


def experts(first, x, own, other):
    width = own[0].shape[2]
    args = (own[0], own[1], other[0], other[1], own[2], other[2])
    return pl.pallas_call(
        experts_kernel,
        in_specs=[smem(), vmem()] + [hbm()] * 6,
        out_specs=vmem(),
        out_shape=jax.ShapeDtypeStruct((x.shape[0], width), BF16),
        scratch_shapes=[pltpu.VMEM(a.shape, BF16) for a in args]
        + [pltpu.SemaphoreType.DMA((len(args),))],
        compiler_params=params(32),
        name="experts",
    )(first, x, *stay(*args))


def row_major(value):
    return with_layout_constraint(value, Layout(major_to_minor=tuple(range(value.ndim))))


def exchange(value, axis):
    return lax.all_to_all(value, axis, split_axis=0, concat_axis=0, tiled=True)


def on_device(
    hidden_in,
    queries,
    new_keys,
    new_values,
    key_cache,
    value_cache,
    prompt_lengths,
    out_weight,
    norm_gain,
    expert_ids,
    top_logits,
    gate_weight,
    up_weight,
    down_weight,
):
    steps, width = hidden_in.shape[1:]
    zaxis = ("w", "v")
    dp = ("x", "y")
    nz = lax.axis_size(zaxis)
    ndp = lax.axis_size(dp)
    z = lax.axis_index(zaxis)
    c = lax.axis_index("c")
    d = lax.axis_index(dp)
    per = gate_weight.shape[0]
    out_rows = out_weight.T
    other_out = lax.ppermute(out_rows, "c", SWAP)
    far_down, far_gate, far_up = (
        lax.ppermute(w, "c", SWAP) for w in (down_weight, gate_weight, up_weight)
    )
    place = jnp.stack([z, c, d]).astype(jnp.int32)
    first = jnp.stack([(2 * z + c) * per, (2 * z + 1 - c) * per]).astype(jnp.int32)
    ids, logits = expert_ids.transpose(1, 2, 0), top_logits.transpose(1, 2, 0)
    attended, own_out, line = attend(
        prompt_lengths, place, queries, new_keys, new_values, key_cache, value_cache,
        out_rows, hidden_in, ids, logits, nz,
    )
    attended, first = lax.optimization_barrier((attended, first))
    by_heads = exchange(attended, zaxis)
    keep, sent = project(place, by_heads, line, own_out, other_out)
    sent, gain, down = lax.optimization_barrier((sent, norm_gain, down_weight))
    got = lax.ppermute(sent, "v", SWAP)
    got, gain, down = lax.optimization_barrier((got, gain[None], row_major(down)))
    keep, sent = join(keep, got)
    sent, far_down = lax.optimization_barrier((sent, far_down))
    quarter = nz // 2
    got = [
        lax.ppermute(sent, "w", [(i, (i + k) % quarter) for i in range(quarter)])
        for k in range(1, quarter)
    ]
    far_down, *got = lax.optimization_barrier((row_major(far_down), *got))
    residual, copies = norm(place, keep, got, gain, ndp, steps)
    copies, *weights = lax.optimization_barrier(
        (copies, gate_weight, up_weight, far_gate, far_up)
    )
    tokens = exchange(copies, dp)
    relaid = [row_major(w.swapaxes(1, 2)) for w in weights]
    tokens, gate, up, far_gate, far_up = lax.optimization_barrier((tokens, *relaid))
    tokens = tokens.reshape(ndp * nz * steps, -1)
    made = experts(first, tokens, (gate, up, down), (far_gate, far_up, far_down))
    back = exchange(made.reshape(ndp, nz * steps, width), dp)
    column_sum = jnp.sum(back.astype(F32), axis=0).astype(BF16)
    final = exchange(column_sum.reshape(nz, steps, width), zaxis)
    out = residual + jnp.sum(final.astype(F32), axis=0)
    return out.astype(BF16)[None]


def solution(mesh):
    shape = dict(mesh.shape)
    side = int(round(shape["dp"] ** 0.5))
    fine = Mesh(
        mesh.devices.reshape(side, shape["dp"] // side, shape["expert"] // 4, 2, 2),
        ("x", "y", "w", "v", "c"),
    )
    row = ("w", "v", "c", "x", "y")
    group = ("w", "v", "c")
    dp = ("x", "y")
    placed = (
        P(row, None, None),
        P(row, None, None),
        P(row, None, None),
        P(row, None, None),
        P(row, None, None),
        P(row, None, None),
        P(row),
        P(group, None),
        P(),
        P(group, None, None),
        P(group, None, None),
        P(group, None, dp),
        P(group, None, dp),
        P(group, dp, None),
    )
    return jax.shard_map(
        on_device,
        mesh=fine,
        in_specs=placed,
        out_specs=P(row, None, None),
        check_vma=False,
    )
```

```python
import jax
import jax.numpy as jnp
from jax import lax
from jax.experimental import pallas as pl
from jax.experimental.pallas import tpu as pltpu
from jax.experimental.layout import Layout, with_layout_constraint
from jax.sharding import Mesh
from jax.sharding import PartitionSpec as P

HQ = 64
KVH = 8
HD = 64
SWAP = [(0, 1), (1, 0)]
F32 = jnp.float32
BF16 = jnp.bfloat16


def params(mib):
    return pltpu.CompilerParams(vmem_limit_bytes=mib * 1024 * 1024)


def vmem():
    return pl.BlockSpec(memory_space=pltpu.VMEM)


def hbm():
    return pl.BlockSpec(memory_space=pltpu.HBM)


def stay(*values):
    return [pltpu.with_memory_space_constraint(v, pltpu.HBM) for v in values]


def smem():
    return pl.BlockSpec(memory_space=pltpu.SMEM)


def attend_kernel(
    len_ref, place_ref, q_hbm, nk_hbm, nv_hbm, k_hbm, v_hbm, w_hbm, hid_hbm, ids_hbm, logits_hbm,
    out_ref, w_ref, extra_ref, hid_ref, ids_ref, logits_ref, q_ref, nk_ref, nv_ref, k_ref, v_ref, rows_ref, flat_ref, sems,
):
    pairs = (
        (k_hbm, k_ref), (q_hbm, q_ref), (nk_hbm, nk_ref), (nv_hbm, nv_ref), (v_hbm, v_ref),
        (w_hbm, w_ref), (hid_hbm, hid_ref), (ids_hbm, ids_ref), (logits_hbm, logits_ref),
    )
    copies = [pltpu.make_async_copy(a, b, sems.at[i]) for i, (a, b) in enumerate(pairs)]
    for i in (1, 0, 6, 7, 8, 2, 3, 4, 5):
        copies[i].start()
    steps = q_ref.shape[1]
    width = KVH * HD
    rows = HQ * steps
    per_group = rows // KVH
    copies[1].wait()
    q = q_ref[0].astype(F32) * 0.125
    for h in range(HQ):
        rows_ref[h * steps : (h + 1) * steps, :] = q[:, h * HD : (h + 1) * HD]
    q_rows = rows_ref[...]
    q_pair = jnp.concatenate([q_rows, q_rows], axis=1)
    q_wide = jnp.concatenate([q_pair] * (KVH // 2), axis=1)
    row_id = lax.broadcasted_iota(jnp.int32, (rows, width), 0)
    col_id = lax.broadcasted_iota(jnp.int32, (rows, width), 1)
    in_group = row_id // per_group == col_id // HD
    q_wide = jnp.where(in_group, q_wide, 0.0)
    q_bf = q_wide.astype(BF16)
    copies[0].wait()
    scores = lax.dot_general(
        q_bf, k_ref[0], (((1,), (1,)), ((), ())), preferred_element_type=F32
    )
    slot = lax.broadcasted_iota(jnp.int32, scores.shape, 1)
    weights = jnp.where(slot < len_ref[0], jnp.exp(scores), 0.0)
    total = jnp.sum(weights, axis=1, keepdims=True)
    copies[2].wait()
    copies[3].wait()
    nk = nk_ref[0].astype(F32)
    nv = nv_ref[0].astype(F32)
    step_id = lax.broadcasted_iota(jnp.int32, (rows, 1), 0) % steps
    fresh = []
    for s in range(steps):
        score = jnp.sum(q_wide * nk[s : s + 1, :], axis=1, keepdims=True)
        weight = jnp.where(step_id >= s, jnp.exp(score), 0.0)
        total = total + weight
        fresh.append(weight)
    probs = (weights / total).astype(BF16)
    copies[4].wait()
    mixed = jnp.dot(probs, v_ref[0], preferred_element_type=F32)
    for s in range(steps):
        mixed = mixed + (fresh[s] / total).astype(BF16).astype(F32) * nv[s : s + 1, :]
    mixed = jnp.where(in_group, mixed, 0.0)
    folded = mixed[:, :128]
    for i in range(1, width // 128):
        folded = folded + mixed[:, i * 128 : (i + 1) * 128]
    rows_ref[...] = folded[:, :HD] + folded[:, HD:]
    for h in range(HQ):
        flat_ref[:, h * HD : (h + 1) * HD] = rows_ref[h * steps : (h + 1) * steps, :]
    blocks = out_ref.shape[0]
    wide = HQ * HD // blocks
    for b in range(blocks):
        out_ref[b] = flat_ref[:, b * wide : (b + 1) * wide].astype(BF16)
    for i in (6, 7, 8):
        copies[i].wait()
    spare = extra_ref.shape[1] - hid_ref.shape[2]
    lane = lax.broadcasted_iota(jnp.int32, (1, spare), 1)
    routes = []
    for ref in (ids_ref, logits_ref):
        held = ref[...].astype(F32)
        row = lax.broadcasted_iota(jnp.int32, held.shape, 2)
        routes.append(
            jnp.sum(jnp.where(row == place_ref[2], held, 0.0), axis=2, keepdims=True)
        )
    top = routes[0].shape[1]
    lines = []
    for s in range(steps):
        line = jnp.zeros((1, spare), F32)
        for i, values in enumerate(routes):
            for k in range(top):
                line = jnp.where(lane == i * top + k, values[s, k : k + 1, :], line)
        lines.append(line)
    route = jnp.concatenate(lines, axis=0)
    extra_ref[...] = jnp.concatenate([hid_ref[0].astype(F32), route], axis=1)
    copies[5].wait()


def attend(length, place, q, nk, nv, k, v, w, hidden, ids, logits, blocks):
    steps = q.shape[1]
    width = hidden.shape[2]
    args = (q, nk, nv, k, v, w, hidden, ids, logits)
    return pl.pallas_call(
        attend_kernel,
        in_specs=[smem(), smem()] + [hbm()] * len(args),
        out_specs=[vmem(), vmem(), vmem()],
        out_shape=[
            jax.ShapeDtypeStruct((blocks, steps, HQ * HD // blocks), BF16),
            jax.ShapeDtypeStruct(w.shape, BF16),
            jax.ShapeDtypeStruct((steps, width + -width % 128), F32),
        ],
        scratch_shapes=[pltpu.VMEM(a.shape, a.dtype) for a in (hidden, ids, logits)]
        + [pltpu.VMEM(a.shape, BF16) for a in (q, nk, nv, k, v)]
        + [
            pltpu.VMEM((HQ * steps, HD), F32),
            pltpu.VMEM((steps, HQ * HD), F32),
            pltpu.SemaphoreType.DMA((len(args),)),
        ],
        compiler_params=params(12),
        name="attend",
    )(length, place, *stay(*args))


def project_kernel(
    place_ref, x_ref, line_ref, own_ref, other_ref, keep_ref, send_ref, rows_ref
):
    width, feats = own_ref.shape
    chunk = 640
    blocks, steps, _ = x_ref.shape
    for i in range(blocks):
        rows_ref[i * steps : (i + 1) * steps, :] = x_ref[i].astype(F32)
    x = rows_ref[...].astype(BF16)
    low, high = x[:, :feats], x[:, feats:]
    first = place_ref[1] == 0
    mine = jnp.where(first, low, high)
    theirs = jnp.where(first, high, low)
    extra = jnp.concatenate([line_ref[...]] * blocks, axis=0)
    block = lax.broadcasted_iota(jnp.int32, extra.shape, 0) // steps
    extra = jnp.where(block == place_ref[0], extra, 0.0)
    dims = (((1,), (1,)), ((), ()))
    for start in range(0, width, chunk):
        stop = min(start + chunk, width)
        part = lax.dot_general(mine, own_ref[start:stop], dims, preferred_element_type=F32)
        part = part + lax.dot_general(
            theirs, other_ref[start:stop], dims, preferred_element_type=F32
        )
        part = part + extra[:, start:stop]
        keep_ref[:, start:stop] = part
        send_ref[:, start:stop] = part.astype(BF16)
    keep_ref[:, width:] = extra[:, width:]
    send_ref[:, width:] = extra[:, width:].astype(BF16)


def project(place, x, line, own, other):
    blocks, steps, feats = x.shape
    rows = blocks * steps
    return pl.pallas_call(
        project_kernel,
        in_specs=[smem()] + [vmem()] * 4,
        out_specs=[vmem(), vmem()],
        out_shape=[
            jax.ShapeDtypeStruct((rows, line.shape[1]), F32),
            jax.ShapeDtypeStruct((rows, line.shape[1]), BF16),
        ],
        scratch_shapes=[pltpu.VMEM((rows, feats), F32)],
        compiler_params=params(12),
        name="project",
    )(place, x, line, own, other)


def join_kernel(keep_ref, got_ref, next_ref, send_ref):
    total = keep_ref[...] + got_ref[...].astype(F32)
    next_ref[...] = total
    send_ref[...] = total.astype(BF16)


def join(keep, got):
    return pl.pallas_call(
        join_kernel,
        in_specs=[vmem(), vmem()],
        out_specs=[vmem(), vmem()],
        out_shape=[
            jax.ShapeDtypeStruct(keep.shape, F32),
            jax.ShapeDtypeStruct(keep.shape, BF16),
        ],
        compiler_params=params(12),
        name="join",
    )(keep, got)


def norm_kernel(
    place_ref, keep_ref, near_ref, back_ref, far_ref, gain_ref, res_ref, out_hbm, full_ref, sems
):
    steps, width = res_ref.shape
    total = keep_ref[...]
    for ref in (near_ref, back_ref, far_ref):
        total = total + ref[...].astype(F32)
    res = total[:, :width]
    scale = lax.rsqrt(jnp.sum(res * res, axis=1, keepdims=True) / width + 1e-05)
    normed = (res * scale * gain_ref[...]).astype(BF16)
    full_ref[...] = jnp.concatenate([normed.astype(F32), total[:, width:]], axis=1).astype(BF16)
    copies = [
        pltpu.make_async_copy(full_ref, out_hbm.at[i], sems.at[i])
        for i in range(out_hbm.shape[0])
    ]
    for copy in copies:
        copy.start()
    own = jnp.zeros((steps, width), F32)
    for i in range(res.shape[0] // steps):
        own = own + jnp.where(place_ref[0] == i, res[i * steps : (i + 1) * steps, :], 0.0)
    res_ref[...] = own
    for copy in copies:
        copy.wait()


def norm(place, keep, got, gain, copies, steps):
    rows, wide = keep.shape
    width = gain.shape[1]
    return pl.pallas_call(
        norm_kernel,
        in_specs=[smem()] + [vmem()] * 5,
        out_specs=[vmem(), hbm()],
        out_shape=[
            jax.ShapeDtypeStruct((steps, width), F32),
            jax.ShapeDtypeStruct((copies, rows, wide), BF16),
        ],
        scratch_shapes=[pltpu.VMEM((rows, wide), BF16), pltpu.SemaphoreType.DMA((copies,))],
        compiler_params=params(12),
        name="norm",
    )(place, keep, *got, gain)


def experts_kernel(
    first_ref, x_ref, g0_hbm, u0_hbm, g1_hbm, u1_hbm, d0_hbm, d1_hbm, out_ref,
    g0, u0, g1, u1, d0, d1, sems,
):
    pairs = (
        (g0_hbm, g0), (u0_hbm, u0), (g1_hbm, g1), (u1_hbm, u1), (d0_hbm, d0), (d1_hbm, d1),
    )
    per, _, width = g0.shape
    copies = [pltpu.make_async_copy(a, b, sems.at[i]) for i, (a, b) in enumerate(pairs)]
    for copy in copies:
        copy.start()
    x = x_ref[:, :width]
    route = x_ref[:, width : width + 8].astype(F32)
    ids = route[:, 0:4]
    expo = jnp.exp(route[:, 4:8])
    total = jnp.sum(expo, axis=1, keepdims=True)
    dims = (((1,), (1,)), ((), ()))
    acts = []
    for side, (g_ref, u_ref) in enumerate(((g0, u0), (g1, u1))):
        copies[2 * side].wait()
        gates = [
            lax.dot_general(x, g_ref[e], dims, preferred_element_type=F32) for e in range(per)
        ]
        copies[2 * side + 1].wait()
        for e in range(per):
            gate = gates[e]
            up = lax.dot_general(x, u_ref[e], dims, preferred_element_type=F32)
            act = gate * jax.nn.sigmoid(1.702 * gate) * (up + 1.0)
            label = (first_ref[side] + e).astype(F32)
            share = jnp.sum(jnp.where(ids == label, expo, 0.0), axis=1, keepdims=True) / total
            acts.append((act * share).astype(BF16))
    copies[4].wait()
    copies[5].wait()
    part = None
    for side, d_ref in enumerate((d0, d1)):
        for e in range(per):
            piece = jnp.dot(acts[side * per + e], d_ref[e], preferred_element_type=F32)
            part = piece if part is None else part + piece
    out_ref[...] = part.astype(BF16)


def experts(first, x, own, other):
    width = own[0].shape[2]
    args = (own[0], own[1], other[0], other[1], own[2], other[2])
    return pl.pallas_call(
        experts_kernel,
        in_specs=[smem(), vmem()] + [hbm()] * 6,
        out_specs=vmem(),
        out_shape=jax.ShapeDtypeStruct((x.shape[0], width), BF16),
        scratch_shapes=[pltpu.VMEM(a.shape, BF16) for a in args]
        + [pltpu.SemaphoreType.DMA((len(args),))],
        compiler_params=params(32),
        name="experts",
    )(first, x, *stay(*args))


def row_major(value):
    return with_layout_constraint(value, Layout(major_to_minor=tuple(range(value.ndim))))


def finish_kernel(res_ref, part_ref, out_ref):
    total = res_ref[...]
    for i in range(part_ref.shape[0]):
        total = total + part_ref[i].astype(F32)
    out_ref[0] = total.astype(BF16)


def finish(residual, parts):
    return pl.pallas_call(
        finish_kernel,
        in_specs=[vmem(), vmem()],
        out_specs=vmem(),
        out_shape=jax.ShapeDtypeStruct((1,) + residual.shape, BF16),
        compiler_params=params(12),
        name="finish",
    )(residual, parts)


def exchange(value, axis):
    return lax.all_to_all(value, axis, split_axis=0, concat_axis=0, tiled=True)


def on_device(
    hidden_in,
    queries,
    new_keys,
    new_values,
    key_cache,
    value_cache,
    prompt_lengths,
    out_weight,
    norm_gain,
    expert_ids,
    top_logits,
    gate_weight,
    up_weight,
    down_weight,
):
    steps, width = hidden_in.shape[1:]
    zaxis = ("w", "v")
    dp = ("x", "y")
    nz = lax.axis_size(zaxis)
    ndp = lax.axis_size(dp)
    z = lax.axis_index(zaxis)
    c = lax.axis_index("c")
    d = lax.axis_index(dp)
    per = gate_weight.shape[0]
    out_rows = out_weight.T
    other_out = lax.ppermute(out_rows, "c", SWAP)
    far_down, far_gate, far_up = (
        lax.ppermute(w, "c", SWAP) for w in (down_weight, gate_weight, up_weight)
    )
    place = jnp.stack([z, c, d]).astype(jnp.int32)
    first = jnp.stack([(2 * z + c) * per, (2 * z + 1 - c) * per]).astype(jnp.int32)
    ids, logits = expert_ids.transpose(1, 2, 0), top_logits.transpose(1, 2, 0)
    attended, own_out, line = attend(
        prompt_lengths, place, queries, new_keys, new_values, key_cache, value_cache,
        out_rows, hidden_in, ids, logits, nz,
    )
    attended, first = lax.optimization_barrier((attended, first))
    by_heads = exchange(attended, zaxis)
    keep, sent = project(place, by_heads, line, own_out, other_out)
    sent, gain, down = lax.optimization_barrier((sent, norm_gain, down_weight))
    got = lax.ppermute(sent, "v", SWAP)
    got, gain, down = lax.optimization_barrier((got, gain[None], row_major(down)))
    keep, sent = join(keep, got)
    sent, far_down = lax.optimization_barrier((sent, far_down))
    quarter = nz // 2
    got = [
        lax.ppermute(sent, "w", [(i, (i + k) % quarter) for i in range(quarter)])
        for k in range(1, quarter)
    ]
    far_down, *got = lax.optimization_barrier((row_major(far_down), *got))
    residual, copies = norm(place, keep, got, gain, ndp, steps)
    copies, *weights = lax.optimization_barrier(
        (copies, gate_weight, up_weight, far_gate, far_up)
    )
    tokens = exchange(copies, dp)
    relaid = [row_major(w.swapaxes(1, 2)) for w in weights]
    tokens, gate, up, far_gate, far_up = lax.optimization_barrier((tokens, *relaid))
    tokens = tokens.reshape(ndp * nz * steps, -1)
    made = experts(first, tokens, (gate, up, down), (far_gate, far_up, far_down))
    back = exchange(made.reshape(ndp, nz * steps, width), dp)
    column_sum = jnp.sum(back.astype(F32), axis=0).astype(BF16)
    final = exchange(column_sum.reshape(nz, steps, width), zaxis)
    return finish(residual, final)


def solution(mesh):
    shape = dict(mesh.shape)
    side = int(round(shape["dp"] ** 0.5))
    fine = Mesh(
        mesh.devices.reshape(side, shape["dp"] // side, shape["expert"] // 4, 2, 2),
        ("x", "y", "w", "v", "c"),
    )
    row = ("w", "v", "c", "x", "y")
    group = ("w", "v", "c")
    dp = ("x", "y")
    placed = (
        P(row, None, None),
        P(row, None, None),
        P(row, None, None),
        P(row, None, None),
        P(row, None, None),
        P(row, None, None),
        P(row),
        P(group, None),
        P(),
        P(group, None, None),
        P(group, None, None),
        P(group, None, dp),
        P(group, None, dp),
        P(group, dp, None),
    )
    return jax.shard_map(
        on_device,
        mesh=fine,
        in_specs=placed,
        out_specs=P(row, None, None),
        check_vma=False,
    )
```

```python
import jax
import jax.numpy as jnp
from jax import lax
from jax.experimental import pallas as pl
from jax.experimental.pallas import tpu as pltpu
from jax.experimental.layout import Layout, with_layout_constraint
from jax.sharding import Mesh
from jax.sharding import PartitionSpec as P

HQ = 64
KVH = 8
HD = 64
SWAP = [(0, 1), (1, 0)]
F32 = jnp.float32
BF16 = jnp.bfloat16


def params(mib):
    return pltpu.CompilerParams(vmem_limit_bytes=mib * 1024 * 1024)


def vmem():
    return pl.BlockSpec(memory_space=pltpu.VMEM)


def hbm():
    return pl.BlockSpec(memory_space=pltpu.HBM)


def stay(*values):
    return [pltpu.with_memory_space_constraint(v, pltpu.HBM) for v in values]


def smem():
    return pl.BlockSpec(memory_space=pltpu.SMEM)


def attend_kernel(
    len_ref, q_hbm, nk_hbm, nv_hbm, k_hbm, v_hbm, w_hbm, out_ref, w_ref,
    q_ref, nk_ref, nv_ref, k_ref, v_ref, rows_ref, flat_ref, sems,
):
    pairs = (
        (k_hbm, k_ref), (q_hbm, q_ref), (nk_hbm, nk_ref), (nv_hbm, nv_ref), (v_hbm, v_ref),
        (w_hbm, w_ref),
    )
    copies = [pltpu.make_async_copy(a, b, sems.at[i]) for i, (a, b) in enumerate(pairs)]
    for copy in copies:
        copy.start()
    steps = q_ref.shape[1]
    width = KVH * HD
    rows = HQ * steps
    per_group = rows // KVH
    copies[1].wait()
    q = q_ref[0].astype(F32) * 0.125
    for h in range(HQ):
        rows_ref[h * steps : (h + 1) * steps, :] = q[:, h * HD : (h + 1) * HD]
    q_rows = rows_ref[...]
    q_pair = jnp.concatenate([q_rows, q_rows], axis=1)
    q_wide = jnp.concatenate([q_pair] * (KVH // 2), axis=1)
    row_id = lax.broadcasted_iota(jnp.int32, (rows, width), 0)
    col_id = lax.broadcasted_iota(jnp.int32, (rows, width), 1)
    in_group = row_id // per_group == col_id // HD
    q_wide = jnp.where(in_group, q_wide, 0.0)
    q_bf = q_wide.astype(BF16)
    copies[0].wait()
    scores = lax.dot_general(
        q_bf, k_ref[0], (((1,), (1,)), ((), ())), preferred_element_type=F32
    )
    slot = lax.broadcasted_iota(jnp.int32, scores.shape, 1)
    weights = jnp.where(slot < len_ref[0], jnp.exp(scores), 0.0)
    total = jnp.sum(weights, axis=1, keepdims=True)
    copies[2].wait()
    copies[3].wait()
    nk = nk_ref[0].astype(F32)
    nv = nv_ref[0].astype(F32)
    step_id = lax.broadcasted_iota(jnp.int32, (rows, 1), 0) % steps
    fresh = []
    for s in range(steps):
        score = jnp.sum(q_wide * nk[s : s + 1, :], axis=1, keepdims=True)
        weight = jnp.where(step_id >= s, jnp.exp(score), 0.0)
        total = total + weight
        fresh.append(weight)
    probs = (weights / total).astype(BF16)
    copies[4].wait()
    mixed = jnp.dot(probs, v_ref[0], preferred_element_type=F32)
    for s in range(steps):
        mixed = mixed + (fresh[s] / total).astype(BF16).astype(F32) * nv[s : s + 1, :]
    mixed = jnp.where(in_group, mixed, 0.0)
    folded = mixed[:, :128]
    for i in range(1, width // 128):
        folded = folded + mixed[:, i * 128 : (i + 1) * 128]
    rows_ref[...] = folded[:, :HD] + folded[:, HD:]
    for h in range(HQ):
        flat_ref[:, h * HD : (h + 1) * HD] = rows_ref[h * steps : (h + 1) * steps, :]
    blocks = out_ref.shape[0]
    wide = HQ * HD // blocks
    for b in range(blocks):
        out_ref[b] = flat_ref[:, b * wide : (b + 1) * wide].astype(BF16)
    copies[5].wait()


def attend(length, q, nk, nv, k, v, w, blocks):
    steps = q.shape[1]
    return pl.pallas_call(
        attend_kernel,
        in_specs=[smem()] + [hbm()] * 6,
        out_specs=[vmem(), vmem()],
        out_shape=[
            jax.ShapeDtypeStruct((blocks, steps, HQ * HD // blocks), BF16),
            jax.ShapeDtypeStruct(w.shape, BF16),
        ],
        scratch_shapes=[pltpu.VMEM(a.shape, BF16) for a in (q, nk, nv, k, v)]
        + [
            pltpu.VMEM((HQ * steps, HD), F32),
            pltpu.VMEM((steps, HQ * HD), F32),
            pltpu.SemaphoreType.DMA((6,)),
        ],
        compiler_params=params(12),
        name="attend",
    )(length, *stay(q, nk, nv, k, v, w))


def project_kernel(
    place_ref, x_ref, own_ref, other_ref, hid_hbm, ids_hbm, logits_hbm, keep_ref, send_ref,
    rows_ref, hid_ref, ids_ref, logits_ref, sems,
):
    width, feats = own_ref.shape
    chunk = 640
    cuts = [(start, min(start + chunk, width)) for start in range(0, width, chunk)]
    small = [
        pltpu.make_async_copy(hid_hbm, hid_ref, sems.at[0]),
        pltpu.make_async_copy(ids_hbm, ids_ref, sems.at[1]),
        pltpu.make_async_copy(logits_hbm, logits_ref, sems.at[2]),
    ]
    for copy in small:
        copy.start()
    blocks, steps, _ = x_ref.shape
    for i in range(blocks):
        rows_ref[i * steps : (i + 1) * steps, :] = x_ref[i].astype(F32)
    x = rows_ref[...].astype(BF16)
    low, high = x[:, :feats], x[:, feats:]
    first = place_ref[1] == 0
    mine = jnp.where(first, low, high)
    theirs = jnp.where(first, high, low)
    for copy in small:
        copy.wait()
    spare = keep_ref.shape[1] - width
    lane = lax.broadcasted_iota(jnp.int32, (1, spare), 1)
    routes = []
    for ref in (ids_ref, logits_ref):
        held = ref[...].astype(F32)
        row = lax.broadcasted_iota(jnp.int32, held.shape, 2)
        routes.append(
            jnp.sum(jnp.where(row == place_ref[2], held, 0.0), axis=2, keepdims=True)
        )
    top = routes[0].shape[1]
    lines = []
    for s in range(steps):
        line = jnp.zeros((1, spare), F32)
        for i, values in enumerate(routes):
            for k in range(top):
                line = jnp.where(lane == i * top + k, values[s, k : k + 1, :], line)
        lines.append(line)
    route = jnp.concatenate(lines, axis=0)
    extra = jnp.concatenate([hid_ref[0].astype(F32), route], axis=1)
    extra = jnp.concatenate([extra] * blocks, axis=0)
    block = lax.broadcasted_iota(jnp.int32, extra.shape, 0) // steps
    extra = jnp.where(block == place_ref[0], extra, 0.0)
    dims = (((1,), (1,)), ((), ()))
    for start, stop in cuts:
        part = lax.dot_general(mine, own_ref[start:stop], dims, preferred_element_type=F32)
        part = part + lax.dot_general(
            theirs, other_ref[start:stop], dims, preferred_element_type=F32
        )
        part = part + extra[:, start:stop]
        keep_ref[:, start:stop] = part
        send_ref[:, start:stop] = part.astype(BF16)
    keep_ref[:, width:] = extra[:, width:]
    send_ref[:, width:] = extra[:, width:].astype(BF16)


def project(place, x, hidden, ids, logits, own, other):
    blocks, steps, feats = x.shape
    wide = own.shape[0] + -own.shape[0] % 128
    rows = blocks * steps
    return pl.pallas_call(
        project_kernel,
        in_specs=[smem(), vmem(), vmem(), vmem()] + [hbm()] * 3,
        out_specs=[vmem(), vmem()],
        out_shape=[
            jax.ShapeDtypeStruct((rows, wide), F32),
            jax.ShapeDtypeStruct((rows, wide), BF16),
        ],
        scratch_shapes=[
            pltpu.VMEM((rows, feats), F32),
            pltpu.VMEM(hidden.shape, BF16),
            pltpu.VMEM(ids.shape, jnp.int32),
            pltpu.VMEM(logits.shape, BF16),
            pltpu.SemaphoreType.DMA((3,)),
        ],
        compiler_params=params(12),
        name="project",
    )(place, x, own, other, *stay(hidden, ids, logits))


def join_kernel(keep_ref, got_ref, next_ref, send_ref):
    total = keep_ref[...] + got_ref[...].astype(F32)
    next_ref[...] = total
    send_ref[...] = total.astype(BF16)


def join(keep, got):
    return pl.pallas_call(
        join_kernel,
        in_specs=[vmem(), vmem()],
        out_specs=[vmem(), vmem()],
        out_shape=[
            jax.ShapeDtypeStruct(keep.shape, F32),
            jax.ShapeDtypeStruct(keep.shape, BF16),
        ],
        compiler_params=params(12),
        name="join",
    )(keep, got)


def norm_kernel(
    place_ref, keep_ref, near_ref, back_ref, far_ref, gain_ref, res_ref, out_hbm, full_ref, sems
):
    steps, width = res_ref.shape
    total = keep_ref[...]
    for ref in (near_ref, back_ref, far_ref):
        total = total + ref[...].astype(F32)
    res = total[:, :width]
    scale = lax.rsqrt(jnp.sum(res * res, axis=1, keepdims=True) / width + 1e-05)
    normed = (res * scale * gain_ref[...]).astype(BF16)
    full_ref[...] = jnp.concatenate([normed.astype(F32), total[:, width:]], axis=1).astype(BF16)
    copies = [
        pltpu.make_async_copy(full_ref, out_hbm.at[i], sems.at[i])
        for i in range(out_hbm.shape[0])
    ]
    for copy in copies:
        copy.start()
    own = jnp.zeros((steps, width), F32)
    for i in range(res.shape[0] // steps):
        own = own + jnp.where(place_ref[0] == i, res[i * steps : (i + 1) * steps, :], 0.0)
    res_ref[...] = own
    for copy in copies:
        copy.wait()


def norm(place, keep, got, gain, copies, steps):
    rows, wide = keep.shape
    width = gain.shape[1]
    return pl.pallas_call(
        norm_kernel,
        in_specs=[smem()] + [vmem()] * 5,
        out_specs=[vmem(), hbm()],
        out_shape=[
            jax.ShapeDtypeStruct((steps, width), F32),
            jax.ShapeDtypeStruct((copies, rows, wide), BF16),
        ],
        scratch_shapes=[pltpu.VMEM((rows, wide), BF16), pltpu.SemaphoreType.DMA((copies,))],
        compiler_params=params(12),
        name="norm",
    )(place, keep, *got, gain)


def experts_kernel(
    first_ref, x_ref, g0_hbm, u0_hbm, g1_hbm, u1_hbm, d0_hbm, d1_hbm, out_ref,
    g0, u0, g1, u1, d0, d1, sems,
):
    pairs = (
        (g0_hbm, g0), (u0_hbm, u0), (g1_hbm, g1), (u1_hbm, u1), (d0_hbm, d0), (d1_hbm, d1),
    )
    per, _, width = g0.shape
    copies = [pltpu.make_async_copy(a, b, sems.at[i]) for i, (a, b) in enumerate(pairs)]
    for copy in copies:
        copy.start()
    x = x_ref[:, :width]
    route = x_ref[:, width : width + 8].astype(F32)
    ids = route[:, 0:4]
    expo = jnp.exp(route[:, 4:8])
    total = jnp.sum(expo, axis=1, keepdims=True)
    dims = (((1,), (1,)), ((), ()))
    acts = []
    for side, (g_ref, u_ref) in enumerate(((g0, u0), (g1, u1))):
        copies[2 * side].wait()
        gates = [
            lax.dot_general(x, g_ref[e], dims, preferred_element_type=F32) for e in range(per)
        ]
        copies[2 * side + 1].wait()
        for e in range(per):
            gate = gates[e]
            up = lax.dot_general(x, u_ref[e], dims, preferred_element_type=F32)
            act = gate * jax.nn.sigmoid(1.702 * gate) * (up + 1.0)
            label = (first_ref[side] + e).astype(F32)
            share = jnp.sum(jnp.where(ids == label, expo, 0.0), axis=1, keepdims=True) / total
            acts.append((act * share).astype(BF16))
    copies[4].wait()
    copies[5].wait()
    chunk = 1536
    for start in range(0, width, chunk):
        stop = min(start + chunk, width)
        part = None
        for side, d_ref in enumerate((d0, d1)):
            for e in range(per):
                piece = jnp.dot(
                    acts[side * per + e], d_ref[e, :, start:stop], preferred_element_type=F32
                )
                part = piece if part is None else part + piece
        out_ref[:, start:stop] = part.astype(BF16)


def experts(first, x, own, other):
    width = own[0].shape[2]
    args = (own[0], own[1], other[0], other[1], own[2], other[2])
    return pl.pallas_call(
        experts_kernel,
        in_specs=[smem(), vmem()] + [hbm()] * 6,
        out_specs=vmem(),
        out_shape=jax.ShapeDtypeStruct((x.shape[0], width), BF16),
        scratch_shapes=[pltpu.VMEM(a.shape, BF16) for a in args]
        + [pltpu.SemaphoreType.DMA((len(args),))],
        compiler_params=params(32),
        name="experts",
    )(first, x, *stay(*args))


def row_major(value):
    return with_layout_constraint(value, Layout(major_to_minor=tuple(range(value.ndim))))


def exchange(value, axis):
    return lax.all_to_all(value, axis, split_axis=0, concat_axis=0, tiled=True)


def on_device(
    hidden_in,
    queries,
    new_keys,
    new_values,
    key_cache,
    value_cache,
    prompt_lengths,
    out_weight,
    norm_gain,
    expert_ids,
    top_logits,
    gate_weight,
    up_weight,
    down_weight,
):
    steps, width = hidden_in.shape[1:]
    zaxis = ("w", "v")
    dp = ("x", "y")
    nz = lax.axis_size(zaxis)
    ndp = lax.axis_size(dp)
    z = lax.axis_index(zaxis)
    c = lax.axis_index("c")
    d = lax.axis_index(dp)
    per = gate_weight.shape[0]
    out_rows = out_weight.T
    other_out = lax.ppermute(out_rows, "c", SWAP)
    far_down, far_gate, far_up = (
        lax.ppermute(w, "c", SWAP) for w in (down_weight, gate_weight, up_weight)
    )
    attended, own_out = attend(
        prompt_lengths, queries, new_keys, new_values, key_cache, value_cache, out_rows, nz
    )
    place = jnp.stack([z, c, d]).astype(jnp.int32)
    first = jnp.stack([(2 * z + c) * per, (2 * z + 1 - c) * per]).astype(jnp.int32)
    attended, place, first = lax.optimization_barrier((attended, place, first))
    by_heads = exchange(attended, zaxis)
    ids, logits = expert_ids.transpose(1, 2, 0), top_logits.transpose(1, 2, 0)
    keep, sent = project(place, by_heads, hidden_in, ids, logits, own_out, other_out)
    sent, gain, down = lax.optimization_barrier((sent, norm_gain, down_weight))
    got = lax.ppermute(sent, "v", SWAP)
    got, gain, down = lax.optimization_barrier((got, gain[None], row_major(down)))
    keep, sent = join(keep, got)
    sent, far_down = lax.optimization_barrier((sent, far_down))
    quarter = nz // 2
    got = [
        lax.ppermute(sent, "w", [(i, (i + k) % quarter) for i in range(quarter)])
        for k in range(1, quarter)
    ]
    far_down, *got = lax.optimization_barrier((row_major(far_down), *got))
    residual, copies = norm(place, keep, got, gain, ndp, steps)
    copies, *weights = lax.optimization_barrier(
        (copies, gate_weight, up_weight, far_gate, far_up)
    )
    tokens = exchange(copies, ("y", "x"))
    relaid = [row_major(w.swapaxes(1, 2)) for w in weights]
    tokens, gate, up, far_gate, far_up = lax.optimization_barrier((tokens, *relaid))
    tokens = tokens.reshape(ndp * nz * steps, -1)
    made = experts(first, tokens, (gate, up, down), (far_gate, far_up, far_down))
    back = exchange(made.reshape(ndp, nz * steps, width), ("y", "x"))
    column_sum = jnp.sum(back.astype(F32), axis=0).astype(BF16)
    final = exchange(column_sum.reshape(nz, steps, width), zaxis)
    out = residual + jnp.sum(final.astype(F32), axis=0)
    return out.astype(BF16)[None]


def solution(mesh):
    shape = dict(mesh.shape)
    side = int(round(shape["dp"] ** 0.5))
    fine = Mesh(
        mesh.devices.reshape(side, shape["dp"] // side, shape["expert"] // 4, 2, 2),
        ("x", "y", "w", "v", "c"),
    )
    row = ("w", "v", "c", "x", "y")
    group = ("w", "v", "c")
    dp = ("x", "y")
    placed = (
        P(row, None, None),
        P(row, None, None),
        P(row, None, None),
        P(row, None, None),
        P(row, None, None),
        P(row, None, None),
        P(row),
        P(group, None),
        P(),
        P(group, None, None),
        P(group, None, None),
        P(group, None, dp),
        P(group, None, dp),
        P(group, dp, None),
    )
    return jax.shard_map(
        on_device,
        mesh=fine,
        in_specs=placed,
        out_specs=P(row, None, None),
        check_vma=False,
    )
```
